32 devices in a mesh: row: 8 (over z, y), col: 4 (over x, core).
Axes of the slice: x: 2, y: 2, z: 4, core: 2. Of those that a mesh axis runs over, the one named last changes fastest.
Arguments:
- latents: bfloat16 [4, 1152, 4096], P(None, 'col', 'row'), may hold values from -6 to 6
- cond: bfloat16 [4, 1, 1152], P(None, None, 'row'), may hold values from -6 to 6
- w_ada: bfloat16 [2, 1152, 6, 1152], P(None, 'row', None, 'col'), may hold values from -0.1875 to 0.1875
- b_ada: bfloat16 [2, 6, 1152], P(None, None, 'col'), may hold values from -3 to 3
- w_qkv: bfloat16 [2, 1152, 3, 1152], P(None, 'row', None, 'col'), may hold values from -0.1875 to 0.1875
- b_qv: bfloat16 [2, 2, 1152], P(None, None, 'col'), may hold values from -3 to 3
- w_out: bfloat16 [2, 1152, 1152], P(None, 'row', 'col'), may hold values from -0.5 to 0.5
- b_out: bfloat16 [2, 1152], P(None, 'col'), may hold values from -2 to 2
- w_fc1: bfloat16 [2, 1152, 4608], P(None, 'row', 'col'), may hold values from -0.1875 to 0.1875
- b_fc1: bfloat16 [2, 4608], P(None, 'col'), may hold values from -3 to 3
- w_fc2: bfloat16 [2, 1152, 4608], P(None, 'row', 'col'), may hold values from -0.09375 to 0.09375
- b_fc2: bfloat16 [2, 1152], P(None, 'col'), may hold values from -2 to 2
- cotangent: bfloat16 [4, 1152, 4096], P(None, 'col', 'row'), may hold values from -6 to 6
Outputs:
- output: bfloat16 [4, 1152, 4096], P(None, 'col', 'row')
- grad_latents: float32 [4, 1152, 4096], P(None, 'col', 'row')
- grad_cond: float32 [4, 1, 1152], P(None, None, 'row')
- grad_w_ada: float32 [2, 1152, 6, 1152], P(None, 'row', None, 'col')
- grad_b_ada: float32 [2, 6, 1152], P(None, None, 'col')
- grad_w_qkv: float32 [2, 1152, 3, 1152], P(None, 'row', None, 'col')
- grad_b_qv: float32 [2, 2, 1152], P(None, None, 'col')
- grad_w_out: float32 [2, 1152, 1152], P(None, 'row', 'col')
- grad_b_out: float32 [2, 1152], P(None, 'col')
- grad_w_fc1: float32 [2, 1152, 4608], P(None, 'row', 'col')
- grad_b_fc1: float32 [2, 4608], P(None, 'col')
- grad_w_fc2: float32 [2, 1152, 4608], P(None, 'row', 'col')
- grad_b_fc2: float32 [2, 1152], P(None, 'col')
The draws below stay inside these ranges and needn't reach their ends.
All inputs are finite; a program needn't handle non-finite values.
Results may differ from the reference program's by a relative error of at most 0.03.
Values may be sent and summed in bfloat16 or wider, within the bound.
No kernel may reach another device: no remote copies, remote signals or barrier semaphores. Data moves between devices by JAX's collectives and lax.ppermute only.
A program may use at most 320 MiB of HBM per device.

```python
import jax
import jax.numpy as jnp
from jax import lax

D = 1152
HEADS = 16
HD = 72
FF = 4608
P_SIZE = 256
NF = 16
MB = 4
LAT_MB = 1
TOK_MB = 4096


def levels(own_key, shape, cuts, least, top_value):
    factor_of, own = 1.0, jax.random.fold_in(own_key, 6)
    for dim, shards_of in cuts:
        draws = jnp.exp(jax.random.uniform(jax.random.fold_in(own, dim), (shards_of,), jnp.float32, least / len(cuts), top_value / len(cuts)))
        factor_of = factor_of * jnp.repeat(draws, shape[dim] // shards_of).reshape([-1 if axis == dim else 1 for axis in range(len(shape))])
    return factor_of


def scatter_about(stream_key, shape, scale, bound, cuts=(), kind=jnp.bfloat16):
    values = jax.random.normal(stream_key, shape, jnp.float32) * scale
    if len(cuts) > 0:
        values = levels(stream_key, shape, cuts, -0.22, 0.18) * values
    return jnp.clip(values, min=-bound, max=bound).astype(kind)


def setup_inputs(seed: int = 0) -> dict:
    seeds = jax.random.split(jax.random.key(seed), 14)
    return {
        "latents": scatter_about(seeds[0], (MB, D, TOK_MB), 1.0, 6.0, ((1, 4), (2, 8))),
        "cond": scatter_about(seeds[1], (MB, LAT_MB, D), 1.0, 6.0, ((2, 8),)),
        "w_ada": scatter_about(seeds[2], (2, D, 6, D), D ** -0.5, 0.1875, ((1, 8), (3, 4))),
        "b_ada": scatter_about(seeds[3], (2, 6, D), 0.5, 3.0, ((2, 4),)),
        "w_qkv": scatter_about(seeds[4], (2, D, 3, D), D ** -0.5, 0.1875, ((1, 8), (3, 4))),
        "b_qv": scatter_about(seeds[5], (2, 2, D), 0.5, 3.0, ((2, 4),)),
        "w_out": scatter_about(seeds[6], (2, D, D), (D // 8) ** -0.5, 0.5, ((1, 8), (2, 4))),
        "b_out": scatter_about(seeds[7], (2, D), 0.3, 2.0, ((1, 4),)),
        "w_fc1": scatter_about(seeds[8], (2, D, FF), D ** -0.5, 0.1875, ((1, 8), (2, 4))),
        "b_fc1": scatter_about(seeds[9], (2, FF), 0.5, 3.0, ((1, 4),)),
        "w_fc2": scatter_about(seeds[10], (2, D, FF), FF ** -0.5, 0.09375, ((1, 8), (2, 4))),
        "b_fc2": scatter_about(seeds[11], (2, D), 0.3, 2.0, ((1, 4),)),
        "cotangent": scatter_about(seeds[12], (MB, D, TOK_MB), 1.0, 6.0, ((1, 4), (2, 8))),
    }


@jax.custom_vjp
def low(v):
    return lax.optimization_barrier(v.astype(jnp.bfloat16)).astype(jnp.float32)

@jax.custom_vjp
def low_back(v):
    return v

def low_keep(v):
    return (low(v), None)

def low_pass(kept, grad):
    return (grad,)

def back_keep(v):
    return (v, None)

def back_low(kept, grad):
    return (low(grad),)
low.defvjp(low_keep, low_pass)
low_back.defvjp(back_keep, back_low)
highest = lax.Precision.HIGHEST
epsilon = 1e-06
spatial_patterns = ('fqhd,fkhd->fhqk', 'fhqk,fkhd->fqhd')
temporal_patterns = ('lqphd,lkphd->lphqk', 'lphqk,lkphd->lqphd')

def layer_norm(stream):
    center = stream - lax.optimization_barrier(jnp.mean(stream, -1, keepdims=True))
    variance = lax.optimization_barrier(jnp.mean(center * center, -1, keepdims=True))
    return center * lax.rsqrt(variance + epsilon)

def attend(query_heads, key_heads, value_heads, patterns):
    scores = jnp.einsum(patterns[0], query_heads, key_heads, precision=highest) * HD ** (-0.5)
    scores = low_back(scores)
    weights = low(jax.nn.softmax(scores, axis=-1))
    return jnp.einsum(patterns[1], weights, value_heads, precision=highest)

def spatial_attend(triple):
    return attend(triple[0], triple[1], triple[2], spatial_patterns)

def block(stream, modulate, w_qkv, b_qv, w_out, b_out, w_fc1, b_fc1, w_fc2, b_fc2, temporal):
    pieces = [modulate[:, column][:, None, None, :] for column in range(6)]
    hidden = low(layer_norm(stream) * (1.0 + pieces[1]) + pieces[0])
    projected = jnp.einsum('lfpd,dje->lfpje', hidden, w_qkv, precision=highest)
    biases = jnp.stack([b_qv[0], jnp.zeros_like(b_qv[0]), b_qv[1]])
    projected = low_back(low(projected + biases))
    shaped = stream.shape[:3] + (HEADS, HD)
    query_heads = projected[..., 0, :].reshape(shaped)
    key_heads = projected[..., 1, :].reshape(shaped)
    value_heads = projected[..., 2, :].reshape(shaped)
    if temporal:
        attended = attend(query_heads, key_heads, value_heads, temporal_patterns)
    else:
        attended = lax.map(jax.checkpoint(spatial_attend), (query_heads, key_heads, value_heads))
    attended = low_back(low(attended.reshape(stream.shape)))
    branch = low_back(jnp.einsum('lfpe,de->lfpd', attended, w_out, precision=highest) + b_out)
    middle = stream + pieces[2] * branch
    hidden_two = low(layer_norm(middle) * (1.0 + pieces[4]) + pieces[3])
    preact = low_back(jnp.einsum('lfpd,dg->lfpg', hidden_two, w_fc1, precision=highest) + b_fc1)
    activated = low(jax.nn.gelu(preact, approximate=True))
    branch_two = low_back(jnp.einsum('lfpg,dg->lfpd', activated, w_fc2, precision=highest) + b_fc2)
    return middle + pieces[5] * branch_two

def forward(stream, condition, w_ada, b_ada, w_qkv, b_qv, w_out, b_out, w_fc1, b_fc1, w_fc2, b_fc2):
    gated = low(jax.nn.silu(condition))
    modulate = low_back(jnp.einsum('ld,bdjk->lbjk', gated, w_ada, precision=highest) + b_ada)
    frames = stream.reshape(LAT_MB, NF, P_SIZE, D)
    frames = block(frames, modulate[:, 0], w_qkv[0], b_qv[0], w_out[0], b_out[0], w_fc1[0], b_fc1[0], w_fc2[0], b_fc2[0], False)
    frames = block(frames, modulate[:, 1], w_qkv[1], b_qv[1], w_out[1], b_out[1], w_fc1[1], b_fc1[1], w_fc2[1], b_fc2[1], True)
    return frames.reshape(TOK_MB, D)

def reference(latents, cond, w_ada, b_ada, w_qkv, b_qv, w_out, b_out, w_fc1, b_fc1, w_fc2, b_fc2, cotangent):
    params = tuple((weight.astype(jnp.float32) for weight in (w_ada, b_ada, w_qkv, b_qv, w_out, b_out, w_fc1, b_fc1, w_fc2, b_fc2)))
    outputs = []
    grad_inputs = []
    grad_conds = []
    totals = None
    for batch_index in range(MB):
        result, pullback = jax.vjp(forward, latents[batch_index].T.astype(jnp.float32), cond[batch_index].astype(jnp.float32), *params)
        gradients = pullback(cotangent[batch_index].T.astype(jnp.float32))
        outputs.append(result.astype(jnp.bfloat16).T)
        grad_inputs.append(gradients[0].T)
        grad_conds.append(gradients[1])
        if totals is None:
            totals = gradients[2:]
        else:
            totals = tuple((first + second for first, second in zip(totals, gradients[2:])))
    return (jnp.stack(outputs), jnp.stack(grad_inputs), jnp.stack(grad_conds), totals[0], totals[1], totals[2], totals[3], totals[4], totals[5], totals[6], totals[7], totals[8], totals[9])
```

```python
import functools

import jax
import jax.numpy as jnp
import numpy as np
from jax import lax
from jax.experimental import pallas as pl
from jax.experimental.pallas import tpu as pltpu
from jax.sharding import Mesh
from jax.sharding import PartitionSpec as P

D = 1152
HD = 72
P_SIZE = 256
NF = 16
SCALE = HD ** (-0.5)
EPSILON = 1e-06


f32 = jnp.float32
bf16 = jnp.bfloat16


def bits_of(count):
    found = []
    bit = count // 2
    while bit:
        found.append(bit)
        bit //= 2
    return found


def swap(value, axis, bit):
    count = lax.axis_size(axis)
    return lax.ppermute(value, axis, [(i, i ^ bit) for i in range(count)])


def row_order(rows):
    order = [0]
    for bit in bits_of(rows):
        order = order + [j ^ bit for j in order]
    return order


def step_plan(rows, parts, kind):
    by_row = [("row", bit) for bit in bits_of(rows)]
    by_part = [("m", bit) for bit in bits_of(parts)]
    if kind == 0 or not by_row or len(by_part) < 2:
        return by_row + by_part
    return by_row[:-1] + by_part[:-1] + by_row[-1:] + by_part[-1:]


def moved(label, axis, bit):
    return (label[0] ^ bit, label[1]) if axis == "row" else (label[0], label[1] ^ bit)


def gather_blocks(shard, rows, parts, kind):
    buffers = [([(0, 0)], shard[None])]
    plan = step_plan(rows, parts, kind)
    for number, (axis, bit) in enumerate(plan):
        fresh = []
        for labels, value in buffers:
            other = swap(value, axis, bit)
            other_labels = [moved(label, axis, bit) for label in labels]
            if number < len(plan) - 2:
                fresh.append((labels + other_labels, jnp.concatenate([value, other], 0)))
            else:
                fresh.append((labels, value))
                fresh.append((other_labels, other))
        buffers = fresh
    depth, width = shard.shape
    blocks = []
    for part in range(parts):
        wanted = [(j, part) for j in row_order(rows)]
        pieces = []
        for labels, value in buffers:
            hits = [place for place, label in enumerate(labels) if label[1] == part]
            if hits:
                rank = wanted.index(labels[hits[0]])
                pieces.append((rank, value[hits[0] : hits[-1] + 1]))
                assert [labels[h] for h in hits] == wanted[rank : rank + len(hits)]
        pieces = [piece for _, piece in sorted(pieces, key=lambda item: item[0])]
        whole = pieces[0] if len(pieces) == 1 else jnp.concatenate(pieces, 0)
        blocks.append(whole.reshape(rows * depth, width))
    return blocks


def total(terms):
    result = terms[0].astype(f32)
    for term in terms[1:]:
        result = result + term.astype(f32)
    return result


def scatter_blocks(blocks, rows, parts, kind):
    order = row_order(rows)
    height = blocks[0].shape[0] // rows
    live = {part: [blocks[part]] for part in range(parts)}
    span = rows
    for axis, bit in reversed(step_plan(rows, parts, kind)):
        if axis == "m":
            for part in [p for p in live if p & bit]:
                terms = live.pop(part)
                sent = terms[0] if len(terms) == 1 else total(terms).astype(bf16)
                live[part ^ bit].append(swap(sent, axis, bit))
        else:
            half = span // 2
            assert all(order[half + p] == order[p] ^ bit for p in range(half))
            names = sorted(live)
            sent = jnp.stack(
                [total([t[half * height :] for t in live[n]]).astype(bf16) for n in names]
            )
            got = swap(sent, axis, bit)
            for place, name in enumerate(names):
                live[name] = [t[: half * height] for t in live[name]] + [got[place]]
            span = half
    return total(live[0])


def all_sum(value, axis):
    for bit in bits_of(lax.axis_size(axis)):
        value = value + swap(value, axis, bit)
    return value


def over_u(value):
    return lax.psum(value, "u") if lax.axis_size("u") > 1 else value


def features_all(value):
    return lax.all_gather(value, "u", axis=1, tiled=True) if lax.axis_size("u") > 1 else value


def features_sum(value):
    if lax.axis_size("u") > 1:
        return lax.psum_scatter(value, "u", scatter_dimension=1, tiled=True)
    return value


def dot_nn(left, right):
    return lax.dot_general(left, right, (((1,), (0,)), ((), ())), preferred_element_type=f32)


def dot_nt(left, right):
    return lax.dot_general(left, right, (((1,), (1,)), ((), ())), preferred_element_type=f32)


def dot_tn(left, right):
    return lax.dot_general(left, right, (((0,), (0,)), ((), ())), preferred_element_type=f32)


def apart(value):
    return lax.optimization_barrier(value)


def gelu_tanh(value):
    return jax.nn.gelu(value, approximate=True)


def probabilities(query, key, allowed):
    scores = dot_nt(query, key) * SCALE
    if allowed is not None:
        scores = jnp.where(allowed, scores, -jnp.inf)
    powered = jnp.exp(scores - jnp.max(scores, -1, keepdims=True))
    return powered / jnp.sum(powered, -1, keepdims=True)


def allowed_pairs(temporal, span, tokens):
    if not temporal:
        return None
    first = lax.broadcasted_iota(jnp.int32, (tokens, tokens), 0)
    second = lax.broadcasted_iota(jnp.int32, (tokens, tokens), 1)
    return lax.rem(first, span) == lax.rem(second, span)


def forward_kernel(parts, temporal, span, *refs):
    ins, out = refs[:parts], refs[parts]
    width = ins[0].shape[-1] // 3
    tokens = int(np.prod(ins[0].shape[:-1]))
    allowed = allowed_pairs(temporal, span, tokens)
    for part in range(parts):
        block = ins[part][...].reshape(tokens, 3 * width)
        done = []
        for start in range(0, width, HD):
            query, key, value = [block[:, c * width + start : c * width + start + HD] for c in range(3)]
            weights = probabilities(query, key, allowed).astype(bf16)
            done.append(dot_nn(weights, value).astype(bf16))
        joined = done[0] if len(done) == 1 else jnp.concatenate(done, 1)
        where = (Ellipsis, slice(part * width, (part + 1) * width))
        out[where] = joined.reshape(out.shape[:-1] + (width,))


def backward_kernel(parts, temporal, span, *refs):
    ins, grad, outs = refs[:parts], refs[parts], refs[parts + 1 :]
    width = ins[0].shape[-1] // 3
    tokens = int(np.prod(ins[0].shape[:-1]))
    allowed = allowed_pairs(temporal, span, tokens)
    for part in range(parts):
        block = ins[part][...].reshape(tokens, 3 * width)
        outer = grad[..., part * width : (part + 1) * width].reshape(tokens, width)
        pieces = [[], [], []]
        for start in range(0, width, HD):
            query, key, value = [block[:, c * width + start : c * width + start + HD] for c in range(3)]
            above = outer[:, start : start + HD]
            weights = probabilities(query, key, allowed)
            grad_weights = dot_nt(above, value)
            inner = jnp.sum(grad_weights * weights, -1, keepdims=True)
            grad_scores = (weights * (grad_weights - inner)).astype(bf16)
            pieces[0].append((dot_nn(grad_scores, key) * SCALE).astype(bf16))
            pieces[1].append((dot_tn(grad_scores, query) * SCALE).astype(bf16))
            pieces[2].append(dot_tn(weights.astype(bf16), above).astype(bf16))
        joined = jnp.concatenate(pieces[0] + pieces[1] + pieces[2], 1)
        outs[part][...] = joined.reshape(outs[part].shape)


def attention_specs(layout, width):
    if len(layout) == 2:
        return (layout[0],), pl.BlockSpec((1, layout[1], width), lambda g: (g, 0, 0))
    chunk = 16
    assert layout[2] % chunk == 0
    return (
        (layout[0], layout[2] // chunk),
        pl.BlockSpec((1, layout[1], chunk, width), lambda g, c: (g, 0, c, 0)),
    )


def attend_forward(qkv, layout):
    parts = len(qkv)
    tokens, triple = qkv[0].shape
    width = triple // 3
    grid, in_spec = attention_specs(layout, triple)
    out_spec = attention_specs(layout, parts * width)[1]
    temporal = len(layout) == 3
    heads = parts * width // HD
    attended = pl.pallas_call(
        functools.partial(forward_kernel, parts, temporal, 16),
        grid=grid,
        in_specs=[in_spec] * parts,
        out_specs=out_spec,
        out_shape=jax.ShapeDtypeStruct(layout + (parts * width,), bf16),
        cost_estimate=pl.CostEstimate(
            flops=tokens * heads * 256 * 128 * 4,
            transcendentals=tokens * heads * 256,
            bytes_accessed=tokens * width * parts * 8,
        ),
        name="attend_forward",
    )(*[block.reshape(layout + (triple,)) for block in qkv])
    return attended.reshape(tokens, parts * width)


def attend_backward(qkv, grad, layout):
    parts = len(qkv)
    tokens, triple = qkv[0].shape
    width = triple // 3
    grid, in_spec = attention_specs(layout, triple)
    grad_spec = attention_specs(layout, parts * width)[1]
    temporal = len(layout) == 3
    heads = parts * width // HD
    grads = pl.pallas_call(
        functools.partial(backward_kernel, parts, temporal, 16),
        grid=grid,
        in_specs=[in_spec] * parts + [grad_spec],
        out_specs=[in_spec] * parts,
        out_shape=[jax.ShapeDtypeStruct(layout + (triple,), bf16)] * parts,
        cost_estimate=pl.CostEstimate(
            flops=tokens * heads * 256 * 128 * 10,
            transcendentals=tokens * heads * 256,
            bytes_accessed=tokens * width * parts * 14,
        ),
        name="attend_backward",
    )(*[block.reshape(layout + (triple,)) for block in qkv], grad.reshape(layout + (parts * width,)))
    return [block.reshape(tokens, triple) for block in grads]


def norm_forward(stream):
    center = stream - over_u(jnp.sum(stream, 1, keepdims=True)) / D
    inverse = lax.rsqrt(over_u(jnp.sum(center * center, 1, keepdims=True)) / D + EPSILON)
    return center * inverse, inverse


def norm_backward(grad_normed, normed, inverse):
    first, second = over_u(
        (
            jnp.sum(grad_normed, 1, keepdims=True),
            jnp.sum(grad_normed * normed, 1, keepdims=True),
        )
    )
    return inverse * (grad_normed - first / D - normed * (second / D))


def spread(vector, tokens):
    groups, width = vector.shape
    if groups == 1:
        return vector
    return jnp.broadcast_to(vector[:, None, :], (groups, tokens // groups, width)).reshape(tokens, width)


def group_sum(value, groups):
    return jnp.sum(value.reshape(groups, -1, value.shape[-1]), 1)


def block_forward(stream, modulate, weights, layout):
    w_qkv, w_out, w_fc1, w_fc2, b_qkv, b_out, b_fc1, b_fc2 = weights
    tokens = stream.shape[0]
    pieces = [spread(modulate[:, column], tokens) for column in range(6)]
    normed, inverse = norm_forward(stream)
    hidden = features_all((normed * (1.0 + pieces[1]) + pieces[0]).astype(bf16))
    qkv = [(dot_nn(hidden, w) + b).astype(bf16) for w, b in zip(w_qkv, b_qkv)]
    attended = attend_forward(qkv, layout)
    branch = apart(features_sum(dot_nt(attended, w_out))) + b_out
    middle = stream + pieces[2] * branch
    normed_two, inverse_two = norm_forward(middle)
    hidden_two = features_all((normed_two * (1.0 + pieces[4]) + pieces[3]).astype(bf16))
    preact = [dot_nn(hidden_two, w) + b for w, b in zip(w_fc1, b_fc1)]
    activated = [gelu_tanh(p).astype(bf16) for p in preact]
    branch_two = apart(features_sum(total([dot_nt(a, w) for a, w in zip(activated, w_fc2)]))) + b_fc2
    result = middle + pieces[5] * branch_two
    kept = (
        pieces, normed, inverse, hidden, qkv, attended, branch,
        normed_two, inverse_two, hidden_two, preact, activated, branch_two,
    )
    return result, kept


def block_backward(grad, kept, groups, weights, layout, place):
    (
        pieces, normed, inverse, hidden, qkv, attended, branch,
        normed_two, inverse_two, hidden_two, preact, activated, branch_two,
    ) = kept
    w_qkv, w_out, w_fc1, w_fc2 = weights[:4]
    width = w_out.shape[1] // len(w_qkv)
    grad_branch_two = (pieces[5] * grad).astype(bf16)
    grad_two_all = features_all(grad_branch_two)
    d_fc2 = [dot_tn(grad_two_all, a).astype(bf16) for a in activated]
    sum_fc2 = place(d_fc2, 1)
    grad_preact = [
        jax.vjp(gelu_tanh, p)[1](dot_nn(grad_two_all, w))[0].astype(bf16) for p, w in zip(preact, w_fc2)
    ]
    d_fc1 = [dot_tn(hidden_two, g).astype(bf16) for g in grad_preact]
    sum_fc1 = place(d_fc1, 0)
    grad_hidden_two = apart(features_sum(total([dot_nt(g, w) for g, w in zip(grad_preact, w_fc1)])))
    grad_middle = grad + norm_backward(grad_hidden_two * (1.0 + pieces[4]), normed_two, inverse_two)
    grad_branch = (pieces[2] * grad_middle).astype(bf16)
    grad_branch_all = features_all(grad_branch)
    grad_attended = dot_nn(grad_branch_all, w_out).astype(bf16)
    d_out = dot_tn(grad_branch_all, attended).astype(bf16)
    grad_qkv = attend_backward(qkv, grad_attended, layout)
    d_mixed = [
        jnp.concatenate(
            [dot_tn(hidden, g).astype(bf16), d_out[:, part * width : (part + 1) * width]], 1
        )
        for part, g in enumerate(grad_qkv)
    ]
    sum_mixed = place(d_mixed, 1)
    grad_hidden = apart(features_sum(total([dot_nt(g, w) for g, w in zip(grad_qkv, w_qkv)])))
    grad_stream = grad_middle + norm_backward(grad_hidden * (1.0 + pieces[1]), normed, inverse)
    modulate_grad = jnp.stack(
        [
            group_sum(grad_hidden, groups),
            group_sum(grad_hidden * normed, groups),
            group_sum(grad_middle * branch, groups),
            group_sum(grad_hidden_two, groups),
            group_sum(grad_hidden_two * normed_two, groups),
            group_sum(grad * branch_two, groups),
        ],
        1,
    )
    summed = lambda value: jnp.sum(value.astype(f32), 0)
    bias_grads = (
        jnp.stack([summed(g[:, :width]) for g in grad_qkv]),
        jnp.stack([summed(g[:, 2 * width :]) for g in grad_qkv]),
        summed(grad_branch),
        jnp.stack([summed(g) for g in grad_preact]),
        summed(grad_branch_two),
    )
    return grad_stream, (sum_mixed, sum_fc1, sum_fc2), bias_grads, modulate_grad


def shards(
    latents, cond, w_ada, b_ada, w_qkv, b_qv, w_out, b_out, w_fc1, b_fc1, w_fc2, b_fc2, cotangent
):
    batches, width, tokens = latents.shape
    lat_count = cond.shape[1]
    rows = lax.axis_size("row")
    parts = lax.axis_size("m")
    split = lax.axis_size("u")
    row = lax.axis_index("row")
    part_here = lax.axis_index("m")
    span = parts * width
    order = jnp.asarray(row_order(rows), jnp.int32)
    inverse_order = jnp.asarray(np.argsort(row_order(rows)), jnp.int32)
    part_ids = part_here ^ jnp.arange(parts)
    frames_dev = tokens // P_SIZE
    pos_block = tokens // (lat_count * NF)
    spatial = (frames_dev, P_SIZE)
    temporal = (lat_count, NF, pos_block)

    relative = split == 1
    depth = D // rows
    if relative:
        slot = jnp.arange(D)
        source = (row ^ order[slot // depth]) * depth + slot % depth
        exchange = (jnp.arange(D)[:, None] == source[None, :]).astype(bf16)

    def vector_rel(value):
        if not relative:
            return value
        shaped = value.reshape(value.shape[:-1] + (rows, depth))
        return jnp.take(shaped, row ^ order, axis=-2).reshape(value.shape)

    def vector_plain(value):
        if not relative:
            return value
        shaped = value.reshape(value.shape[:-1] + (rows, depth))
        return jnp.take(shaped, inverse_order[row ^ jnp.arange(rows)], axis=-2).reshape(value.shape)

    def stream_plain(value):
        return dot_nt(value, exchange).astype(bf16) if relative else value

    def stream_rel(value):
        return dot_nn(value, exchange) if relative else value.astype(f32)

    def to_positions(value):
        shaped = stream_plain(value.astype(bf16)).reshape(frames_dev, rows, pos_block, span)
        got = lax.all_to_all(shaped, "row", split_axis=1, concat_axis=0, tiled=True)
        return stream_rel(got.reshape(tokens, span))

    def to_frames(value):
        shaped = stream_plain(value.astype(bf16)).reshape(frames_dev * rows, 1, pos_block, span)
        got = lax.all_to_all(shaped, "row", split_axis=0, concat_axis=1, tiled=True)
        return got.reshape(tokens, span)

    def whole(shard, kind):
        blocks = gather_blocks(shard, rows, parts, kind)
        if relative:
            return blocks
        places = inverse_order[row ^ jnp.arange(rows)]
        return [jnp.take(b.reshape(rows, depth, -1), places, axis=0).reshape(b.shape) for b in blocks]

    def place(blocks, kind):
        if not relative:
            blocks = [
                jnp.take(b.reshape(rows, depth, -1), row ^ order, axis=0).reshape(b.shape)
                for b in blocks
            ]
        return scatter_blocks(blocks, rows, parts, kind)

    cond_float = cond.astype(f32)
    cond_low = jax.nn.silu(cond_float).astype(bf16)
    mod_partial = jnp.einsum("mlr,brjk->mlbjk", cond_low, w_ada, preferred_element_type=f32)
    mod_partial = mod_partial + jnp.where(row == 0, b_ada.astype(f32), 0.0)[None, None]
    small = jnp.concatenate(
        [b.astype(f32).reshape(-1) for b in (b_qv, b_out, b_fc1, b_fc2)]
    )
    packed = jnp.concatenate(
        [mod_partial.reshape(batches, -1), jnp.broadcast_to(small, (parts,) + small.shape)], 1
    )
    packed = lax.all_to_all(packed, "m", split_axis=0, concat_axis=0, tiled=True)
    mod_size = lat_count * 12 * width
    mod_here = all_sum(packed[:, :mod_size], "row").reshape(parts, lat_count, 2, 6, width)
    mod_here = vector_rel(jnp.moveaxis(mod_here, 0, -2).reshape(lat_count, 2, 6, span))
    small = packed[:, mod_size:]
    sizes = np.cumsum([0, 4 * width, 2 * width, 2 * b_fc1.shape[1], 2 * width])
    all_qv, all_out, all_fc1, all_fc2 = [small[:, a:b] for a, b in zip(sizes[:-1], sizes[1:])]
    all_qv = jnp.take(all_qv.reshape(parts, 2, 2, width), part_ids, axis=0)
    all_fc1 = jnp.take(all_fc1.reshape(parts, 2, -1), part_ids, axis=0)
    all_out = vector_rel(jnp.moveaxis(all_out.reshape(parts, 2, width), 0, 1).reshape(2, span))
    all_fc2 = vector_rel(jnp.moveaxis(all_fc2.reshape(parts, 2, width), 0, 1).reshape(2, span))

    block_weights = []
    for which in range(2):
        mixed = jnp.concatenate([w_qkv[which].reshape(depth, 3 * width), w_out[which]], 1)
        mixed = whole(mixed, 0)
        zeros = jnp.zeros((width,), f32)
        block_weights.append(
            (
                [b[:, : 3 * width] for b in mixed],
                jnp.concatenate([b[:, 3 * width :] for b in mixed], 1),
                whole(w_fc1[which], 1),
                whole(w_fc2[which], 0),
                [jnp.concatenate([all_qv[i, which, 0], zeros, all_qv[i, which, 1]]) for i in range(parts)],
                all_out[which],
                [all_fc1[i, which] for i in range(parts)],
                all_fc2[which],
            )
        )

    def own_batch(value):
        return lax.all_to_all(value, "m", split_axis=0, concat_axis=1, tiled=True)[0]

    def to_stream(value):
        return dot_tn(value, exchange) if relative else value.T.astype(f32)

    def to_argument(value):
        return lax.all_to_all(value[None], "m", split_axis=1, concat_axis=0, tiled=True)

    lat_here = row * frames_dev // NF
    mod_space = lax.dynamic_slice_in_dim(mod_here[:, 0], lat_here, 1, 0)
    mod_time = mod_here[:, 1]
    first_in = to_stream(own_batch(latents))
    grad_top = own_batch(cotangent).T
    shaped = grad_top.reshape(frames_dev, rows, pos_block, span)
    grad_top = stream_rel(
        lax.all_to_all(shaped, "row", split_axis=1, concat_axis=0, tiled=True).reshape(tokens, span)
    )
    first_out, kept_space = block_forward(first_in, mod_space, block_weights[0], spatial)
    second_in = to_positions(first_out)
    second_out, kept_time = block_forward(second_in, mod_time, block_weights[1], temporal)
    output = to_argument(to_frames(second_out).T)

    grad_mid, weights_time, biases_time, mod_grad_time = block_backward(
        grad_top, kept_time, lat_count, block_weights[1], temporal, place
    )
    grad_low = stream_rel(to_frames(grad_mid))
    grad_first, weights_space, biases_space, mod_grad_space = block_backward(
        grad_low, kept_space, 1, block_weights[0], spatial, place
    )
    grad_first = grad_first.astype(bf16)
    grad_first = dot_nt(exchange, grad_first).astype(bf16) if relative else grad_first.T
    grad_latents = to_argument(grad_first).astype(f32)

    onehot = (jnp.arange(lat_count) == lat_here).astype(f32)
    mod_grads = jnp.stack([onehot[:, None, None] * mod_grad_space, mod_grad_time], 1)
    mod_grads = vector_plain(mod_grads).reshape(lat_count, 2, 6, parts, width)
    mod_grads = jnp.moveaxis(mod_grads, -2, 0).reshape(parts, -1)

    def by_part(value):
        return jnp.take(value, part_ids, axis=0)

    def by_stream(value):
        return vector_plain(value).reshape(parts, width)

    pieces = [mod_grads]
    for space, time in zip(biases_space, biases_time):
        for value in (space, time):
            pieces.append(by_part(value) if value.ndim == 2 else by_stream(value))
    counts = np.cumsum([0] + [piece.shape[1] for piece in pieces])
    packed = jnp.concatenate(pieces, 1)
    packed = lax.all_to_all(packed, "m", split_axis=0, concat_axis=0, tiled=True)
    mod_part = packed[:, : counts[1]]
    bias_part = jnp.sum(packed[:, counts[1] :], 0, keepdims=True)
    flat = jnp.concatenate([mod_part.reshape(1, -1), bias_part], 1)
    flat = all_sum(flat, "row")[0]
    mod_grad_low = flat[: batches * counts[1]].reshape(batches, lat_count, 2, 6, width).astype(bf16)
    bias_part = flat[batches * counts[1] :]
    bias_out = [bias_part[a - counts[1] : b - counts[1]] for a, b in zip(counts[1:-1], counts[2:])]
    grad_bias_qv = jnp.stack(
        [jnp.stack([bias_out[0], bias_out[2]]), jnp.stack([bias_out[1], bias_out[3]])]
    )
    grad_bias_out = jnp.stack(bias_out[4:6])
    grad_bias_fc1 = jnp.stack(bias_out[6:8])
    grad_bias_fc2 = jnp.stack(bias_out[8:10])
    grad_bias_ada = jnp.sum(mod_grad_low.astype(f32), (0, 1))
    grad_weight_ada = jnp.einsum("mlr,mlbjk->brjk", cond_low, mod_grad_low, preferred_element_type=f32)
    cond_partial = jnp.einsum("mlbjk,brjk->mlr", mod_grad_low, w_ada, preferred_element_type=f32)
    cond_total = over_u(all_sum(cond_partial, "m"))
    sigmoid_cond = jax.nn.sigmoid(cond_float)
    grad_condition = cond_total * sigmoid_cond * (1.0 + cond_float * (1.0 - sigmoid_cond))
    grad_weight_qkv, grad_weight_out, grad_weight_fc1, grad_weight_fc2 = [], [], [], []
    for mixed, first, second in (weights_space, weights_time):
        grad_weight_qkv.append(mixed[:, : 3 * width].reshape(depth, 3, width))
        grad_weight_out.append(mixed[:, 3 * width :])
        grad_weight_fc1.append(first)
        grad_weight_fc2.append(second)
    return (
        output,
        grad_latents,
        grad_condition,
        grad_weight_ada,
        grad_bias_ada,
        jnp.stack(grad_weight_qkv),
        grad_bias_qv,
        jnp.stack(grad_weight_out),
        grad_bias_out,
        jnp.stack(grad_weight_fc1),
        grad_bias_fc1,
        jnp.stack(grad_weight_fc2),
        grad_bias_fc2,
    )


def solution(mesh):
    rows, columns = mesh.devices.shape

    def placed(latents, *rest):
        parts = latents.shape[0]
        inner = Mesh(mesh.devices.reshape(rows, columns // parts, parts), ("row", "u", "m"))
        col = ("u", "m")
        in_specs = (
            P(None, col, "row"),
            P(None, None, "row"),
            P(None, "row", None, col),
            P(None, None, col),
            P(None, "row", None, col),
            P(None, None, col),
            P(None, "row", col),
            P(None, col),
            P(None, "row", col),
            P(None, col),
            P(None, "row", col),
            P(None, col),
            P(None, col, "row"),
        )
        out_specs = (P(None, col, "row"),) + in_specs[:1] + in_specs[1:-1]
        return jax.shard_map(
            shards, mesh=inner, in_specs=in_specs, out_specs=out_specs, check_vma=False
        )(latents, *rest)

    return placed
```

```python
import functools

import jax
import jax.numpy as jnp
import numpy as np
from jax import lax
from jax.experimental import pallas as pl
from jax.experimental.pallas import tpu as pltpu
from jax.sharding import Mesh
from jax.sharding import PartitionSpec as P

D = 1152
HD = 72
P_SIZE = 256
NF = 16
SCALE = HD ** (-0.5)
EPSILON = 1e-06


KINDS = ({"mixed": 0, "fc1": 1, "fc2": 0}, {"mixed": 1, "fc1": 0, "fc2": 1})

f32 = jnp.float32
bf16 = jnp.bfloat16


def bits_of(count):
    found = []
    bit = count // 2
    while bit:
        found.append(bit)
        bit //= 2
    return found


def swap(value, axis, bit):
    count = lax.axis_size(axis)
    return lax.ppermute(value, axis, [(i, i ^ bit) for i in range(count)])


def row_order(rows):
    order = [0]
    for bit in bits_of(rows):
        order = order + [j ^ bit for j in order]
    return order


def step_plan(rows, parts, kind):
    by_row = [("row", bit) for bit in bits_of(rows)]
    by_part = [("m", bit) for bit in bits_of(parts)]
    if kind == 0:
        return by_row + by_part
    return by_row[:-1] + by_part[:-1] + by_row[-1:] + by_part[-1:]


def moved(label, axis, bit):
    return (label[0] ^ bit, label[1]) if axis == "row" else (label[0], label[1] ^ bit)


def total(terms):
    result = terms[0].astype(f32)
    for term in terms[1:]:
        result = result + term.astype(f32)
    return result


class Gather:
    def __init__(self, shard, rows, parts, kind):
        self.rows, self.parts, self.depth = rows, parts, shard.shape[0]
        self.plan = step_plan(rows, parts, kind)
        self.labels = [[(0, 0)]]
        self.arrays = [shard]
        self.done = 0

    def step(self):
        axis, bit = self.plan[self.done]
        merge = self.done < len(self.plan) - 2
        labels, arrays = [], []
        for names, value in zip(self.labels, self.arrays):
            other = swap(value, axis, bit)
            other_names = [moved(name, axis, bit) for name in names]
            if merge:
                labels.append(names + other_names)
                arrays.append(jnp.concatenate([value, other], 0))
            else:
                labels += [names, other_names]
                arrays += [value, other]
        self.labels, self.arrays = labels, arrays
        self.done += 1

    def pieces(self):
        order, depth = row_order(self.rows), self.depth
        found = []
        for part in range(self.parts):
            entries = []
            for number, names in enumerate(self.labels):
                hits = [place for place, name in enumerate(names) if name[1] == part]
                if hits:
                    rank = order.index(names[hits[0]][0])
                    assert [names[h][0] for h in hits] == order[rank : rank + len(hits)]
                    assert hits == list(range(hits[0], hits[0] + len(hits)))
                    entries.append((number, hits[0] * depth, len(hits) * depth, rank * depth))
            found.append(entries)
        return found


class Scatter:
    def __init__(self, sent, kept, rows, parts, kind):
        self.plan = step_plan(rows, parts, kind)[::-1]
        self.order = row_order(rows)
        self.depth = kept.shape[1] // rows
        self.span = rows
        self.arrays = [sent, kept]
        evens = [part for part in range(parts) if not part & 1]
        self.live = {part: [(1, place, 0)] for place, part in enumerate(evens)}
        self.done = 0

    def take(self, term, first, count):
        number, lead, start = term
        return self.arrays[number][lead, start + first : start + first + count]

    def sums(self, names, first, count):
        return [total([self.take(t, first, count) for t in self.live[n]]).astype(bf16) for n in names]

    def step(self):
        axis, bit = self.plan[self.done]
        if self.done == 0:
            assert (axis, bit) == ("m", 1)
            self.arrays.append(swap(self.arrays[0], axis, bit))
            for place, name in enumerate(sorted(self.live)):
                self.live[name].append((len(self.arrays) - 1, place, 0))
        elif axis == "m":
            names = [name for name in sorted(self.live) if name & bit]
            sent = self.sums(names, 0, self.span * self.depth)
            for name in names:
                self.live.pop(name)
            self.arrays.append(swap(jnp.stack(sent), axis, bit))
            for place, name in enumerate(names):
                self.live[name ^ bit].append((len(self.arrays) - 1, place, 0))
        else:
            half = self.span // 2
            order = self.order
            assert all(order[half + p] == order[p] ^ bit for p in range(half))
            names = sorted(self.live)
            sent = self.sums(names, half * self.depth, half * self.depth)
            self.arrays.append(swap(jnp.stack(sent), axis, bit))
            for place, name in enumerate(names):
                self.live[name].append((len(self.arrays) - 1, place, 0))
            self.span = half
        self.done += 1

    def result(self):
        return total([self.take(t, 0, self.depth) for t in self.live[0]])


def fence(objects, values):
    arrays, values = lax.optimization_barrier(([o.arrays for o in objects], values))
    for o, fresh in zip(objects, arrays):
        o.arrays = list(fresh)
    return values


def all_sum(value, axis):
    for bit in bits_of(lax.axis_size(axis)):
        value = value + swap(value, axis, bit)
    return value


def over_u(value):
    return lax.psum(value, "u") if lax.axis_size("u") > 1 else value


def features_all(value):
    return lax.all_gather(value, "u", axis=1, tiled=True) if lax.axis_size("u") > 1 else value


def features_sum(value):
    if lax.axis_size("u") > 1:
        return lax.psum_scatter(value, "u", scatter_dimension=1, tiled=True)
    return value


def dot_nn(left, right):
    return lax.dot_general(left, right, (((1,), (0,)), ((), ())), preferred_element_type=f32)


def dot_nt(left, right):
    return lax.dot_general(left, right, (((1,), (1,)), ((), ())), preferred_element_type=f32)


def dot_tn(left, right):
    return lax.dot_general(left, right, (((0,), (0,)), ((), ())), preferred_element_type=f32)


LIMIT = 56 * 1024 * 1024


class Weight:
    def __init__(self, arrays, pieces):
        self.arrays = [value.reshape(-1, value.shape[-1]) for value in arrays]
        self.places = pieces
        self.parts = len(pieces)
        self.height = sum(rows for _, _, rows, _ in pieces[0])
        self.width = self.arrays[0].shape[1]

    def scratch(self):
        pieces = len(self.places[0])
        return [
            pltpu.VMEM((self.parts, self.height, self.width), bf16),
            pltpu.SemaphoreType.DMA((self.parts, pieces)),
        ]

    def copies(self, part, refs, held, sems):
        return [
            pltpu.make_async_copy(
                refs[number].at[pl.ds(start, rows)], held.at[part, pl.ds(to, rows)], sems.at[part, place]
            )
            for place, (number, start, rows, to) in enumerate(self.places[part])
        ]

    def arrive(self, step, refs, held, sems):
        @pl.when(step == 0)
        def _():
            for part in range(self.parts):
                for copy in self.copies(part, refs, held, sems):
                    copy.start()

        for part in range(self.parts):

            @pl.when(step == part)
            def _(part=part):
                for copy in self.copies(part, refs, held, sems):
                    copy.wait()


def cut_last(load, low, high):
    base = low // 128 * 128
    value = load(base, high)
    return value if base == low else value[:, low - base :]


def whole_spec(shape):
    return pl.BlockSpec(shape, lambda s: (0,) * len(shape))


def part_spec(shape):
    return pl.BlockSpec((1,) + shape, lambda s: (s,) + (0,) * len(shape))


def project(x, weight, columns, extras, epilogue, out_types, name):
    tokens, depth = x.shape
    low, high = columns
    n = high - low
    count = len(weight.arrays)

    def body(*refs):
        x_ref, refs = refs[0], refs[1:]
        w_refs, refs = refs[:count], refs[count:]
        extra_refs, refs = refs[: len(extras)], refs[len(extras) :]
        outs, (held, sems) = refs[: len(out_types)], refs[len(out_types) :]
        step = pl.program_id(0)
        weight.arrive(step, w_refs, held, sems)
        left = x_ref[...]
        right = cut_last(lambda a, b: held[step, :, a:b], low, high)
        made = epilogue(dot_nn(left, right), *[e[0] for e in extra_refs])
        for out, piece in zip(outs, made):
            out[0] = piece.astype(out.dtype)

    return pl.pallas_call(
        body,
        grid=(weight.parts,),
        in_specs=[whole_spec((tokens, depth))]
        + [pl.BlockSpec(memory_space=pl.ANY)] * count
        + [part_spec(e.shape[1:]) for e in extras],
        out_specs=[part_spec((tokens, n))] * len(out_types),
        out_shape=[jax.ShapeDtypeStruct((weight.parts, tokens, n), t) for t in out_types],
        scratch_shapes=weight.scratch(),
        compiler_params=pltpu.CompilerParams(vmem_limit_bytes=LIMIT),
        cost_estimate=pl.CostEstimate(
            flops=2 * tokens * depth * n * weight.parts,
            transcendentals=0,
            bytes_accessed=2 * weight.parts * n * (depth + 2 * tokens),
        ),
        name=name,
    )(x, *weight.arrays, *extras)


def contract(xs, weight, columns, name):
    parts, tokens, n = xs.shape
    low, high = columns
    count = len(weight.arrays)
    height = weight.height

    def body(*refs):
        x_ref, refs = refs[0], refs[1:]
        w_refs, (out, held, sems) = refs[:count], refs[count:]
        step = pl.program_id(0)
        weight.arrive(step, w_refs, held, sems)
        left = x_ref[0]
        right = cut_last(lambda a, b: held[step, :, a:b], low, high)
        value = dot_nt(left, right)

        @pl.when(step == 0)
        def _():
            out[...] = value

        @pl.when(step > 0)
        def _():
            out[...] += value

    return pl.pallas_call(
        body,
        grid=(parts,),
        in_specs=[part_spec((tokens, n))] + [pl.BlockSpec(memory_space=pl.ANY)] * count,
        out_specs=whole_spec((tokens, height)),
        out_shape=jax.ShapeDtypeStruct((tokens, height), f32),
        scratch_shapes=weight.scratch(),
        compiler_params=pltpu.CompilerParams(vmem_limit_bytes=LIMIT),
        cost_estimate=pl.CostEstimate(
            flops=2 * tokens * height * n * parts,
            transcendentals=0,
            bytes_accessed=2 * parts * n * (height + tokens) + 4 * tokens * height,
        ),
        name=name,
    )(xs, *weight.arrays)


def weight_grads(pairs, name):
    tokens, depth = pairs[0][0].shape
    parts = pairs[0][1].shape[0]
    half = parts // 2
    widths = [g.shape[2] for _, g in pairs]
    full = sum(widths)
    count = len(pairs)

    def which(step):
        return jnp.where(step < half, 2 * step + 1, 2 * (step - half))

    def body(*refs):
        x_refs, refs = refs[:count], refs[count:]
        g_refs, refs = refs[:count], refs[count:]
        (sent, kept), refs = refs[:2], refs[2:]
        x_sums, refs = refs[:count], refs[count:]
        g_sums, turned = refs[:count], refs[count:]
        step = pl.program_id(0)

        @pl.when(step == 0)
        def _():
            for x_ref, x_sum, t_ref in zip(x_refs, x_sums, turned):
                value = x_ref[...].astype(f32)
                x_sum[...] = jnp.sum(value, 0, keepdims=True)
                t_ref[...] = value.T.astype(bf16)

        rights = [g_ref[0] for g_ref in g_refs]
        for right, g_sum in zip(rights, g_sums):
            g_sum[0] = jnp.sum(right.astype(f32), 0, keepdims=True)

        def fill(out):
            made = [dot_nn(t_ref[...], r).astype(bf16) for t_ref, r in zip(turned, rights)]
            out[0] = made[0] if count == 1 else jnp.concatenate(made, 1)

        @pl.when(step < half)
        def _():
            fill(sent)

        @pl.when(step >= half)
        def _():
            fill(kept)

    outs = pl.pallas_call(
        body,
        grid=(parts,),
        in_specs=[whole_spec((tokens, depth))] * count
        + [pl.BlockSpec((1, tokens, n), lambda s: (which(s), 0, 0)) for n in widths],
        out_specs=[
            pl.BlockSpec((1, depth, full), lambda s: (jnp.minimum(s, half - 1), 0, 0)),
            pl.BlockSpec((1, depth, full), lambda s: (jnp.maximum(s - half, 0), 0, 0)),
        ]
        + [whole_spec((1, depth))] * count
        + [pl.BlockSpec((1, 1, n), lambda s: (which(s), 0, 0)) for n in widths],
        out_shape=[jax.ShapeDtypeStruct((half, depth, full), bf16)] * 2
        + [jax.ShapeDtypeStruct((1, depth), f32)] * count
        + [jax.ShapeDtypeStruct((parts, 1, n), f32) for n in widths],
        scratch_shapes=[pltpu.VMEM((depth, tokens), bf16)] * count,
        compiler_params=pltpu.CompilerParams(vmem_limit_bytes=LIMIT),
        cost_estimate=pl.CostEstimate(
            flops=2 * tokens * depth * full * parts,
            transcendentals=0,
            bytes_accessed=2 * parts * full * (depth + tokens),
        ),
        name=name,
    )(*[x for x, _ in pairs], *[g for _, g in pairs])
    return outs[:2], outs[2 : 2 + count], outs[2 + count :]


def gelu_pair(value, bias):
    v = value + bias
    slope = 0.7978845608028654
    inner = jnp.tanh(slope * (v + 0.044715 * v * v * v))
    outer = 0.5 * (1.0 + inner)
    change = outer + 0.5 * v * (1.0 - inner * inner) * (slope * (1.0 + 3.0 * 0.044715 * v * v))
    return v * outer, change


POWER = SCALE * 1.4426950408889634


def allowed_pairs(temporal, span, tokens):
    if not temporal:
        return None
    first = lax.broadcasted_iota(jnp.int32, (tokens, tokens), 0)
    second = lax.broadcasted_iota(jnp.int32, (tokens, tokens), 1)
    return lax.rem(first, span) == lax.rem(second, span)


def head_columns(block, start, width):
    return [block[:, c * width + start : c * width + start + HD] for c in range(3)]


def forward_kernel(temporal, span, qkv, out, logs):
    width = qkv.shape[-1] // 3
    tokens = int(np.prod(qkv.shape[:-1]))
    allowed = allowed_pairs(temporal, span, tokens)
    block = qkv[...].reshape(tokens, 3 * width)
    done, kept = [], []
    for start in range(0, width, HD):
        query, key, value = head_columns(block, start, width)
        scores = dot_nt(key, query)
        if allowed is not None:
            scores = jnp.where(allowed, scores, -jnp.inf)
        largest = jnp.max(scores, 0, keepdims=True)
        powered = jnp.exp2((scores - largest) * POWER)
        summed = jnp.sum(powered, 0, keepdims=True)
        done.append(dot_tn(value, powered.astype(bf16)) / summed)
        kept.append(largest * POWER + jnp.log2(summed))
    out[...] = jnp.concatenate(done, 0).T.astype(bf16).reshape(out.shape)
    logs[...] = jnp.concatenate(kept, 0).reshape(logs.shape)


def backward_kernel(temporal, span, qkv, grad, attended, logs, out):
    width = qkv.shape[-1] // 3
    tokens = int(np.prod(qkv.shape[:-1]))
    allowed = allowed_pairs(temporal, span, tokens)
    block = qkv[...].reshape(tokens, 3 * width)
    outer = grad[...].reshape(tokens, width)
    turned = outer.astype(f32).T * attended[...].reshape(tokens, width).astype(f32).T
    log_rows = logs[...].reshape(width // HD, tokens)
    pieces = [[], [], []]
    for place, start in enumerate(range(0, width, HD)):
        query, key, value = head_columns(block, start, width)
        above = outer[:, start : start + HD]
        inner = jnp.sum(turned[start : start + HD], 0, keepdims=True)
        weights = jnp.exp2(dot_nt(key, query) * POWER - log_rows[place : place + 1])
        if allowed is not None:
            weights = jnp.where(allowed, weights, 0.0)
        grad_scores = (weights * (dot_nt(value, above) - inner)).astype(bf16)
        pieces[0].append(dot_tn(key, grad_scores) * SCALE)
        pieces[1].append((dot_nn(grad_scores, query) * SCALE).astype(bf16))
        pieces[2].append(dot_nn(weights.astype(bf16), above).astype(bf16))
    first = jnp.concatenate(pieces[0], 0).T.astype(bf16)
    out[...] = jnp.concatenate([first] + pieces[1] + pieces[2], 1).reshape(out.shape)


def attention_call(kernel, values, logs, layout, out_width, work, name):
    parts, tokens, triple = values[0].shape
    heads = triple // 3 // HD
    temporal = len(layout) == 3
    chunk = 16
    grid = (parts, layout[0])
    if temporal:
        assert layout[2] % chunk == 0
        grid = grid + (layout[2] // chunk,)
    groups = tokens // P_SIZE

    def spec(width):
        if temporal:
            return pl.BlockSpec((1, 1, layout[1], chunk, width), lambda p, g, c: (p, g, 0, c, 0))
        return pl.BlockSpec((1, 1, layout[1], width), lambda p, g: (p, g, 0, 0))

    if temporal:
        log_spec = pl.BlockSpec((1, 1, heads, P_SIZE), lambda p, g, c: (p, g * grid[2] + c, 0, 0))
    else:
        log_spec = pl.BlockSpec((1, 1, heads, P_SIZE), lambda p, g: (p, g, 0, 0))
    out_shape = [jax.ShapeDtypeStruct((parts,) + layout + (out_width,), bf16)]
    out_specs = [spec(out_width)]
    in_specs = [spec(v.shape[-1]) for v in values]
    given = [v.reshape((parts,) + layout + (v.shape[-1],)) for v in values]
    if logs is None:
        out_shape.append(jax.ShapeDtypeStruct((parts, groups, heads, P_SIZE), f32))
        out_specs.append(log_spec)
    else:
        in_specs.append(log_spec)
        given.append(logs)
    result = pl.pallas_call(
        functools.partial(kernel, temporal, chunk),
        grid=grid,
        in_specs=in_specs,
        out_specs=out_specs,
        out_shape=out_shape,
        cost_estimate=pl.CostEstimate(
            flops=tokens * parts * heads * P_SIZE * 128 * work,
            transcendentals=tokens * parts * heads * P_SIZE,
            bytes_accessed=tokens * parts * out_width * 8,
        ),
        name=name,
    )(*given)
    return [result[0].reshape(parts, tokens, out_width)] + list(result[1:])


def norm_forward(stream):
    center = stream - over_u(jnp.sum(stream, 1, keepdims=True)) / D
    inverse = lax.rsqrt(over_u(jnp.sum(center * center, 1, keepdims=True)) / D + EPSILON)
    return center * inverse, inverse


def norm_backward(grad_normed, normed, inverse):
    first, second = over_u(
        (
            jnp.sum(grad_normed, 1, keepdims=True),
            jnp.sum(grad_normed * normed, 1, keepdims=True),
        )
    )
    return inverse * (grad_normed - first / D - normed * (second / D))


def spread(vector, tokens):
    groups, width = vector.shape
    if groups == 1:
        return vector
    return jnp.broadcast_to(vector[:, None, :], (groups, tokens // groups, width)).reshape(tokens, width)


def group_sum(value, groups):
    return jnp.sum(value.reshape(groups, -1, value.shape[-1]), 1)


def shards(
    latents, cond, w_ada, b_ada, w_qkv, b_qv, w_out, b_out, w_fc1, b_fc1, w_fc2, b_fc2, cotangent
):
    batches, width, tokens = latents.shape
    lat_count = cond.shape[1]
    rows = lax.axis_size("row")
    parts = lax.axis_size("m")
    split = lax.axis_size("u")
    row = lax.axis_index("row")
    part_here = lax.axis_index("m")
    span = parts * width
    order = jnp.asarray(row_order(rows), jnp.int32)
    inverse_order = jnp.asarray(np.argsort(row_order(rows)), jnp.int32)
    part_ids = part_here ^ jnp.arange(parts)
    frames_dev = tokens // P_SIZE
    pos_block = tokens // (lat_count * NF)
    spatial = (frames_dev, P_SIZE)
    temporal = (lat_count, NF, pos_block)

    relative = split == 1
    depth = D // rows
    if relative:
        slot = jnp.arange(D)
        source = (row ^ order[slot // depth]) * depth + slot % depth
        exchange = (jnp.arange(D)[:, None] == source[None, :]).astype(bf16)

    def vector_rel(value):
        if not relative:
            return value
        shaped = value.reshape(value.shape[:-1] + (rows, depth))
        return jnp.take(shaped, row ^ order, axis=-2).reshape(value.shape)

    def vector_plain(value):
        if not relative:
            return value
        shaped = value.reshape(value.shape[:-1] + (rows, depth))
        return jnp.take(shaped, inverse_order[row ^ jnp.arange(rows)], axis=-2).reshape(value.shape)

    def stream_plain(value):
        return dot_nt(value, exchange).astype(bf16) if relative else value

    def stream_rel(value):
        return dot_nn(value, exchange) if relative else value.astype(f32)

    def to_positions(value):
        return stream_rel(send_positions(stream_plain(value.astype(bf16))))

    def send_positions(value):
        shaped = value.reshape(frames_dev, rows, pos_block, span).swapaxes(0, 1)
        return lax.all_to_all(shaped, "row", 0, 0).reshape(tokens, span)

    def to_frames(value):
        shaped = stream_plain(value.astype(bf16)).reshape(rows, frames_dev, pos_block, span)
        return lax.all_to_all(shaped, "row", 0, 0).swapaxes(0, 1).reshape(tokens, span)

    def gathered(gather):
        pieces = gather.pieces()
        arrays = [value.reshape(-1, value.shape[-1]) for value in gather.arrays]
        if relative:
            return Weight(arrays, pieces)
        places = inverse_order[row ^ jnp.arange(rows)]
        blocks = []
        for entries in pieces:
            entries = sorted(entries, key=lambda entry: entry[3])
            block = jnp.concatenate([arrays[n][a : a + count] for n, a, count, _ in entries], 0)
            blocks.append(jnp.take(block.reshape(rows, depth, -1), places, axis=0).reshape(block.shape))
        return Weight(blocks, [[(part, 0, D, 0)] for part in range(parts)])

    def scatter(stacks, kind):
        if not relative:
            stacks = [
                jnp.take(s.reshape(s.shape[0], rows, depth, -1), row ^ order, axis=1).reshape(s.shape)
                for s in stacks
            ]
        return Scatter(stacks[0], stacks[1], rows, parts, kind)

    def own_share(value):
        return value if relative else lax.dynamic_slice_in_dim(value, lax.axis_index("u") * span, span, 1)

    cond_float = cond.astype(f32)
    cond_low = jax.nn.silu(cond_float).astype(bf16)
    mod_partial = jnp.einsum("mlr,brjk->mlbjk", cond_low, w_ada, preferred_element_type=f32)
    mod_partial = mod_partial + jnp.where(row == 0, b_ada.astype(f32), 0.0)[None, None]
    small = jnp.concatenate(
        [b.astype(f32).reshape(-1) for b in (b_qv, b_out, b_fc1, b_fc2)]
    )
    packed = jnp.concatenate(
        [mod_partial.reshape(batches, -1), jnp.broadcast_to(small, (parts,) + small.shape)], 1
    )
    packed = lax.all_to_all(packed, "m", split_axis=0, concat_axis=0, tiled=True)
    mod_size = lat_count * 12 * width
    mod_here = all_sum(packed[:, :mod_size], "row").reshape(parts, lat_count, 2, 6, width)
    mod_here = vector_rel(jnp.moveaxis(mod_here, 0, -2).reshape(lat_count, 2, 6, span))
    small = packed[:, mod_size:]
    sizes = np.cumsum([0, 4 * width, 2 * width, 2 * b_fc1.shape[1], 2 * width])
    all_qv, all_out, all_fc1, all_fc2 = [small[:, a:b] for a, b in zip(sizes[:-1], sizes[1:])]
    all_qv = jnp.take(all_qv.reshape(parts, 2, 2, width), part_ids, axis=0)
    all_fc1 = jnp.take(all_fc1.reshape(parts, 2, -1), part_ids, axis=0)
    all_out = vector_rel(jnp.moveaxis(all_out.reshape(parts, 2, width), 0, 1).reshape(2, span))
    all_fc2 = vector_rel(jnp.moveaxis(all_fc2.reshape(parts, 2, width), 0, 1).reshape(2, span))

    zeros = jnp.zeros((parts, width), f32)
    bias_qkv = [
        jnp.concatenate([all_qv[:, b, 0], zeros, all_qv[:, b, 1]], 1)[:, None, :] for b in range(2)
    ]
    bias_fc1 = [all_fc1[:, b][:, None, :] for b in range(2)]
    hidden_width = w_fc1.shape[2]
    mixed_cols, out_cols, hidden_cols = (0, 3 * width), (3 * width, 4 * width), (0, hidden_width)
    layouts = (spatial, temporal)
    groups_of = (1, lat_count)

    def shard_of(b, name):
        if name == "mixed":
            return jnp.concatenate([w_qkv[b].reshape(depth, 3 * width), w_out[b]], 1)
        return (w_fc1 if name == "fc1" else w_fc2)[b]

    def own_batch(value):
        return lax.all_to_all(value, "m", 0, 0).reshape(span, tokens)

    def to_stream(value):
        return dot_tn(value, exchange) if relative else value.T.astype(f32)

    def to_argument(value):
        return lax.all_to_all(value.reshape(parts, width, tokens), "m", 0, 0)

    lat_here = row * frames_dev // NF
    mod_space = lax.dynamic_slice_in_dim(mod_here[:, 0], lat_here, 1, 0)
    mods = [
        [spread(m[:, column], tokens) for column in range(6)] for m in (mod_space, mod_here[:, 1])
    ]

    def open_stage(b, stream):
        normed, inverse = norm_forward(stream)
        hidden = features_all((normed * (1.0 + mods[b][1]) + mods[b][0]).astype(bf16))
        return {"stream": stream, "normed": normed, "inverse": inverse, "hidden": hidden}

    def attention_stage(b, k):
        qkv = project(
            k["hidden"], weights[b]["mixed"], mixed_cols, [bias_qkv[b]], lambda v, c: (v + c,), [bf16], "qkv"
        )[0]
        attended, logs = attention_call(forward_kernel, [qkv], None, layouts[b], width, 4, "attend")
        return {**k, "qkv": qkv, "attended": attended, "logs": logs}

    def middle_stage(b, k):
        branch = features_sum(contract(k["attended"], weights[b]["mixed"], out_cols, "out")) + all_out[b]
        middle = k["stream"] + mods[b][2] * branch
        normed, inverse = norm_forward(middle)
        hidden = features_all((normed * (1.0 + mods[b][4]) + mods[b][3]).astype(bf16))
        return {**k, "branch": branch, "middle": middle, "normed2": normed, "inverse2": inverse, "hidden2": hidden}

    def up_stage(b, k):
        act, slope = project(
            k["hidden2"], weights[b]["fc1"], hidden_cols, [bias_fc1[b]], gelu_pair, [bf16, bf16], "up"
        )
        return {**k, "act": act, "slope": slope}

    def down_stage(b, k):
        branch = features_sum(contract(k["act"], weights[b]["fc2"], hidden_cols, "down")) + all_fc2[b]
        return k["middle"] + mods[b][5] * branch, {**k, "branch2": branch}

    def fc2_grads(b, k, grad):
        low = features_all((mods[b][5] * grad).astype(bf16))
        stacks, (total_low,), _ = weight_grads([(low, k["act"])], "grad_fc2")
        return {**k, "grad": grad, "low2": low, "sum_b2": own_share(total_low)}, scatter(stacks, KINDS[b]["fc2"])

    def up_back(b, k):
        grad_pre = project(
            k["low2"], weights[b]["fc2"], hidden_cols, [k["slope"]],
            lambda v, s: (v * s.astype(f32),), [bf16], "up_back",
        )[0]
        stacks, _, (total_pre,) = weight_grads([(k["hidden2"], grad_pre)], "grad_fc1")
        return {**k, "pre": grad_pre, "sum_b1": total_pre[:, 0]}, scatter(stacks, KINDS[b]["fc1"])

    def hidden2_back(b, k):
        grad_hidden = features_sum(contract(k["pre"], weights[b]["fc1"], hidden_cols, "hidden2_back"))
        return {**k, "g_hidden2": grad_hidden}

    def attention_back(b, k):
        grad_hidden = k["g_hidden2"]
        back = norm_backward(grad_hidden * (1.0 + mods[b][4]), k["normed2"], k["inverse2"])
        middle = k["grad"] + back
        low = features_all((mods[b][2] * middle).astype(bf16))
        grad_att = project(low, weights[b]["mixed"], out_cols, [], lambda v: (v,), [bf16], "out_back")[0]
        grad_qkv = attention_call(
            backward_kernel, [k["qkv"], grad_att, k["attended"]], k["logs"], layouts[b], 3 * width, 10, "attend_back"
        )[0]
        return {**k, "g_middle": middle, "low1": low, "g_qkv": grad_qkv}

    def mixed_grads(b, k):
        stacks, (_, total_low), (total_qkv, _) = weight_grads(
            [(k["hidden"], k["g_qkv"]), (k["low1"], k["attended"])], "grad_mixed"
        )
        return {**k, "sum_bo": own_share(total_low), "sum_qkv": total_qkv[:, 0]}, scatter(stacks, KINDS[b]["mixed"])

    def stream_back(b, k):
        grad_hidden = features_sum(contract(k["g_qkv"], weights[b]["mixed"], mixed_cols, "hidden_back"))
        back = norm_backward(grad_hidden * (1.0 + mods[b][1]), k["normed"], k["inverse"])
        groups = groups_of[b]
        modulate_grad = jnp.stack(
            [
                group_sum(grad_hidden, groups),
                group_sum(grad_hidden * k["normed"], groups),
                group_sum(k["g_middle"] * k["branch"], groups),
                group_sum(k["g_hidden2"], groups),
                group_sum(k["g_hidden2"] * k["normed2"], groups),
                group_sum(k["grad"] * k["branch2"], groups),
            ],
            1,
        )
        biases = (
            k["sum_qkv"][:, :width], k["sum_qkv"][:, 2 * width :], k["sum_bo"], k["sum_b1"], k["sum_b2"],
        )
        return k["g_middle"] + back, (modulate_grad, biases)

    names = ("mixed", "fc1", "fc2")
    gathers = [Gather(shard_of(b, n), rows, parts, KINDS[b][n]) for b in range(2) for n in names]
    weights = [{}, {}]
    depth_of = len(gathers[0].plan)

    def move(*pairs):
        for item, until in pairs:
            while item.done < min(until, depth_of):
                item.step()

    def ready(number):
        weights[number // 3][names[number % 3]] = gathered(gathers[number])

    last = depth_of
    g = gathers
    first = depth_of - 3
    move((g[0], first - 1), (g[1], first - 1))
    first_in, grad_top = fence(g, (own_batch(latents), own_batch(cotangent)))
    move((g[0], first), (g[1], first))
    grad_top = send_positions(grad_top.T)
    grad_top, mods = fence(g, (grad_top, mods))
    move((g[0], last - 2), (g[1], last - 2), (g[2], first - 1), (g[3], first - 1))
    first_in, grad_top = to_stream(first_in), stream_rel(grad_top)
    first_in, grad_top = fence(g, (first_in, grad_top))
    move((g[0], last - 1), (g[1], last - 1), (g[2], first), (g[3], first))
    fence(g, ())
    move((g[0], last), (g[1], last), (g[2], last - 2), (g[3], last - 2), (g[4], first - 1), (g[5], first - 1))
    k0 = open_stage(0, first_in)
    k0 = fence(g, k0)
    ready(0)
    ready(1)
    move((g[2], last - 1), (g[3], last - 1), (g[4], first), (g[5], first))
    k0 = middle_stage(0, attention_stage(0, k0))
    k0, grad_top = fence(g, (k0, grad_top))
    move((g[2], last), (g[3], last), (g[4], last - 2), (g[5], last - 2))
    k0 = up_stage(0, k0)
    k0 = fence(g, k0)
    ready(2)
    ready(3)
    move((g[4], last - 1), (g[5], last - 1))
    first_out, k0 = down_stage(0, k0)
    k1 = open_stage(1, to_positions(first_out))
    k1 = attention_stage(1, k1)
    k0, k1 = fence(g, (k0, k1))
    move((g[4], last))
    k1 = middle_stage(1, k1)
    k0, k1 = fence(g, (k0, k1))
    ready(4)
    move((g[5], last))
    k1 = up_stage(1, k1)
    k1, s5 = fc2_grads(1, k1, grad_top)
    k0, k1 = fence(g + [s5], (k0, k1))
    ready(5)
    move((s5, 1))
    second_out, k1 = down_stage(1, k1)
    k1, s4 = up_back(1, k1)
    k0, k1, second_out = fence([s4, s5], (k0, k1, second_out))
    move((s4, 1))
    k1 = hidden2_back(1, k1)
    output = to_argument(to_frames(second_out).T)
    k0, k1 = fence([s4, s5], (k0, k1))
    move((s5, 2), (s4, 2))
    k1 = attention_back(1, k1)
    k1, s3 = mixed_grads(1, k1)
    k0, k1 = fence([s3, s4, s5], (k0, k1))
    move((s5, 3), (s4, 3), (s3, 1))
    grad_mid, small_time = stream_back(1, k1)
    grad_low = to_frames(grad_mid)
    k0, grad_low, small_time, output = fence([s3, s4, s5], (k0, grad_low, small_time, output))
    move((s3, 2), (s5, 4), (s4, 4))
    k0, s2 = fc2_grads(0, k0, stream_rel(grad_low))
    k0, s1 = up_back(0, k0)
    k0 = hidden2_back(0, k0)
    k0 = fence([s1, s2, s3, s4, s5], k0)
    move((s3, 3), (s5, last), (s4, last), (s2, 1), (s1, 1))
    k0 = attention_back(0, k0)
    k0 = fence([s1, s2, s3, s4, s5], k0)
    move((s2, 2), (s1, 2), (s3, 4))
    k0, s0 = mixed_grads(0, k0)
    grad_first, small_space = stream_back(0, k0)
    grad_first, small_space, small_time = fence(
        [s0, s1, s2, s3], (grad_first, small_space, small_time)
    )
    move((s2, 3), (s1, 3), (s0, 1), (s3, last))
    fence([s0, s1, s2, s3], ())
    move((s0, 2), (s2, 4), (s1, 4))
    fence([s0, s1, s2], ())
    move((s0, 3), (s2, last), (s1, last))
    for item in (s0, s1, s2, s3, s4, s5):
        move((item, last))
    mod_grad_space, biases_space = small_space
    mod_grad_time, biases_time = small_time
    weights_space = [item.result() for item in (s0, s1, s2)]
    weights_time = [item.result() for item in (s3, s4, s5)]
    grad_first = grad_first.astype(bf16)
    grad_first = dot_nt(exchange, grad_first).astype(bf16) if relative else grad_first.T
    grad_latents = to_argument(grad_first).astype(f32)

    onehot = (jnp.arange(lat_count) == lat_here).astype(f32)
    mod_grads = jnp.stack([onehot[:, None, None] * mod_grad_space, mod_grad_time], 1)
    mod_grads = vector_plain(mod_grads).reshape(lat_count, 2, 6, parts, width)
    mod_grads = jnp.moveaxis(mod_grads, -2, 0).reshape(parts, -1)

    def by_part(value):
        return jnp.take(value, part_ids, axis=0)

    def by_stream(value):
        return vector_plain(value).reshape(parts, width)

    pieces = [mod_grads]
    for space, time in zip(biases_space, biases_time):
        for value in (space, time):
            pieces.append(by_part(value) if value.shape[0] == parts else by_stream(value))
    counts = np.cumsum([0] + [piece.shape[1] for piece in pieces])
    packed = jnp.concatenate(pieces, 1)
    packed = lax.all_to_all(packed, "m", split_axis=0, concat_axis=0, tiled=True)
    mod_part = packed[:, : counts[1]]
    bias_part = jnp.sum(packed[:, counts[1] :], 0, keepdims=True)
    flat = jnp.concatenate([mod_part.reshape(1, -1), bias_part], 1)
    flat = all_sum(flat, "row")[0]
    mod_grad_low = flat[: batches * counts[1]].reshape(batches, lat_count, 2, 6, width).astype(bf16)
    bias_part = flat[batches * counts[1] :]
    bias_out = [bias_part[a - counts[1] : b - counts[1]] for a, b in zip(counts[1:-1], counts[2:])]
    grad_bias_qv = jnp.stack(
        [jnp.stack([bias_out[0], bias_out[2]]), jnp.stack([bias_out[1], bias_out[3]])]
    )
    grad_bias_out = jnp.stack(bias_out[4:6])
    grad_bias_fc1 = jnp.stack(bias_out[6:8])
    grad_bias_fc2 = jnp.stack(bias_out[8:10])
    grad_bias_ada = jnp.sum(mod_grad_low.astype(f32), (0, 1))
    grad_weight_ada = jnp.einsum("mlr,mlbjk->brjk", cond_low, mod_grad_low, preferred_element_type=f32)
    cond_partial = jnp.einsum("mlbjk,brjk->mlr", mod_grad_low, w_ada, preferred_element_type=f32)
    cond_total = over_u(all_sum(cond_partial, "m"))
    sigmoid_cond = jax.nn.sigmoid(cond_float)
    grad_condition = cond_total * sigmoid_cond * (1.0 + cond_float * (1.0 - sigmoid_cond))
    grad_weight_qkv, grad_weight_out, grad_weight_fc1, grad_weight_fc2 = [], [], [], []
    for mixed, first, second in (weights_space, weights_time):
        grad_weight_qkv.append(mixed[:, : 3 * width].reshape(depth, 3, width))
        grad_weight_out.append(mixed[:, 3 * width :])
        grad_weight_fc1.append(first)
        grad_weight_fc2.append(second)
    return (
        output,
        grad_latents,
        grad_condition,
        grad_weight_ada,
        grad_bias_ada,
        jnp.stack(grad_weight_qkv),
        grad_bias_qv,
        jnp.stack(grad_weight_out),
        grad_bias_out,
        jnp.stack(grad_weight_fc1),
        grad_bias_fc1,
        jnp.stack(grad_weight_fc2),
        grad_bias_fc2,
    )


def solution(mesh):
    rows, columns = mesh.devices.shape

    def placed(latents, *rest):
        parts = latents.shape[0]
        inner = Mesh(mesh.devices.reshape(rows, columns // parts, parts), ("row", "u", "m"))
        col = ("u", "m")
        in_specs = (
            P(None, col, "row"),
            P(None, None, "row"),
            P(None, "row", None, col),
            P(None, None, col),
            P(None, "row", None, col),
            P(None, None, col),
            P(None, "row", col),
            P(None, col),
            P(None, "row", col),
            P(None, col),
            P(None, "row", col),
            P(None, col),
            P(None, col, "row"),
        )
        out_specs = (P(None, col, "row"),) + in_specs[:1] + in_specs[1:-1]
        return jax.shard_map(
            shards, mesh=inner, in_specs=in_specs, out_specs=out_specs, check_vma=False
        )(latents, *rest)

    return placed
```

```python
import functools

import jax
import jax.numpy as jnp
import numpy as np
from jax import lax
from jax.experimental import pallas as pl
from jax.experimental.pallas import tpu as pltpu
from jax.sharding import Mesh
from jax.sharding import PartitionSpec as P

D = 1152
HD = 72
P_SIZE = 256
NF = 16
SCALE = HD ** (-0.5)
EPSILON = 1e-06


KINDS = ({"mixed": 0, "fc1": 1, "fc2": 0}, {"mixed": 1, "fc1": 0, "fc2": 1})

f32 = jnp.float32
bf16 = jnp.bfloat16


def bits_of(count):
    found = []
    bit = count // 2
    while bit:
        found.append(bit)
        bit //= 2
    return found


def swap(value, axis, bit):
    count = lax.axis_size(axis)
    return lax.ppermute(value, axis, [(i, i ^ bit) for i in range(count)])


def row_order(rows):
    order = [0]
    for bit in bits_of(rows):
        order = order + [j ^ bit for j in order]
    return order


def step_plan(rows, parts, kind):
    by_row = [("row", bit) for bit in bits_of(rows)]
    by_part = [("m", bit) for bit in bits_of(parts)]
    if kind == 0:
        return by_row + by_part
    return by_row[:-1] + by_part[:-1] + by_row[-1:] + by_part[-1:]


def moved(label, axis, bit):
    return (label[0] ^ bit, label[1]) if axis == "row" else (label[0], label[1] ^ bit)


def total(terms):
    result = terms[0].astype(f32)
    for term in terms[1:]:
        result = result + term.astype(f32)
    return result


def sum_rows(terms, names, first, count):
    width = terms[0][0].shape[2]
    rows = 576 if count % 576 == 0 else count // 2 if count % 32 == 0 else count
    assert first % rows == 0

    def body(*refs):
        value = refs[0][...].astype(f32)
        for ref in refs[1:-1]:
            value = value + ref[...].astype(f32)
        refs[-1][...] = value.astype(bf16)

    def spec(lead):
        return pl.BlockSpec((1, rows, width), lambda i, r: (lead + i, first // rows + r, 0))

    return pl.pallas_call(
        body,
        grid=(names, count // rows),
        in_specs=[spec(lead) for _, lead in terms],
        out_specs=pl.BlockSpec((1, rows, width), lambda i, r: (i, r, 0)),
        out_shape=jax.ShapeDtypeStruct((names, count, width), bf16),
        cost_estimate=pl.CostEstimate(
            flops=len(terms) * names * count * width,
            transcendentals=0,
            bytes_accessed=2 * (len(terms) + 1) * names * count * width,
        ),
        name="sum_rows",
    )(*[value for value, _ in terms])


class Gather:
    def __init__(self, shard, rows, parts, kind):
        self.rows, self.parts, self.depth = rows, parts, shard.shape[0]
        self.plan = step_plan(rows, parts, kind)
        self.labels = [[(0, 0)]]
        self.arrays = [shard]
        self.done = 0

    def step(self, after=None):
        axis, bit = self.plan[self.done]
        last_axis, last_bit = self.plan[-1]
        left = len(self.plan) - self.done

        def behind(value):
            return value if after is None else lax.optimization_barrier((value, after))[0]

        if left == 1:
            names, value = self.labels[1], self.arrays[1]
            result = swap(behind(value), axis, bit)
            self.labels.append([moved(name, axis, bit) for name in names])
            self.arrays.append(result)
        else:
            (names,), (value,) = self.labels, self.arrays
            result = after
            other = swap(value, axis, bit)
            other_names = [moved(name, axis, bit) for name in names]
            if left > 2:
                self.labels = [names + other_names]
                self.arrays = [jnp.concatenate([value, other], 0)]
            else:
                result = swap(behind(value), last_axis, last_bit)
                self.labels = [names, other_names, [moved(name, last_axis, last_bit) for name in names]]
                self.arrays = [value, other, result]
        self.done += 1
        return result

    def pieces(self):
        order, depth = row_order(self.rows), self.depth
        found = []
        for part in range(self.parts):
            entries = []
            for number, names in enumerate(self.labels):
                hits = [place for place, name in enumerate(names) if name[1] == part]
                if hits:
                    rank = order.index(names[hits[0]][0])
                    assert [names[h][0] for h in hits] == order[rank : rank + len(hits)]
                    assert hits == list(range(hits[0], hits[0] + len(hits)))
                    entries.append((number, hits[0] * depth, len(hits) * depth, rank * depth))
            found.append(entries)
        return found


class Scatter:
    def __init__(self, sent, kept, rows, parts, kind):
        self.plan = step_plan(rows, parts, kind)[::-1]
        self.order = row_order(rows)
        self.depth = kept.shape[1] // rows
        self.span = rows
        assert self.plan[0] == ("m", 1)
        self.arrays = [kept, sent]
        self.outgoing = 1
        self.gaining = [part for part in range(parts) if not part & 1]
        self.live = {part: [(0, place)] for place, part in enumerate(self.gaining)}
        self.done = 0

    def take(self, term, first, count):
        number, lead = term
        return self.arrays[number][lead, first : first + count]

    def sums(self, names, first, count):
        if self.depth % 16 == 0:
            leads = [[term[1] for term in terms] for terms in zip(*[self.live[n] for n in names])]
            numbers = [term[0] for term in self.live[names[0]]]
            assert all(list(l) == list(range(l[0], l[0] + len(l))) for l in leads)
            return sum_rows([(self.arrays[n], l[0]) for n, l in zip(numbers, leads)], len(names), first, count)
        return jnp.stack(
            [total([self.take(t, first, count) for t in self.live[n]]).astype(bf16) for n in names]
        )

    def step(self, after=None):
        axis, bit = self.plan[self.done]
        got = swap(self.arrays.pop(self.outgoing), axis, bit)
        if after is not None:
            got, _ = lax.optimization_barrier((got, after))
        self.arrays.append(got)
        for place, name in enumerate(self.gaining):
            self.live[name].append((len(self.arrays) - 1, place))
        self.done += 1
        self.prepare()

    def prepare(self):
        if self.done == len(self.plan):
            return
        axis, bit = self.plan[self.done]
        if axis == "m":
            names = [name for name in sorted(self.live) if name & bit]
            sent = self.sums(names, 0, self.span * self.depth)
            for name in names:
                self.live.pop(name)
            self.gaining = [name ^ bit for name in names]
        else:
            half = self.span // 2
            order = self.order
            assert all(order[half + p] == order[p] ^ bit for p in range(half))
            self.gaining = sorted(self.live)
            sent = self.sums(self.gaining, half * self.depth, half * self.depth)
            self.span = half
        self.outgoing = len(self.arrays)
        self.arrays.append(sent)

    def result(self):
        return total([self.take(t, 0, self.depth) for t in self.live[0]])


def fence(objects, values):
    arrays, values = lax.optimization_barrier(([o.arrays for o in objects], values))
    for o, fresh in zip(objects, arrays):
        o.arrays = list(fresh)
    return values


def all_sum(value, axis):
    for bit in bits_of(lax.axis_size(axis)):
        value = value + swap(value, axis, bit)
    return value


def over_u(value):
    return lax.psum(value, "u") if lax.axis_size("u") > 1 else value


def features_all(value):
    return lax.all_gather(value, "u", axis=1, tiled=True) if lax.axis_size("u") > 1 else value


def features_sum(value):
    if lax.axis_size("u") > 1:
        return lax.psum_scatter(value, "u", scatter_dimension=1, tiled=True)
    return value


def dot_nn(left, right):
    return lax.dot_general(left, right, (((1,), (0,)), ((), ())), preferred_element_type=f32)


def dot_nt(left, right):
    return lax.dot_general(left, right, (((1,), (1,)), ((), ())), preferred_element_type=f32)


def dot_tn(left, right):
    return lax.dot_general(left, right, (((0,), (0,)), ((), ())), preferred_element_type=f32)


LIMIT = 56 * 1024 * 1024


class Weight:
    def __init__(self, arrays, pieces):
        self.arrays = [value.reshape(-1, value.shape[-1]) for value in arrays]
        self.places = pieces
        self.parts = len(pieces)
        self.height = sum(rows for _, _, rows, _ in pieces[0])
        self.width = self.arrays[0].shape[1]

    def scratch(self):
        pieces = len(self.places[0])
        return [
            pltpu.VMEM((self.parts, self.height, self.width), bf16),
            pltpu.SemaphoreType.DMA((self.parts, pieces)),
        ]

    def copies(self, part, refs, held, sems):
        return [
            pltpu.make_async_copy(
                refs[number].at[pl.ds(start, rows)], held.at[part, pl.ds(to, rows)], sems.at[part, place]
            )
            for place, (number, start, rows, to) in enumerate(self.places[part])
        ]

    def arrive(self, step, refs, held, sems):
        @pl.when(step == 0)
        def _():
            for part in range(self.parts):
                for copy in self.copies(part, refs, held, sems):
                    copy.start()

        for part in range(self.parts):

            @pl.when(step == part)
            def _(part=part):
                for copy in self.copies(part, refs, held, sems):
                    copy.wait()


def cut_last(load, low, high):
    base = low // 128 * 128
    value = load(base, high)
    return value if base == low else value[:, low - base :]


def whole_spec(shape):
    return pl.BlockSpec(shape, lambda s: (0,) * len(shape))


def part_spec(shape):
    return pl.BlockSpec((1,) + shape, lambda s: (s,) + (0,) * len(shape))


def project(x, weight, columns, extras, epilogue, out_types, name):
    tokens, depth = x.shape
    low, high = columns
    n = high - low
    count = len(weight.arrays)

    def body(*refs):
        x_ref, refs = refs[0], refs[1:]
        w_refs, refs = refs[:count], refs[count:]
        extra_refs, refs = refs[: len(extras)], refs[len(extras) :]
        outs, (held, sems) = refs[: len(out_types)], refs[len(out_types) :]
        step = pl.program_id(0)
        weight.arrive(step, w_refs, held, sems)
        left = x_ref[...]
        right = cut_last(lambda a, b: held[step, :, a:b], low, high)
        made = epilogue(dot_nn(left, right), *[e[0] for e in extra_refs])
        for out, piece in zip(outs, made):
            out[0] = piece.astype(out.dtype)

    return pl.pallas_call(
        body,
        grid=(weight.parts,),
        in_specs=[whole_spec((tokens, depth))]
        + [pl.BlockSpec(memory_space=pl.ANY)] * count
        + [part_spec(e.shape[1:]) for e in extras],
        out_specs=[part_spec((tokens, n))] * len(out_types),
        out_shape=[jax.ShapeDtypeStruct((weight.parts, tokens, n), t) for t in out_types],
        scratch_shapes=weight.scratch(),
        compiler_params=pltpu.CompilerParams(vmem_limit_bytes=LIMIT),
        cost_estimate=pl.CostEstimate(
            flops=2 * tokens * depth * n * weight.parts,
            transcendentals=0,
            bytes_accessed=2 * weight.parts * n * (depth + 2 * tokens),
        ),
        name=name,
    )(x, *weight.arrays, *extras)


def contract(xs, weight, columns, name, large=(), small=(), outs=None, finish=None):
    parts, tokens, n = xs.shape
    low, high = columns
    count = len(weight.arrays)
    height = weight.height
    if finish is None:
        outs = [jax.ShapeDtypeStruct((tokens, height), f32)]

    def body(*refs):
        x_ref, refs = refs[0], refs[1:]
        w_refs, refs = refs[:count], refs[count:]
        large_refs, refs = refs[: len(large)], refs[len(large) :]
        small_refs, refs = refs[: len(small)], refs[len(small) :]
        out_refs, refs = refs[: len(outs)], refs[len(outs) :]
        held, sems = refs[:2]
        step = pl.program_id(0)
        acc = out_refs[0]
        if finish is not None:
            acc, local, large_sems = refs[2], refs[3:-1], refs[-1]
            copies = [
                pltpu.make_async_copy(ref, to, large_sems.at[place])
                for place, (ref, to) in enumerate(zip(large_refs, local))
            ]
        weight.arrive(step, w_refs, held, sems)
        if finish is not None:

            @pl.when(step == 0)
            def _():
                for copy in copies:
                    copy.start()

        right = cut_last(lambda a, b: held[step, :, a:b], low, high)
        value = dot_nt(x_ref[0], right)

        @pl.when(step == 0)
        def _():
            acc[...] = value

        @pl.when(step > 0)
        def _():
            acc[...] += value

        if finish is not None:

            @pl.when(step == parts - 1)
            def _():
                for copy in copies:
                    copy.wait()
                finish(acc, local, small_refs, out_refs)

    scratch = weight.scratch()
    if finish is not None:
        scratch.append(pltpu.VMEM((tokens, height), f32))
        scratch += [pltpu.VMEM(value.shape, value.dtype) for value in large]
        scratch.append(pltpu.SemaphoreType.DMA((max(len(large), 1),)))
    results = pl.pallas_call(
        body,
        grid=(parts,),
        in_specs=[part_spec((tokens, n))]
        + [pl.BlockSpec(memory_space=pl.ANY)] * (count + len(large))
        + [whole_spec(value.shape) for value in small],
        out_specs=[whole_spec(out.shape) for out in outs],
        out_shape=outs,
        scratch_shapes=scratch,
        compiler_params=pltpu.CompilerParams(vmem_limit_bytes=LIMIT),
        cost_estimate=pl.CostEstimate(
            flops=2 * tokens * height * n * parts,
            transcendentals=0,
            bytes_accessed=2 * parts * n * (height + tokens) + 4 * tokens * height * (1 + len(large)),
        ),
        name=name,
    )(xs, *weight.arrays, *large, *small)
    return results[0] if finish is None else results


ROWS = 32


def by_rows(tokens, work, sums=0, width=0):
    def turn(index, carried):
        made = work(pl.ds(pl.multiple_of(index * ROWS, ROWS), ROWS))
        return tuple(c + jnp.sum(m, 0, keepdims=True) for c, m in zip(carried, made or ()))

    return lax.fori_loop(0, tokens // ROWS, turn, (jnp.zeros((1, width), f32),) * sums)


def finish_middle(acc, large, small, outs):
    (stream,), (bias, gate, scale, shift) = large, small
    branch_out, middle_out, normed_out, inverse_out, hidden_out = outs

    def work(rows):
        branch = acc[rows, :] + bias[...]
        middle = stream[rows, :] + gate[...] * branch
        center = middle - jnp.sum(middle, 1, keepdims=True) / D
        inverse = lax.rsqrt(jnp.sum(center * center, 1, keepdims=True) / D + EPSILON)
        normed = center * inverse
        branch_out[rows, :] = branch
        middle_out[rows, :] = middle
        normed_out[rows, :] = normed
        inverse_out[rows, :] = inverse
        hidden_out[rows, :] = (normed * (1.0 + scale[...]) + shift[...]).astype(bf16)

    by_rows(acc.shape[0], work)


def finish_stream(acc, large, small, outs):
    (middle,), (bias, gate) = large, small
    branch_out, result_out = outs

    def work(rows):
        branch = acc[rows, :] + bias[...]
        branch_out[rows, :] = branch
        result_out[rows, :] = (middle[rows, :] + gate[...] * branch).astype(bf16)

    by_rows(acc.shape[0], work)


def norm_back(grad_hidden, scale, normed, inverse):
    grad_normed = grad_hidden * (1.0 + scale)
    first = jnp.sum(grad_normed, 1, keepdims=True) / D
    second = jnp.sum(grad_normed * normed, 1, keepdims=True) / D
    return inverse * (grad_normed - first - normed * second)


def finish_middle_back(acc, large, small, outs):
    (grad, normed, branch, inverse), (scale, gate) = large, small
    middle_out, low_out, sums_out = outs

    def work(rows):
        grad_hidden = acc[rows, :]
        middle = grad[rows, :] + norm_back(grad_hidden, scale[...], normed[rows, :], inverse[rows, :])
        middle_out[rows, :] = middle
        low_out[rows, :] = (gate[...] * middle).astype(bf16)
        return grad_hidden, grad_hidden * normed[rows, :], middle * branch[rows, :]

    made = by_rows(acc.shape[0], work, 3, acc.shape[1])
    sums_out[...] = jnp.concatenate(made, 0)


def finish_stream_back(acc, large, small, outs):
    (middle, normed, inverse), (scale,) = large, small
    stream_out, sums_out = outs

    def work(rows):
        grad_hidden = acc[rows, :]
        back = norm_back(grad_hidden, scale[...], normed[rows, :], inverse[rows, :])
        stream_out[rows, :] = (middle[rows, :] + back).astype(bf16)
        return grad_hidden, grad_hidden * normed[rows, :]

    made = by_rows(acc.shape[0], work, 2, acc.shape[1])
    sums_out[...] = jnp.concatenate(made, 0)


def weight_grads(pairs, cuts, name):
    tokens, depth = pairs[0][0].shape
    parts = pairs[0][1].shape[0]
    half = parts // 2
    widths = [g.shape[2] for _, g in pairs]
    full = sum(widths)
    count = len(pairs)

    def which(step):
        return jnp.where(step < half, 2 * step + 1, 2 * (step - half))

    def body(*refs):
        x_refs, refs = refs[:count], refs[count:]
        g_refs, refs = refs[:count], refs[count:]
        sent, refs = refs[: len(cuts)], refs[len(cuts) :]
        kept, refs = refs[: len(cuts)], refs[len(cuts) :]
        x_sums, refs = refs[:count], refs[count:]
        g_sums, turned = refs[:count], refs[count:]
        step = pl.program_id(0)

        @pl.when(step == 0)
        def _():
            for x_ref, x_sum, t_ref in zip(x_refs, x_sums, turned):
                value = x_ref[...].astype(f32)
                x_sum[...] = jnp.sum(value, 0, keepdims=True)
                t_ref[...] = value.T.astype(bf16)

        rights = [g_ref[0] for g_ref in g_refs]
        for right, g_sum in zip(rights, g_sums):
            g_sum[0] = jnp.sum(right.astype(f32), 0, keepdims=True)

        def fill(outs):
            made = [dot_nn(t_ref[...], r).astype(bf16) for t_ref, r in zip(turned, rights)]
            made = made[0] if count == 1 else jnp.concatenate(made, 1)
            for out, (low, high) in zip(outs, cuts):
                out[0] = made[:, low:high]

        @pl.when(step < half)
        def _():
            fill(sent)

        @pl.when(step >= half)
        def _():
            fill(kept)

    outs = pl.pallas_call(
        body,
        grid=(parts,),
        in_specs=[whole_spec((tokens, depth))] * count
        + [pl.BlockSpec((1, tokens, n), lambda s: (which(s), 0, 0)) for n in widths],
        out_specs=[
            pl.BlockSpec((1, depth, high - low), lambda s: (jnp.minimum(s, half - 1), 0, 0))
            for low, high in cuts
        ]
        + [
            pl.BlockSpec((1, depth, high - low), lambda s: (jnp.maximum(s - half, 0), 0, 0))
            for low, high in cuts
        ]
        + [whole_spec((1, depth))] * count
        + [pl.BlockSpec((1, 1, n), lambda s: (which(s), 0, 0)) for n in widths],
        out_shape=[jax.ShapeDtypeStruct((half, depth, high - low), bf16) for low, high in cuts] * 2
        + [jax.ShapeDtypeStruct((1, depth), f32)] * count
        + [jax.ShapeDtypeStruct((parts, 1, n), f32) for n in widths],
        scratch_shapes=[pltpu.VMEM((depth, tokens), bf16)] * count,
        compiler_params=pltpu.CompilerParams(vmem_limit_bytes=LIMIT),
        cost_estimate=pl.CostEstimate(
            flops=2 * tokens * depth * full * parts,
            transcendentals=0,
            bytes_accessed=2 * parts * full * (depth + tokens),
        ),
        name=name,
    )(*[x for x, _ in pairs], *[g for _, g in pairs])
    ranges = len(cuts)
    stacks = list(zip(outs[:ranges], outs[ranges : 2 * ranges]))
    outs = outs[2 * ranges :]
    return stacks, outs[:count], outs[count:]


def gelu_pair(value, bias):
    v = value + bias
    slope = 0.7978845608028654
    inner = jnp.tanh(slope * (v + 0.044715 * v * v * v))
    outer = 0.5 * (1.0 + inner)
    change = outer + 0.5 * v * (1.0 - inner * inner) * (slope * (1.0 + 3.0 * 0.044715 * v * v))
    return v * outer, change


POWER = SCALE * 1.4426950408889634


def allowed_pairs(temporal, span, tokens):
    if not temporal:
        return None
    first = lax.broadcasted_iota(jnp.int32, (tokens, tokens), 0)
    second = lax.broadcasted_iota(jnp.int32, (tokens, tokens), 1)
    return lax.rem(first, span) == lax.rem(second, span)


def head_columns(block, start, width):
    return [block[:, c * width + start : c * width + start + HD] for c in range(3)]


def forward_kernel(temporal, span, qkv, out, logs):
    width = qkv.shape[-1] // 3
    tokens = int(np.prod(qkv.shape[:-1]))
    allowed = allowed_pairs(temporal, span, tokens)
    block = qkv[...].reshape(tokens, 3 * width)
    done, kept = [], []
    for start in range(0, width, HD):
        query, key, value = head_columns(block, start, width)
        scores = dot_nt(key, query)
        if allowed is not None:
            scores = jnp.where(allowed, scores, -jnp.inf)
        largest = jnp.max(scores, 0, keepdims=True)
        powered = jnp.exp2((scores - largest) * POWER)
        summed = jnp.sum(powered, 0, keepdims=True)
        done.append(dot_tn(value, powered.astype(bf16)) / summed)
        kept.append(largest * POWER + jnp.log2(summed))
    out[...] = jnp.concatenate(done, 0).T.astype(bf16).reshape(out.shape)
    logs[...] = jnp.concatenate(kept, 0).reshape(logs.shape)


def backward_kernel(temporal, span, qkv, grad, attended, logs, out):
    width = qkv.shape[-1] // 3
    tokens = int(np.prod(qkv.shape[:-1]))
    allowed = allowed_pairs(temporal, span, tokens)
    block = qkv[...].reshape(tokens, 3 * width)
    outer = grad[...].reshape(tokens, width)
    turned = outer.astype(f32).T * attended[...].reshape(tokens, width).astype(f32).T
    log_rows = logs[...].reshape(width // HD, tokens)
    pieces = [[], [], []]
    for place, start in enumerate(range(0, width, HD)):
        query, key, value = head_columns(block, start, width)
        above = outer[:, start : start + HD]
        inner = jnp.sum(turned[start : start + HD], 0, keepdims=True)
        weights = jnp.exp2(dot_nt(key, query) * POWER - log_rows[place : place + 1])
        if allowed is not None:
            weights = jnp.where(allowed, weights, 0.0)
        grad_scores = (weights * (dot_nt(value, above) - inner)).astype(bf16)
        pieces[0].append(dot_tn(key, grad_scores) * SCALE)
        pieces[1].append((dot_nn(grad_scores, query) * SCALE).astype(bf16))
        pieces[2].append(dot_nn(weights.astype(bf16), above).astype(bf16))
    first = jnp.concatenate(pieces[0], 0).T.astype(bf16)
    out[...] = jnp.concatenate([first] + pieces[1] + pieces[2], 1).reshape(out.shape)


def attention_call(kernel, values, logs, layout, out_width, work, name):
    parts, tokens, triple = values[0].shape
    heads = triple // 3 // HD
    temporal = len(layout) == 3
    chunk = 16
    grid = (parts, layout[0])
    if temporal:
        assert layout[2] % chunk == 0
        grid = grid + (layout[2] // chunk,)
    groups = tokens // P_SIZE

    def spec(width):
        if temporal:
            return pl.BlockSpec((1, 1, layout[1], chunk, width), lambda p, g, c: (p, g, 0, c, 0))
        return pl.BlockSpec((1, 1, layout[1], width), lambda p, g: (p, g, 0, 0))

    if temporal:
        log_spec = pl.BlockSpec((1, 1, heads, P_SIZE), lambda p, g, c: (p, g * grid[2] + c, 0, 0))
    else:
        log_spec = pl.BlockSpec((1, 1, heads, P_SIZE), lambda p, g: (p, g, 0, 0))
    out_shape = [jax.ShapeDtypeStruct((parts,) + layout + (out_width,), bf16)]
    out_specs = [spec(out_width)]
    in_specs = [spec(v.shape[-1]) for v in values]
    given = [v.reshape((parts,) + layout + (v.shape[-1],)) for v in values]
    if logs is None:
        out_shape.append(jax.ShapeDtypeStruct((parts, groups, heads, P_SIZE), f32))
        out_specs.append(log_spec)
    else:
        in_specs.append(log_spec)
        given.append(logs)
    result = pl.pallas_call(
        functools.partial(kernel, temporal, chunk),
        grid=grid,
        in_specs=in_specs,
        out_specs=out_specs,
        out_shape=out_shape,
        cost_estimate=pl.CostEstimate(
            flops=tokens * parts * heads * P_SIZE * 128 * work,
            transcendentals=tokens * parts * heads * P_SIZE,
            bytes_accessed=tokens * parts * out_width * 8,
        ),
        name=name,
    )(*given)
    return [result[0].reshape(parts, tokens, out_width)] + list(result[1:])


def norm_forward(stream):
    center = stream - over_u(jnp.sum(stream, 1, keepdims=True)) / D
    inverse = lax.rsqrt(over_u(jnp.sum(center * center, 1, keepdims=True)) / D + EPSILON)
    return center * inverse, inverse


def norm_backward(grad_normed, normed, inverse):
    first, second = over_u(
        (
            jnp.sum(grad_normed, 1, keepdims=True),
            jnp.sum(grad_normed * normed, 1, keepdims=True),
        )
    )
    return inverse * (grad_normed - first / D - normed * (second / D))


def spread(vector, tokens):
    groups, width = vector.shape
    if groups == 1:
        return vector
    return jnp.broadcast_to(vector[:, None, :], (groups, tokens // groups, width)).reshape(tokens, width)


def group_sum(value, groups):
    return jnp.sum(value.reshape(groups, -1, value.shape[-1]), 1)


def shards(
    latents, cond, w_ada, b_ada, w_qkv, b_qv, w_out, b_out, w_fc1, b_fc1, w_fc2, b_fc2, cotangent
):
    batches, width, tokens = latents.shape
    lat_count = cond.shape[1]
    rows = lax.axis_size("row")
    parts = lax.axis_size("m")
    split = lax.axis_size("u")
    row = lax.axis_index("row")
    part_here = lax.axis_index("m")
    span = parts * width
    order = jnp.asarray(row_order(rows), jnp.int32)
    inverse_order = jnp.asarray(np.argsort(row_order(rows)), jnp.int32)
    part_ids = part_here ^ jnp.arange(parts)
    frames_dev = tokens // P_SIZE
    pos_block = tokens // (lat_count * NF)
    spatial = (frames_dev, P_SIZE)
    temporal = (lat_count, NF, pos_block)

    relative = split == 1
    depth = D // rows
    if relative:
        slot = jnp.arange(D)
        source = (row ^ order[slot // depth]) * depth + slot % depth
        exchange = (jnp.arange(D)[:, None] == source[None, :]).astype(bf16)

    def vector_rel(value):
        if not relative:
            return value
        shaped = value.reshape(value.shape[:-1] + (rows, depth))
        return jnp.take(shaped, row ^ order, axis=-2).reshape(value.shape)

    def vector_plain(value):
        if not relative:
            return value
        shaped = value.reshape(value.shape[:-1] + (rows, depth))
        return jnp.take(shaped, inverse_order[row ^ jnp.arange(rows)], axis=-2).reshape(value.shape)

    def stream_plain(value):
        return dot_nt(value, exchange).astype(bf16) if relative else value

    def stream_rel(value):
        return dot_nn(value, exchange) if relative else value.astype(f32)

    def to_positions(value):
        return stream_rel(send_positions(stream_plain(value.astype(bf16))))

    def send_positions(value):
        shaped = value.reshape(frames_dev, rows, pos_block, span).swapaxes(0, 1)
        return lax.all_to_all(shaped, "row", 0, 0).reshape(tokens, span)

    def to_frames(value):
        return send_frames(stream_plain(value.astype(bf16)))

    def send_frames(value):
        shaped = value.reshape(rows, frames_dev, pos_block, span)
        return lax.all_to_all(shaped, "row", 0, 0).swapaxes(0, 1).reshape(tokens, span)

    def gathered(gather):
        pieces = gather.pieces()
        arrays = [value.reshape(-1, value.shape[-1]) for value in gather.arrays]
        if relative:
            return Weight(arrays, pieces)
        places = inverse_order[row ^ jnp.arange(rows)]
        blocks = []
        for entries in pieces:
            entries = sorted(entries, key=lambda entry: entry[3])
            block = jnp.concatenate([arrays[n][a : a + count] for n, a, count, _ in entries], 0)
            blocks.append(jnp.take(block.reshape(rows, depth, -1), places, axis=0).reshape(block.shape))
        return Weight(blocks, [[(part, 0, D, 0)] for part in range(parts)])

    def scatter(stacks, kind):
        if not relative:
            stacks = [
                jnp.take(s.reshape(s.shape[0], rows, depth, -1), row ^ order, axis=1).reshape(s.shape)
                for s in stacks
            ]
        return Scatter(stacks[0], stacks[1], rows, parts, kind)

    def own_share(value):
        return value if relative else lax.dynamic_slice_in_dim(value, lax.axis_index("u") * span, span, 1)

    cond_float = cond.astype(f32)
    cond_low = jax.nn.silu(cond_float).astype(bf16)
    mod_partial = jnp.einsum("mlr,brjk->mlbjk", cond_low, w_ada, preferred_element_type=f32)
    mod_partial = mod_partial + jnp.where(row == 0, b_ada.astype(f32), 0.0)[None, None]
    small = jnp.concatenate(
        [b.astype(f32).reshape(-1) for b in (b_qv, b_out, b_fc1, b_fc2)]
    )
    packed = jnp.concatenate(
        [mod_partial.reshape(batches, -1), jnp.broadcast_to(small, (parts,) + small.shape)], 1
    )
    packed = lax.all_to_all(packed, "m", split_axis=0, concat_axis=0, tiled=True)
    mod_size = lat_count * 12 * width
    mod_here = all_sum(packed[:, :mod_size], "row").reshape(parts, lat_count, 2, 6, width)
    mod_here = vector_rel(jnp.moveaxis(mod_here, 0, -2).reshape(lat_count, 2, 6, span))
    small = packed[:, mod_size:]
    sizes = np.cumsum([0, 4 * width, 2 * width, 2 * b_fc1.shape[1], 2 * width])
    all_qv, all_out, all_fc1, all_fc2 = [small[:, a:b] for a, b in zip(sizes[:-1], sizes[1:])]
    all_qv = jnp.take(all_qv.reshape(parts, 2, 2, width), part_ids, axis=0)
    all_fc1 = jnp.take(all_fc1.reshape(parts, 2, -1), part_ids, axis=0)
    all_out = vector_rel(jnp.moveaxis(all_out.reshape(parts, 2, width), 0, 1).reshape(2, span))
    all_fc2 = vector_rel(jnp.moveaxis(all_fc2.reshape(parts, 2, width), 0, 1).reshape(2, span))

    zeros = jnp.zeros((parts, width), f32)
    bias_qkv = [
        jnp.concatenate([all_qv[:, b, 0], zeros, all_qv[:, b, 1]], 1)[:, None, :] for b in range(2)
    ]
    bias_fc1 = [all_fc1[:, b][:, None, :] for b in range(2)]
    hidden_width = w_fc1.shape[2]
    mixed_cols, out_cols, hidden_cols = (0, 3 * width), (3 * width, 4 * width), (0, hidden_width)
    middle_cut = 4 * width // 256 * 128 + 128
    mixed_cuts = [(0, middle_cut), (middle_cut, 4 * width)]
    layouts = (spatial, temporal)
    groups_of = (1, lat_count)

    def shard_of(b, name):
        if name == "mixed":
            return jnp.concatenate([w_qkv[b].reshape(depth, 3 * width), w_out[b]], 1)
        return (w_fc1 if name == "fc1" else w_fc2)[b]

    def own_batch(value):
        return lax.all_to_all(value, "m", 0, 0).reshape(span, tokens)

    def to_stream(value):
        return dot_tn(value, exchange) if relative else value.T.astype(f32)

    def to_argument(value):
        return lax.all_to_all(value.reshape(parts, width, tokens), "m", 0, 0)

    lat_here = row * frames_dev // NF
    mod_space = lax.dynamic_slice_in_dim(mod_here[:, 0], lat_here, 1, 0)
    mods = [
        [spread(m[:, column], tokens) for column in range(6)] for m in (mod_space, mod_here[:, 1])
    ]

    def open_stage(b, stream):
        normed, inverse = norm_forward(stream)
        hidden = features_all((normed * (1.0 + mods[b][1]) + mods[b][0]).astype(bf16))
        return {"stream": stream, "normed": normed, "inverse": inverse, "hidden": hidden}

    def attention_stage(b, k):
        qkv = project(
            k["hidden"], weights[b]["mixed"], mixed_cols, [bias_qkv[b]], lambda v, c: (v + c,), [bf16], "qkv"
        )[0]
        attended, logs = attention_call(forward_kernel, [qkv], None, layouts[b], width, 4, "attend")
        return {**k, "qkv": qkv, "attended": attended, "logs": logs}

    fused = relative and lat_count == 1

    def shaped(*kinds):
        return [jax.ShapeDtypeStruct(shape, kind) for shape, kind in kinds]

    full = (tokens, span)

    def middle_stage(b, k):
        if fused:
            made = contract(
                k["attended"], weights[b]["mixed"], out_cols, "out",
                [k["stream"]], [all_out[b][None], mods[b][2], mods[b][4], mods[b][3]],
                shaped((full, f32), (full, f32), (full, f32), ((tokens, 1), f32), (full, bf16)),
                finish_middle,
            )
            return {**k, **dict(zip(("branch", "middle", "normed2", "inverse2", "hidden2"), made))}
        branch = features_sum(contract(k["attended"], weights[b]["mixed"], out_cols, "out")) + all_out[b]
        middle = k["stream"] + mods[b][2] * branch
        normed, inverse = norm_forward(middle)
        hidden = features_all((normed * (1.0 + mods[b][4]) + mods[b][3]).astype(bf16))
        return {**k, "branch": branch, "middle": middle, "normed2": normed, "inverse2": inverse, "hidden2": hidden}

    def up_stage(b, k):
        act, slope = project(
            k["hidden2"], weights[b]["fc1"], hidden_cols, [bias_fc1[b]], gelu_pair, [bf16, bf16], "up"
        )
        return {**k, "act": act, "slope": slope}

    def down_stage(b, k):
        if fused:
            branch, result = contract(
                k["act"], weights[b]["fc2"], hidden_cols, "down",
                [k["middle"]], [all_fc2[b][None], mods[b][5]],
                shaped((full, f32), (full, bf16)), finish_stream,
            )
            return result, {**k, "branch2": branch}
        branch = features_sum(contract(k["act"], weights[b]["fc2"], hidden_cols, "down")) + all_fc2[b]
        return k["middle"] + mods[b][5] * branch, {**k, "branch2": branch}

    def fc2_grads(b, k, grad):
        low = features_all((mods[b][5] * grad).astype(bf16))
        stacks, (total_low,), _ = weight_grads([(low, k["act"])], [hidden_cols], "grad_fc2")
        return {**k, "grad": grad, "low2": low, "sum_b2": own_share(total_low)}, scatter(stacks[0], KINDS[b]["fc2"])

    def up_back(b, k):
        grad_pre = project(
            k["low2"], weights[b]["fc2"], hidden_cols, [k["slope"]],
            lambda v, s: (v * s.astype(f32),), [bf16], "up_back",
        )[0]
        stacks, _, (total_pre,) = weight_grads([(k["hidden2"], grad_pre)], [hidden_cols], "grad_fc1")
        return {**k, "pre": grad_pre, "sum_b1": total_pre[:, 0]}, scatter(stacks[0], KINDS[b]["fc1"])

    def hidden2_back(b, k):
        if fused:
            middle, low, sums = contract(
                k["pre"], weights[b]["fc1"], hidden_cols, "hidden2_back",
                [k["grad"], k["normed2"], k["branch"], k["inverse2"]], [mods[b][4], mods[b][2]],
                shaped((full, f32), (full, bf16), ((3, span), f32)), finish_middle_back,
            )
            return {**k, "g_middle": middle, "low1": low, "sums2": sums}
        grad_hidden = features_sum(contract(k["pre"], weights[b]["fc1"], hidden_cols, "hidden2_back"))
        return {**k, "g_hidden2": grad_hidden}

    def attention_back(b, k):
        if fused:
            middle, low = k["g_middle"], k["low1"]
        else:
            grad_hidden = k["g_hidden2"]
            back = norm_backward(grad_hidden * (1.0 + mods[b][4]), k["normed2"], k["inverse2"])
            middle = k["grad"] + back
            low = features_all((mods[b][2] * middle).astype(bf16))
        grad_att = project(low, weights[b]["mixed"], out_cols, [], lambda v: (v,), [bf16], "out_back")[0]
        grad_qkv = attention_call(
            backward_kernel, [k["qkv"], grad_att, k["attended"]], k["logs"], layouts[b], 3 * width, 10, "attend_back"
        )[0]
        return {**k, "g_middle": middle, "low1": low, "g_qkv": grad_qkv}

    def mixed_grads(b, k):
        stacks, (_, total_low), (total_qkv, _) = weight_grads(
            [(k["hidden"], k["g_qkv"]), (k["low1"], k["attended"])], mixed_cuts, "grad_mixed"
        )
        return {**k, "sum_bo": own_share(total_low), "sum_qkv": total_qkv[:, 0]}, [
            scatter(pair, kind) for kind, pair in enumerate(stacks)
        ]

    def stream_back(b, k):
        biases = (
            k["sum_qkv"][:, :width], k["sum_qkv"][:, 2 * width :], k["sum_bo"], k["sum_b1"], k["sum_b2"],
        )
        if fused:
            stream, sums = contract(
                k["g_qkv"], weights[b]["mixed"], mixed_cols, "hidden_back",
                [k["g_middle"], k["normed"], k["inverse"]], [mods[b][1]],
                shaped((full, bf16), ((2, span), f32)), finish_stream_back,
            )
            return stream, ((sums, k["sums2"], k["grad"], k["branch2"]), biases)
        grad_hidden = features_sum(contract(k["g_qkv"], weights[b]["mixed"], mixed_cols, "hidden_back"))
        back = norm_backward(grad_hidden * (1.0 + mods[b][1]), k["normed"], k["inverse"])
        groups = groups_of[b]
        modulate_grad = jnp.stack(
            [
                group_sum(grad_hidden, groups),
                group_sum(grad_hidden * k["normed"], groups),
                group_sum(k["g_middle"] * k["branch"], groups),
                group_sum(k["g_hidden2"], groups),
                group_sum(k["g_hidden2"] * k["normed2"], groups),
                group_sum(k["grad"] * k["branch2"], groups),
            ],
            1,
        )
        return k["g_middle"] + back, (modulate_grad, biases)

    def modulate_sums(made):
        if not fused:
            return made
        sums, sums2, grad, branch = made
        last_sum = jnp.sum(grad * branch, 0, keepdims=True)
        return jnp.concatenate([sums, sums2[2:], sums2[:2], last_sum], 0)[None]

    def pack_small(small_space, small_time):
        mod_grad_space, biases_space = modulate_sums(small_space[0]), small_space[1]
        mod_grad_time, biases_time = modulate_sums(small_time[0]), small_time[1]
        onehot = (jnp.arange(lat_count) == lat_here).astype(f32)
        mod_grads = jnp.stack([onehot[:, None, None] * mod_grad_space, mod_grad_time], 1)
        mod_grads = vector_plain(mod_grads).reshape(lat_count, 2, 6, parts, width)
        mod_grads = jnp.moveaxis(mod_grads, -2, 0).reshape(parts, -1)

        def by_part(value):
            return jnp.take(value, part_ids, axis=0)

        def by_stream(value):
            return vector_plain(value).reshape(parts, width)

        pieces = [mod_grads]
        for space, time in zip(biases_space, biases_time):
            for value in (space, time):
                pieces.append(by_part(value) if value.shape[0] == parts else by_stream(value))
        counts = np.cumsum([0] + [piece.shape[1] for piece in pieces])
        packed = jnp.concatenate(pieces, 1)
        packed = lax.all_to_all(packed, "m", split_axis=0, concat_axis=0, tiled=True)
        return packed, counts

    names = ("mixed", "fc1", "fc2")
    gathers = [Gather(shard_of(b, n), rows, parts, KINDS[b][n]) for b in range(2) for n in names]
    weights = [{}, {}]
    depth_of = len(gathers[0].plan)

    def move(*pairs, after=None):
        tail = None
        for item, until in pairs:
            while item.done < min(until, depth_of):
                if isinstance(item, Gather):
                    tail = item.step(tail)
                else:
                    item.step(after)

    def ready(number):
        weights[number // 3][names[number % 3]] = gathered(gathers[number])

    last = depth_of
    g = gathers
    first = depth_of - 3
    move((g[0], first - 1), (g[1], first - 1))
    fence(g, ())
    move((g[0], first), (g[1], first))
    first_in, top = fence(g, (own_batch(latents), own_batch(cotangent)))
    move((g[0], last - 2), (g[1], last - 2), (g[2], first - 1), (g[3], first - 1))
    first_in, mods, top = fence(g, (to_stream(first_in), mods, top.T))
    move((g[0], last - 1), (g[1], last - 1), (g[2], first), (g[3], first))
    k0 = fence(g, open_stage(0, first_in))
    move((g[2], last - 2), (g[3], last - 2), (g[4], first - 1), (g[5], first - 1), (g[0], last), (g[1], last))
    fence(g, ())
    ready(0)
    ready(1)
    move((g[2], last - 1), (g[3], last - 1), (g[4], first), (g[5], first))
    k0 = fence(g, middle_stage(0, attention_stage(0, k0)))
    move((g[4], last - 2), (g[5], last - 2), (g[2], last), (g[3], last))
    k0, top = fence(g, (up_stage(0, k0), top))
    ready(2)
    ready(3)
    move((g[4], last - 1), (g[5], last - 1))
    first_out, k0 = down_stage(0, k0)
    k1 = open_stage(1, to_positions(first_out))
    k1 = attention_stage(1, k1)
    k0, k1, top = fence(g, (k0, k1, top))
    move((g[4], last), (g[5], last))
    grad_top = send_positions(top)
    k1 = middle_stage(1, k1)
    k0, k1 = fence(g, (k0, k1))
    ready(4)
    ready(5)
    k1 = up_stage(1, k1)
    k1, s5 = fc2_grads(1, k1, stream_rel(grad_top))
    k0, k1 = fence([s5], (k0, k1))
    move((s5, 1))
    second_out, k1 = down_stage(1, k1)
    second_out, k1 = lax.optimization_barrier((stream_plain(second_out.astype(bf16)), k1))
    output = send_frames(second_out)
    k1, s4 = up_back(1, k1)
    k0, k1, output = fence([s4, s5], (k0, k1, output))
    move((s4, 1))
    k1 = hidden2_back(1, k1)
    k0, k1 = fence([s4, s5], (k0, k1))
    move((s5, 2), (s4, 2))
    k1 = attention_back(1, k1)
    k1, s3 = mixed_grads(1, k1)
    k0, k1, output = fence(s3 + [s4, s5], (k0, k1, output.T))
    move((s5, 3), (s4, 3), *[(s, 1) for s in s3])
    grad_mid, small_time = stream_back(1, k1)
    grad_mid = stream_plain(grad_mid.astype(bf16))
    k0, grad_mid, small_time, output = fence(s3 + [s4, s5], (k0, grad_mid, small_time, output))
    k0, s2 = fc2_grads(0, k0, stream_rel(send_frames(grad_mid)))
    k0, s1 = up_back(0, k0)
    move((s5, 4), (s4, 4), *[(s, 2) for s in s3], after=k0["pre"])
    k0, small_time, output = fence([s1, s2] + s3 + [s4, s5], (k0, small_time, output))
    move((s2, 1), (s5, last), (s4, last), *[(s, 3) for s in s3])
    k0 = attention_back(0, hidden2_back(0, k0))
    move((s1, 1))
    k0, small_time, output = fence([s1, s2] + s3 + [s4, s5], (k0, small_time, output))
    move((s2, 2), (s1, 2), *[(s, 4) for s in s3])
    k0, s0 = mixed_grads(0, k0)
    grad_first, small_space = stream_back(0, k0)
    grad_first, small, output = fence(s0 + [s1, s2] + s3, (grad_first, (small_space, small_time), output))
    move((s2, 3), (s1, 3), *[(s, last) for s in s3], *[(s, 1) for s in s0])
    small, _ = lax.optimization_barrier((small, s0[0].arrays[1]))
    packed, counts = pack_small(small[0], small[1])
    grad_first, packed, output = fence(s0 + [s1, s2] + s3, (grad_first, packed, output))
    move((s2, 4), (s1, 4), *[(s, 2) for s in s0])
    output = to_argument(output)
    output, grad_first = fence(s0 + [s1, s2], (output, grad_first))
    move((s2, last), (s1, last), *[(s, 3) for s in s0])
    fence(s0 + [s1, s2], ())
    for item in s0 + [s1, s2] + s3 + [s4, s5]:
        move((item, last))
    weights_space = [jnp.concatenate([s.result() for s in s0], 1), s1.result(), s2.result()]
    weights_time = [jnp.concatenate([s.result() for s in s3], 1), s4.result(), s5.result()]
    grad_first = grad_first.astype(bf16)
    grad_first = dot_nt(exchange, grad_first).astype(bf16) if relative else grad_first.T
    grad_latents = to_argument(grad_first).astype(f32)

    mod_part = packed[:, : counts[1]]
    bias_part = jnp.sum(packed[:, counts[1] :], 0, keepdims=True)
    flat = jnp.concatenate([mod_part.reshape(1, -1), bias_part], 1)
    flat = all_sum(flat, "row")[0]
    mod_grad_low = flat[: batches * counts[1]].reshape(batches, lat_count, 2, 6, width).astype(bf16)
    bias_part = flat[batches * counts[1] :]
    bias_out = [bias_part[a - counts[1] : b - counts[1]] for a, b in zip(counts[1:-1], counts[2:])]
    grad_bias_qv = jnp.stack(
        [jnp.stack([bias_out[0], bias_out[2]]), jnp.stack([bias_out[1], bias_out[3]])]
    )
    grad_bias_out = jnp.stack(bias_out[4:6])
    grad_bias_fc1 = jnp.stack(bias_out[6:8])
    grad_bias_fc2 = jnp.stack(bias_out[8:10])
    grad_bias_ada = jnp.sum(mod_grad_low.astype(f32), (0, 1))
    grad_weight_ada = jnp.einsum("mlr,mlbjk->brjk", cond_low, mod_grad_low, preferred_element_type=f32)
    cond_partial = jnp.einsum("mlbjk,brjk->mlr", mod_grad_low, w_ada, preferred_element_type=f32)
    cond_total = over_u(all_sum(cond_partial, "m"))
    sigmoid_cond = jax.nn.sigmoid(cond_float)
    grad_condition = cond_total * sigmoid_cond * (1.0 + cond_float * (1.0 - sigmoid_cond))
    grad_weight_qkv, grad_weight_out, grad_weight_fc1, grad_weight_fc2 = [], [], [], []
    for mixed, first, second in (weights_space, weights_time):
        grad_weight_qkv.append(mixed[:, : 3 * width].reshape(depth, 3, width))
        grad_weight_out.append(mixed[:, 3 * width :])
        grad_weight_fc1.append(first)
        grad_weight_fc2.append(second)
    return (
        output,
        grad_latents,
        grad_condition,
        grad_weight_ada,
        grad_bias_ada,
        jnp.stack(grad_weight_qkv),
        grad_bias_qv,
        jnp.stack(grad_weight_out),
        grad_bias_out,
        jnp.stack(grad_weight_fc1),
        grad_bias_fc1,
        jnp.stack(grad_weight_fc2),
        grad_bias_fc2,
    )


def solution(mesh):
    rows, columns = mesh.devices.shape

    def placed(latents, *rest):
        parts = latents.shape[0]
        inner = Mesh(mesh.devices.reshape(rows, columns // parts, parts), ("row", "u", "m"))
        col = ("u", "m")
        in_specs = (
            P(None, col, "row"),
            P(None, None, "row"),
            P(None, "row", None, col),
            P(None, None, col),
            P(None, "row", None, col),
            P(None, None, col),
            P(None, "row", col),
            P(None, col),
            P(None, "row", col),
            P(None, col),
            P(None, "row", col),
            P(None, col),
            P(None, col, "row"),
        )
        out_specs = (P(None, col, "row"),) + in_specs[:1] + in_specs[1:-1]
        return jax.shard_map(
            shards, mesh=inner, in_specs=in_specs, out_specs=out_specs, check_vma=False
        )(latents, *rest)

    return placed
```

```python
import functools

import jax
import jax.numpy as jnp
import numpy as np
from jax import lax
from jax.experimental import pallas as pl
from jax.experimental.pallas import tpu as pltpu
from jax.sharding import Mesh
from jax.sharding import PartitionSpec as P

D = 1152
HD = 72
P_SIZE = 256
NF = 16
SCALE = HD ** (-0.5)
EPSILON = 1e-06


KINDS = ({"mixed": 0, "fc1": 1, "fc2": 0}, {"mixed": 1, "fc1": 0, "fc2": 1})

f32 = jnp.float32
bf16 = jnp.bfloat16


def bits_of(count):
    found = []
    bit = count // 2
    while bit:
        found.append(bit)
        bit //= 2
    return found


def swap(value, axis, bit):
    count = lax.axis_size(axis)
    return lax.ppermute(value, axis, [(i, i ^ bit) for i in range(count)])


def row_order(rows):
    order = [0]
    for bit in bits_of(rows):
        order = order + [j ^ bit for j in order]
    return order


def step_plan(rows, parts, kind):
    by_row = [("row", bit) for bit in bits_of(rows)]
    by_part = [("m", bit) for bit in bits_of(parts)]
    if kind == 0:
        return by_row + by_part
    return by_row[:-1] + by_part[:-1] + by_row[-1:] + by_part[-1:]


def moved(label, axis, bit):
    return (label[0] ^ bit, label[1]) if axis == "row" else (label[0], label[1] ^ bit)


def total(terms):
    result = terms[0].astype(f32)
    for term in terms[1:]:
        result = result + term.astype(f32)
    return result


def sum_rows(terms, names, first, count):
    width = terms[0][0].shape[2]
    rows = 576 if count % 576 == 0 else count // 2 if count % 32 == 0 else count
    assert first % rows == 0

    def body(*refs):
        value = refs[0][...].astype(f32)
        for ref in refs[1:-1]:
            value = value + ref[...].astype(f32)
        refs[-1][...] = value.astype(bf16)

    def spec(lead):
        return pl.BlockSpec((1, rows, width), lambda i, r: (lead + i, first // rows + r, 0))

    return pl.pallas_call(
        body,
        grid=(names, count // rows),
        in_specs=[spec(lead) for _, lead in terms],
        out_specs=pl.BlockSpec((1, rows, width), lambda i, r: (i, r, 0)),
        out_shape=jax.ShapeDtypeStruct((names, count, width), bf16),
        cost_estimate=pl.CostEstimate(
            flops=len(terms) * names * count * width,
            transcendentals=0,
            bytes_accessed=2 * (len(terms) + 1) * names * count * width,
        ),
        name="sum_rows",
    )(*[value for value, _ in terms])


class Gather:
    def __init__(self, shard, rows, parts, kind):
        self.rows, self.parts, self.depth = rows, parts, shard.shape[0]
        self.plan = step_plan(rows, parts, kind)
        self.labels = [[(0, 0)]]
        self.arrays = [shard]
        self.done = 0

    def step(self, after=None):
        axis, bit = self.plan[self.done]
        last_axis, last_bit = self.plan[-1]
        left = len(self.plan) - self.done

        def behind(value):
            return value if after is None else lax.optimization_barrier((value, after))[0]

        if left == 1:
            names, value = self.labels[1], self.arrays[1]
            result = swap(behind(value), axis, bit)
            self.labels.append([moved(name, axis, bit) for name in names])
            self.arrays.append(result)
        else:
            (names,), (value,) = self.labels, self.arrays
            result = after
            other = swap(value, axis, bit)
            other_names = [moved(name, axis, bit) for name in names]
            if left > 2:
                self.labels = [names + other_names]
                self.arrays = [jnp.concatenate([value, other], 0)]
            else:
                result = swap(behind(value), last_axis, last_bit)
                self.labels = [names, other_names, [moved(name, last_axis, last_bit) for name in names]]
                self.arrays = [value, other, result]
        self.done += 1
        return result

    def pieces(self):
        order, depth = row_order(self.rows), self.depth
        found = []
        for part in range(self.parts):
            entries = []
            for number, names in enumerate(self.labels):
                hits = [place for place, name in enumerate(names) if name[1] == part]
                if hits:
                    rank = order.index(names[hits[0]][0])
                    assert [names[h][0] for h in hits] == order[rank : rank + len(hits)]
                    assert hits == list(range(hits[0], hits[0] + len(hits)))
                    entries.append((number, hits[0] * depth, len(hits) * depth, rank * depth))
            found.append(entries)
        return found


class Scatter:
    def __init__(self, sent, kept, rows, parts, kind):
        self.plan = step_plan(rows, parts, kind)[::-1]
        self.order = row_order(rows)
        self.depth = kept.shape[1] // rows
        self.span = rows
        assert self.plan[0] == ("m", 1)
        self.arrays = [kept, sent]
        self.outgoing = 1
        self.gaining = [part for part in range(parts) if not part & 1]
        self.live = {part: [(0, place)] for place, part in enumerate(self.gaining)}
        self.done = 0

    def take(self, term, first, count):
        number, lead = term
        return self.arrays[number][lead, first : first + count]

    def sums(self, names, first, count):
        if self.depth % 16 == 0:
            leads = [[term[1] for term in terms] for terms in zip(*[self.live[n] for n in names])]
            numbers = [term[0] for term in self.live[names[0]]]
            assert all(list(l) == list(range(l[0], l[0] + len(l))) for l in leads)
            return sum_rows([(self.arrays[n], l[0]) for n, l in zip(numbers, leads)], len(names), first, count)
        return jnp.stack(
            [total([self.take(t, first, count) for t in self.live[n]]).astype(bf16) for n in names]
        )

    def step(self, after=None):
        axis, bit = self.plan[self.done]
        got = swap(self.arrays.pop(self.outgoing), axis, bit)
        if after is not None:
            got, _ = lax.optimization_barrier((got, after))
        self.arrays.append(got)
        for place, name in enumerate(self.gaining):
            self.live[name].append((len(self.arrays) - 1, place))
        self.done += 1
        self.prepare()

    def prepare(self):
        if self.done == len(self.plan):
            return
        axis, bit = self.plan[self.done]
        if axis == "m":
            names = [name for name in sorted(self.live) if name & bit]
            sent = self.sums(names, 0, self.span * self.depth)
            for name in names:
                self.live.pop(name)
            self.gaining = [name ^ bit for name in names]
        else:
            half = self.span // 2
            order = self.order
            assert all(order[half + p] == order[p] ^ bit for p in range(half))
            self.gaining = sorted(self.live)
            sent = self.sums(self.gaining, half * self.depth, half * self.depth)
            self.span = half
        self.outgoing = len(self.arrays)
        self.arrays.append(sent)

    def result(self):
        return total([self.take(t, 0, self.depth) for t in self.live[0]])


def fence(objects, values):
    arrays, values = lax.optimization_barrier(([o.arrays for o in objects], values))
    for o, fresh in zip(objects, arrays):
        o.arrays = list(fresh)
    return values


def all_sum(value, axis):
    for bit in bits_of(lax.axis_size(axis)):
        value = value + swap(value, axis, bit)
    return value


def over_u(value):
    return lax.psum(value, "u") if lax.axis_size("u") > 1 else value


def features_all(value):
    return lax.all_gather(value, "u", axis=1, tiled=True) if lax.axis_size("u") > 1 else value


def features_sum(value):
    if lax.axis_size("u") > 1:
        return lax.psum_scatter(value, "u", scatter_dimension=1, tiled=True)
    return value


def dot_nn(left, right):
    return lax.dot_general(left, right, (((1,), (0,)), ((), ())), preferred_element_type=f32)


def dot_nt(left, right):
    return lax.dot_general(left, right, (((1,), (1,)), ((), ())), preferred_element_type=f32)


def dot_tn(left, right):
    return lax.dot_general(left, right, (((0,), (0,)), ((), ())), preferred_element_type=f32)


LIMIT = 56 * 1024 * 1024


class Weight:
    def __init__(self, arrays, pieces):
        self.arrays = [value.reshape(-1, value.shape[-1]) for value in arrays]
        self.places = pieces
        self.parts = len(pieces)
        self.height = sum(rows for _, _, rows, _ in pieces[0])
        self.width = self.arrays[0].shape[1]

    def scratch(self):
        pieces = len(self.places[0])
        return [
            pltpu.VMEM((self.parts, self.height, self.width), bf16),
            pltpu.SemaphoreType.DMA((self.parts, pieces)),
        ]

    def copies(self, part, refs, held, sems):
        return [
            pltpu.make_async_copy(
                refs[number].at[pl.ds(start, rows)], held.at[part, pl.ds(to, rows)], sems.at[part, place]
            )
            for place, (number, start, rows, to) in enumerate(self.places[part])
        ]

    def arrive(self, step, refs, held, sems):
        @pl.when(step == 0)
        def _():
            for part in range(self.parts):
                for copy in self.copies(part, refs, held, sems):
                    copy.start()

        for part in range(self.parts):

            @pl.when(step == part)
            def _(part=part):
                for copy in self.copies(part, refs, held, sems):
                    copy.wait()


def cut_last(load, low, high):
    base = low // 128 * 128
    value = load(base, high)
    return value if base == low else value[:, low - base :]


def whole_spec(shape):
    return pl.BlockSpec(shape, lambda s: (0,) * len(shape))


def part_spec(shape):
    return pl.BlockSpec((1,) + shape, lambda s: (s,) + (0,) * len(shape))


def project(x, weight, columns, extras, epilogue, out_types, name):
    tokens, depth = x.shape
    low, high = columns
    n = high - low
    count = len(weight.arrays)

    def body(*refs):
        x_ref, refs = refs[0], refs[1:]
        w_refs, refs = refs[:count], refs[count:]
        extra_refs, refs = refs[: len(extras)], refs[len(extras) :]
        outs, (held, sems) = refs[: len(out_types)], refs[len(out_types) :]
        step = pl.program_id(0)
        weight.arrive(step, w_refs, held, sems)
        left = x_ref[...]
        right = cut_last(lambda a, b: held[step, :, a:b], low, high)
        made = epilogue(dot_nn(left, right), *[e[0] for e in extra_refs])
        for out, piece in zip(outs, made):
            out[0] = piece.astype(out.dtype)

    return pl.pallas_call(
        body,
        grid=(weight.parts,),
        in_specs=[whole_spec((tokens, depth))]
        + [pl.BlockSpec(memory_space=pl.ANY)] * count
        + [part_spec(e.shape[1:]) for e in extras],
        out_specs=[part_spec((tokens, n))] * len(out_types),
        out_shape=[jax.ShapeDtypeStruct((weight.parts, tokens, n), t) for t in out_types],
        scratch_shapes=weight.scratch(),
        compiler_params=pltpu.CompilerParams(vmem_limit_bytes=LIMIT),
        cost_estimate=pl.CostEstimate(
            flops=2 * tokens * depth * n * weight.parts,
            transcendentals=0,
            bytes_accessed=2 * weight.parts * n * (depth + 2 * tokens),
        ),
        name=name,
    )(x, *weight.arrays, *extras)


def contract(xs, weight, columns, name, large=(), small=(), outs=None, finish=None):
    parts, tokens, n = xs.shape
    low, high = columns
    count = len(weight.arrays)
    height = weight.height
    if finish is None:
        outs = [jax.ShapeDtypeStruct((tokens, height), f32)]

    def body(*refs):
        x_ref, refs = refs[0], refs[1:]
        w_refs, refs = refs[:count], refs[count:]
        large_refs, refs = refs[: len(large)], refs[len(large) :]
        small_refs, refs = refs[: len(small)], refs[len(small) :]
        out_refs, refs = refs[: len(outs)], refs[len(outs) :]
        held, sems = refs[:2]
        step = pl.program_id(0)
        acc = out_refs[0]
        if finish is not None:
            acc, local, large_sems = refs[2], refs[3:-1], refs[-1]
            copies = [
                pltpu.make_async_copy(ref, to, large_sems.at[place])
                for place, (ref, to) in enumerate(zip(large_refs, local))
            ]
        weight.arrive(step, w_refs, held, sems)
        if finish is not None:

            @pl.when(step == 0)
            def _():
                for copy in copies:
                    copy.start()

        right = cut_last(lambda a, b: held[step, :, a:b], low, high)
        value = dot_nt(x_ref[0], right)

        @pl.when(step == 0)
        def _():
            acc[...] = value

        @pl.when(step > 0)
        def _():
            acc[...] += value

        if finish is not None:

            @pl.when(step == parts - 1)
            def _():
                for copy in copies:
                    copy.wait()
                finish(acc, local, small_refs, out_refs)

    scratch = weight.scratch()
    if finish is not None:
        scratch.append(pltpu.VMEM((tokens, height), f32))
        scratch += [pltpu.VMEM(value.shape, value.dtype) for value in large]
        scratch.append(pltpu.SemaphoreType.DMA((max(len(large), 1),)))
    results = pl.pallas_call(
        body,
        grid=(parts,),
        in_specs=[part_spec((tokens, n))]
        + [pl.BlockSpec(memory_space=pl.ANY)] * (count + len(large))
        + [whole_spec(value.shape) for value in small],
        out_specs=[whole_spec(out.shape) for out in outs],
        out_shape=outs,
        scratch_shapes=scratch,
        compiler_params=pltpu.CompilerParams(vmem_limit_bytes=LIMIT),
        cost_estimate=pl.CostEstimate(
            flops=2 * tokens * height * n * parts,
            transcendentals=0,
            bytes_accessed=2 * parts * n * (height + tokens) + 4 * tokens * height * (1 + len(large)),
        ),
        name=name,
    )(xs, *weight.arrays, *large, *small)
    return results[0] if finish is None else results


ROWS = 32


def by_rows(tokens, work, sums=0, width=0):
    def turn(index, carried):
        made = work(pl.ds(pl.multiple_of(index * ROWS, ROWS), ROWS))
        return tuple(c + jnp.sum(m, 0, keepdims=True) for c, m in zip(carried, made or ()))

    return lax.fori_loop(0, tokens // ROWS, turn, (jnp.zeros((1, width), f32),) * sums)


def finish_middle(acc, large, small, outs):
    (stream,), (bias, gate, scale, shift) = large, small
    branch_out, middle_out, normed_out, inverse_out, hidden_out = outs

    def work(rows):
        branch = acc[rows, :] + bias[...]
        middle = stream[rows, :] + gate[...] * branch
        center = middle - jnp.sum(middle, 1, keepdims=True) / D
        inverse = lax.rsqrt(jnp.sum(center * center, 1, keepdims=True) / D + EPSILON)
        normed = center * inverse
        branch_out[rows, :] = branch
        middle_out[rows, :] = middle
        normed_out[rows, :] = normed
        inverse_out[rows, :] = inverse
        hidden_out[rows, :] = (normed * (1.0 + scale[...]) + shift[...]).astype(bf16)

    by_rows(acc.shape[0], work)


def finish_stream(acc, large, small, outs):
    (middle,), (bias, gate) = large, small
    branch_out, result_out = outs

    def work(rows):
        branch = acc[rows, :] + bias[...]
        branch_out[rows, :] = branch
        result_out[rows, :] = (middle[rows, :] + gate[...] * branch).astype(bf16)

    by_rows(acc.shape[0], work)


def norm_back(grad_hidden, scale, normed, inverse):
    grad_normed = grad_hidden * (1.0 + scale)
    first = jnp.sum(grad_normed, 1, keepdims=True) / D
    second = jnp.sum(grad_normed * normed, 1, keepdims=True) / D
    return inverse * (grad_normed - first - normed * second)


def finish_middle_back(acc, large, small, outs):
    (grad, normed, branch, inverse), (scale, gate) = large, small
    middle_out, low_out, sums_out = outs

    def work(rows):
        grad_hidden = acc[rows, :]
        middle = grad[rows, :] + norm_back(grad_hidden, scale[...], normed[rows, :], inverse[rows, :])
        middle_out[rows, :] = middle
        low_out[rows, :] = (gate[...] * middle).astype(bf16)
        return grad_hidden, grad_hidden * normed[rows, :], middle * branch[rows, :]

    made = by_rows(acc.shape[0], work, 3, acc.shape[1])
    sums_out[...] = jnp.concatenate(made, 0)


def finish_stream_back(acc, large, small, outs):
    (middle, normed, inverse), (scale,) = large, small
    stream_out, sums_out = outs

    def work(rows):
        grad_hidden = acc[rows, :]
        back = norm_back(grad_hidden, scale[...], normed[rows, :], inverse[rows, :])
        stream_out[rows, :] = (middle[rows, :] + back).astype(bf16)
        return grad_hidden, grad_hidden * normed[rows, :]

    made = by_rows(acc.shape[0], work, 2, acc.shape[1])
    sums_out[...] = jnp.concatenate(made, 0)


def weight_grads(pairs, cuts, name):
    tokens, depth = pairs[0][0].shape
    parts = pairs[0][1].shape[0]
    half = parts // 2
    widths = [g.shape[2] for _, g in pairs]
    full = sum(widths)
    count = len(pairs)

    def which(step):
        return jnp.where(step < half, 2 * step + 1, 2 * (step - half))

    def body(*refs):
        x_refs, refs = refs[:count], refs[count:]
        g_refs, refs = refs[:count], refs[count:]
        sent, refs = refs[: len(cuts)], refs[len(cuts) :]
        kept, refs = refs[: len(cuts)], refs[len(cuts) :]
        x_sums, refs = refs[:count], refs[count:]
        g_sums, turned = refs[:count], refs[count:]
        step = pl.program_id(0)

        @pl.when(step == 0)
        def _():
            for x_ref, x_sum, t_ref in zip(x_refs, x_sums, turned):
                value = x_ref[...].astype(f32)
                x_sum[...] = jnp.sum(value, 0, keepdims=True)
                t_ref[...] = value.T.astype(bf16)

        rights = [g_ref[0] for g_ref in g_refs]
        for right, g_sum in zip(rights, g_sums):
            g_sum[0] = jnp.sum(right.astype(f32), 0, keepdims=True)

        def fill(outs):
            made = [dot_nn(t_ref[...], r).astype(bf16) for t_ref, r in zip(turned, rights)]
            made = made[0] if count == 1 else jnp.concatenate(made, 1)
            for out, (low, high) in zip(outs, cuts):
                out[0] = made[:, low:high]

        @pl.when(step < half)
        def _():
            fill(sent)

        @pl.when(step >= half)
        def _():
            fill(kept)

    outs = pl.pallas_call(
        body,
        grid=(parts,),
        in_specs=[whole_spec((tokens, depth))] * count
        + [pl.BlockSpec((1, tokens, n), lambda s: (which(s), 0, 0)) for n in widths],
        out_specs=[
            pl.BlockSpec((1, depth, high - low), lambda s: (jnp.minimum(s, half - 1), 0, 0))
            for low, high in cuts
        ]
        + [
            pl.BlockSpec((1, depth, high - low), lambda s: (jnp.maximum(s - half, 0), 0, 0))
            for low, high in cuts
        ]
        + [whole_spec((1, depth))] * count
        + [pl.BlockSpec((1, 1, n), lambda s: (which(s), 0, 0)) for n in widths],
        out_shape=[jax.ShapeDtypeStruct((half, depth, high - low), bf16) for low, high in cuts] * 2
        + [jax.ShapeDtypeStruct((1, depth), f32)] * count
        + [jax.ShapeDtypeStruct((parts, 1, n), f32) for n in widths],
        scratch_shapes=[pltpu.VMEM((depth, tokens), bf16)] * count,
        compiler_params=pltpu.CompilerParams(vmem_limit_bytes=LIMIT),
        cost_estimate=pl.CostEstimate(
            flops=2 * tokens * depth * full * parts,
            transcendentals=0,
            bytes_accessed=2 * parts * full * (depth + tokens),
        ),
        name=name,
    )(*[x for x, _ in pairs], *[g for _, g in pairs])
    ranges = len(cuts)
    stacks = list(zip(outs[:ranges], outs[ranges : 2 * ranges]))
    outs = outs[2 * ranges :]
    return stacks, outs[:count], outs[count:]


def gelu_pair(value, bias):
    v = value + bias
    slope = 0.7978845608028654
    inner = jnp.tanh(slope * (v + 0.044715 * v * v * v))
    outer = 0.5 * (1.0 + inner)
    change = outer + 0.5 * v * (1.0 - inner * inner) * (slope * (1.0 + 3.0 * 0.044715 * v * v))
    return v * outer, change


POWER = SCALE * 1.4426950408889634


def allowed_pairs(temporal, span, tokens):
    if not temporal:
        return None
    first = lax.broadcasted_iota(jnp.int32, (tokens, tokens), 0)
    second = lax.broadcasted_iota(jnp.int32, (tokens, tokens), 1)
    return lax.rem(first, span) == lax.rem(second, span)


def head_columns(block, start, width):
    return [block[:, c * width + start : c * width + start + HD] for c in range(3)]


def forward_kernel(temporal, span, qkv, out, logs):
    width = qkv.shape[-1] // 3
    tokens = int(np.prod(qkv.shape[:-1]))
    allowed = allowed_pairs(temporal, span, tokens)
    block = qkv[...].reshape(tokens, 3 * width)
    done, kept = [], []
    for start in range(0, width, HD):
        query, key, value = head_columns(block, start, width)
        scores = dot_nt(key, query)
        if allowed is not None:
            scores = jnp.where(allowed, scores, -jnp.inf)
        largest = jnp.max(scores, 0, keepdims=True)
        powered = jnp.exp2((scores - largest) * POWER)
        summed = jnp.sum(powered, 0, keepdims=True)
        done.append(dot_tn(value, powered.astype(bf16)) / summed)
        kept.append(largest * POWER + jnp.log2(summed))
    out[...] = jnp.concatenate(done, 0).T.astype(bf16).reshape(out.shape)
    logs[...] = jnp.concatenate(kept, 0).reshape(logs.shape)


def backward_kernel(temporal, span, qkv, grad, attended, logs, out):
    width = qkv.shape[-1] // 3
    tokens = int(np.prod(qkv.shape[:-1]))
    allowed = allowed_pairs(temporal, span, tokens)
    block = qkv[...].reshape(tokens, 3 * width)
    outer = grad[...].reshape(tokens, width)
    turned = outer.astype(f32).T * attended[...].reshape(tokens, width).astype(f32).T
    log_rows = logs[...].reshape(width // HD, tokens)
    pieces = [[], [], []]
    for place, start in enumerate(range(0, width, HD)):
        query, key, value = head_columns(block, start, width)
        above = outer[:, start : start + HD]
        inner = jnp.sum(turned[start : start + HD], 0, keepdims=True)
        weights = jnp.exp2(dot_nt(key, query) * POWER - log_rows[place : place + 1])
        if allowed is not None:
            weights = jnp.where(allowed, weights, 0.0)
        grad_scores = (weights * (dot_nt(value, above) - inner)).astype(bf16)
        pieces[0].append(dot_tn(key, grad_scores) * SCALE)
        pieces[1].append((dot_nn(grad_scores, query) * SCALE).astype(bf16))
        pieces[2].append(dot_nn(weights.astype(bf16), above).astype(bf16))
    first = jnp.concatenate(pieces[0], 0).T.astype(bf16)
    out[...] = jnp.concatenate([first] + pieces[1] + pieces[2], 1).reshape(out.shape)


def attention_call(kernel, values, logs, layout, out_width, work, name):
    parts, tokens, triple = values[0].shape
    heads = triple // 3 // HD
    temporal = len(layout) == 3
    chunk = 16
    grid = (parts, layout[0])
    if temporal:
        assert layout[2] % chunk == 0
        grid = grid + (layout[2] // chunk,)
    groups = tokens // P_SIZE

    def spec(width):
        if temporal:
            return pl.BlockSpec((1, 1, layout[1], chunk, width), lambda p, g, c: (p, g, 0, c, 0))
        return pl.BlockSpec((1, 1, layout[1], width), lambda p, g: (p, g, 0, 0))

    if temporal:
        log_spec = pl.BlockSpec((1, 1, heads, P_SIZE), lambda p, g, c: (p, g * grid[2] + c, 0, 0))
    else:
        log_spec = pl.BlockSpec((1, 1, heads, P_SIZE), lambda p, g: (p, g, 0, 0))
    out_shape = [jax.ShapeDtypeStruct((parts,) + layout + (out_width,), bf16)]
    out_specs = [spec(out_width)]
    in_specs = [spec(v.shape[-1]) for v in values]
    given = [v.reshape((parts,) + layout + (v.shape[-1],)) for v in values]
    if logs is None:
        out_shape.append(jax.ShapeDtypeStruct((parts, groups, heads, P_SIZE), f32))
        out_specs.append(log_spec)
    else:
        in_specs.append(log_spec)
        given.append(logs)
    result = pl.pallas_call(
        functools.partial(kernel, temporal, chunk),
        grid=grid,
        in_specs=in_specs,
        out_specs=out_specs,
        out_shape=out_shape,
        cost_estimate=pl.CostEstimate(
            flops=tokens * parts * heads * P_SIZE * 128 * work,
            transcendentals=tokens * parts * heads * P_SIZE,
            bytes_accessed=tokens * parts * out_width * 8,
        ),
        name=name,
    )(*given)
    return [result[0].reshape(parts, tokens, out_width)] + list(result[1:])


def norm_forward(stream):
    center = stream - over_u(jnp.sum(stream, 1, keepdims=True)) / D
    inverse = lax.rsqrt(over_u(jnp.sum(center * center, 1, keepdims=True)) / D + EPSILON)
    return center * inverse, inverse


def norm_backward(grad_normed, normed, inverse):
    first, second = over_u(
        (
            jnp.sum(grad_normed, 1, keepdims=True),
            jnp.sum(grad_normed * normed, 1, keepdims=True),
        )
    )
    return inverse * (grad_normed - first / D - normed * (second / D))


def spread(vector, tokens):
    groups, width = vector.shape
    if groups == 1:
        return vector
    return jnp.broadcast_to(vector[:, None, :], (groups, tokens // groups, width)).reshape(tokens, width)


def group_sum(value, groups):
    return jnp.sum(value.reshape(groups, -1, value.shape[-1]), 1)


def shards(
    latents, cond, w_ada, b_ada, w_qkv, b_qv, w_out, b_out, w_fc1, b_fc1, w_fc2, b_fc2, cotangent
):
    batches, width, tokens = latents.shape
    lat_count = cond.shape[1]
    rows = lax.axis_size("row")
    parts = lax.axis_size("m")
    split = lax.axis_size("u")
    row = lax.axis_index("row")
    part_here = lax.axis_index("m")
    span = parts * width
    order = jnp.asarray(row_order(rows), jnp.int32)
    inverse_order = jnp.asarray(np.argsort(row_order(rows)), jnp.int32)
    part_ids = part_here ^ jnp.arange(parts)
    frames_dev = tokens // P_SIZE
    pos_block = tokens // (lat_count * NF)
    spatial = (frames_dev, P_SIZE)
    temporal = (lat_count, NF, pos_block)

    relative = split == 1
    depth = D // rows
    if relative:
        slot = jnp.arange(D)
        source = (row ^ order[slot // depth]) * depth + slot % depth
        exchange = (jnp.arange(D)[:, None] == source[None, :]).astype(bf16)

    def vector_rel(value):
        if not relative:
            return value
        shaped = value.reshape(value.shape[:-1] + (rows, depth))
        return jnp.take(shaped, row ^ order, axis=-2).reshape(value.shape)

    def vector_plain(value):
        if not relative:
            return value
        shaped = value.reshape(value.shape[:-1] + (rows, depth))
        return jnp.take(shaped, inverse_order[row ^ jnp.arange(rows)], axis=-2).reshape(value.shape)

    def stream_plain(value):
        return dot_nt(value, exchange).astype(bf16) if relative else value

    def stream_rel(value):
        return dot_nn(value, exchange) if relative else value.astype(f32)

    def send_positions(value):
        shaped = value.reshape(frames_dev, rows, pos_block, span).swapaxes(0, 1)
        return lax.all_to_all(shaped, "row", 0, 0).reshape(tokens, span)

    def send_frames(value):
        shaped = value.reshape(rows, frames_dev, pos_block, span)
        return lax.all_to_all(shaped, "row", 0, 0).swapaxes(0, 1).reshape(tokens, span)

    def gathered(gather):
        pieces = gather.pieces()
        arrays = [value.reshape(-1, value.shape[-1]) for value in gather.arrays]
        if relative:
            return Weight(arrays, pieces)
        places = inverse_order[row ^ jnp.arange(rows)]
        blocks = []
        for entries in pieces:
            entries = sorted(entries, key=lambda entry: entry[3])
            block = jnp.concatenate([arrays[n][a : a + count] for n, a, count, _ in entries], 0)
            blocks.append(jnp.take(block.reshape(rows, depth, -1), places, axis=0).reshape(block.shape))
        return Weight(blocks, [[(part, 0, D, 0)] for part in range(parts)])

    def scatter(stacks, kind):
        if not relative:
            stacks = [
                jnp.take(s.reshape(s.shape[0], rows, depth, -1), row ^ order, axis=1).reshape(s.shape)
                for s in stacks
            ]
        return Scatter(stacks[0], stacks[1], rows, parts, kind)

    def own_share(value):
        return value if relative else lax.dynamic_slice_in_dim(value, lax.axis_index("u") * span, span, 1)

    cond_float = cond.astype(f32)
    cond_low = jax.nn.silu(cond_float).astype(bf16)
    mod_partial = jnp.einsum("mlr,brjk->mlbjk", cond_low, w_ada, preferred_element_type=f32)
    mod_partial = mod_partial + jnp.where(row == 0, b_ada.astype(f32), 0.0)[None, None]
    small = jnp.concatenate(
        [b.astype(f32).reshape(-1) for b in (b_qv, b_out, b_fc1, b_fc2)]
    )
    packed = jnp.concatenate(
        [mod_partial.reshape(batches, -1), jnp.broadcast_to(small, (parts,) + small.shape)], 1
    )
    packed = lax.all_to_all(packed, "m", split_axis=0, concat_axis=0, tiled=True)
    mod_size = lat_count * 12 * width
    mod_here = all_sum(packed[:, :mod_size], "row").reshape(parts, lat_count, 2, 6, width)
    mod_here = vector_rel(jnp.moveaxis(mod_here, 0, -2).reshape(lat_count, 2, 6, span))
    small = packed[:, mod_size:]
    sizes = np.cumsum([0, 4 * width, 2 * width, 2 * b_fc1.shape[1], 2 * width])
    all_qv, all_out, all_fc1, all_fc2 = [small[:, a:b] for a, b in zip(sizes[:-1], sizes[1:])]
    all_qv = jnp.take(all_qv.reshape(parts, 2, 2, width), part_ids, axis=0)
    all_fc1 = jnp.take(all_fc1.reshape(parts, 2, -1), part_ids, axis=0)
    all_out = vector_rel(jnp.moveaxis(all_out.reshape(parts, 2, width), 0, 1).reshape(2, span))
    all_fc2 = vector_rel(jnp.moveaxis(all_fc2.reshape(parts, 2, width), 0, 1).reshape(2, span))

    zeros = jnp.zeros((parts, width), f32)
    bias_qkv = [
        jnp.concatenate([all_qv[:, b, 0], zeros, all_qv[:, b, 1]], 1)[:, None, :] for b in range(2)
    ]
    bias_fc1 = [all_fc1[:, b][:, None, :] for b in range(2)]
    hidden_width = w_fc1.shape[2]
    mixed_cols, out_cols, hidden_cols = (0, 3 * width), (3 * width, 4 * width), (0, hidden_width)
    middle_cut = 4 * width // 256 * 128 + 128
    mixed_cuts = [(0, middle_cut), (middle_cut, 4 * width)]
    layouts = (spatial, temporal)
    groups_of = (1, lat_count)

    def shard_of(b, name):
        if name == "mixed":
            return jnp.concatenate([w_qkv[b].reshape(depth, 3 * width), w_out[b]], 1)
        return (w_fc1 if name == "fc1" else w_fc2)[b]

    def own_batch(value):
        return lax.all_to_all(value, "m", 0, 0).reshape(span, tokens)

    def to_stream(value):
        return dot_tn(value, exchange) if relative else value.T.astype(f32)

    def to_argument(value):
        return lax.all_to_all(value.reshape(parts, width, tokens), "m", 0, 0)

    lat_here = row * frames_dev // NF
    mod_space = lax.dynamic_slice_in_dim(mod_here[:, 0], lat_here, 1, 0)
    mods = [
        [spread(m[:, column], tokens) for column in range(6)] for m in (mod_space, mod_here[:, 1])
    ]

    def open_stage(b, stream):
        normed, inverse = norm_forward(stream)
        hidden = features_all((normed * (1.0 + mods[b][1]) + mods[b][0]).astype(bf16))
        return {"stream": stream, "normed": normed, "inverse": inverse, "hidden": hidden}

    def attention_stage(b, k):
        qkv = project(
            k["hidden"], weights[b]["mixed"], mixed_cols, [bias_qkv[b]], lambda v, c: (v + c,), [bf16], "qkv"
        )[0]
        attended, logs = attention_call(forward_kernel, [qkv], None, layouts[b], width, 4, "attend")
        return {**k, "qkv": qkv, "attended": attended, "logs": logs}

    fused = relative and lat_count == 1

    def shaped(*kinds):
        return [jax.ShapeDtypeStruct(shape, kind) for shape, kind in kinds]

    full = (tokens, span)

    def middle_stage(b, k):
        if fused:
            made = contract(
                k["attended"], weights[b]["mixed"], out_cols, "out",
                [k["stream"]], [all_out[b][None], mods[b][2], mods[b][4], mods[b][3]],
                shaped((full, f32), (full, f32), (full, f32), ((tokens, 1), f32), (full, bf16)),
                finish_middle,
            )
            return {**k, **dict(zip(("branch", "middle", "normed2", "inverse2", "hidden2"), made))}
        branch = features_sum(contract(k["attended"], weights[b]["mixed"], out_cols, "out")) + all_out[b]
        middle = k["stream"] + mods[b][2] * branch
        normed, inverse = norm_forward(middle)
        hidden = features_all((normed * (1.0 + mods[b][4]) + mods[b][3]).astype(bf16))
        return {**k, "branch": branch, "middle": middle, "normed2": normed, "inverse2": inverse, "hidden2": hidden}

    def up_stage(b, k):
        act, slope = project(
            k["hidden2"], weights[b]["fc1"], hidden_cols, [bias_fc1[b]], gelu_pair, [bf16, bf16], "up"
        )
        return {**k, "act": act, "slope": slope}

    def down_stage(b, k):
        if fused:
            branch, result = contract(
                k["act"], weights[b]["fc2"], hidden_cols, "down",
                [k["middle"]], [all_fc2[b][None], mods[b][5]],
                shaped((full, f32), (full, bf16)), finish_stream,
            )
            return result, {**k, "branch2": branch}
        branch = features_sum(contract(k["act"], weights[b]["fc2"], hidden_cols, "down")) + all_fc2[b]
        return k["middle"] + mods[b][5] * branch, {**k, "branch2": branch}

    def fc2_grads(b, k, grad):
        low = features_all((mods[b][5] * grad).astype(bf16))
        stacks, (total_low,), _ = weight_grads([(low, k["act"])], [hidden_cols], "grad_fc2")
        return {**k, "grad": grad, "low2": low, "sum_b2": own_share(total_low)}, scatter(stacks[0], KINDS[b]["fc2"])

    def up_back(b, k):
        grad_pre = project(
            k["low2"], weights[b]["fc2"], hidden_cols, [k["slope"]],
            lambda v, s: (v * s.astype(f32),), [bf16], "up_back",
        )[0]
        stacks, _, (total_pre,) = weight_grads([(k["hidden2"], grad_pre)], [hidden_cols], "grad_fc1")
        return {**k, "pre": grad_pre, "sum_b1": total_pre[:, 0]}, scatter(stacks[0], KINDS[b]["fc1"])

    def hidden2_back(b, k):
        if fused:
            middle, low, sums = contract(
                k["pre"], weights[b]["fc1"], hidden_cols, "hidden2_back",
                [k["grad"], k["normed2"], k["branch"], k["inverse2"]], [mods[b][4], mods[b][2]],
                shaped((full, f32), (full, bf16), ((3, span), f32)), finish_middle_back,
            )
            return {**k, "g_middle": middle, "low1": low, "sums2": sums}
        grad_hidden = features_sum(contract(k["pre"], weights[b]["fc1"], hidden_cols, "hidden2_back"))
        return {**k, "g_hidden2": grad_hidden}

    def attention_back(b, k):
        if fused:
            middle, low = k["g_middle"], k["low1"]
        else:
            grad_hidden = k["g_hidden2"]
            back = norm_backward(grad_hidden * (1.0 + mods[b][4]), k["normed2"], k["inverse2"])
            middle = k["grad"] + back
            low = features_all((mods[b][2] * middle).astype(bf16))
        grad_att = project(low, weights[b]["mixed"], out_cols, [], lambda v: (v,), [bf16], "out_back")[0]
        grad_qkv = attention_call(
            backward_kernel, [k["qkv"], grad_att, k["attended"]], k["logs"], layouts[b], 3 * width, 10, "attend_back"
        )[0]
        return {**k, "g_middle": middle, "low1": low, "g_qkv": grad_qkv}

    def mixed_grads(b, k):
        stacks, (_, total_low), (total_qkv, _) = weight_grads(
            [(k["hidden"], k["g_qkv"]), (k["low1"], k["attended"])], mixed_cuts, "grad_mixed"
        )
        return {**k, "sum_bo": own_share(total_low), "sum_qkv": total_qkv[:, 0]}, [
            scatter(pair, kind) for kind, pair in enumerate(stacks)
        ]

    def stream_back(b, k):
        biases = (
            k["sum_qkv"][:, :width], k["sum_qkv"][:, 2 * width :], k["sum_bo"], k["sum_b1"], k["sum_b2"],
        )
        if fused:
            stream, sums = contract(
                k["g_qkv"], weights[b]["mixed"], mixed_cols, "hidden_back",
                [k["g_middle"], k["normed"], k["inverse"]], [mods[b][1]],
                shaped((full, bf16), ((2, span), f32)), finish_stream_back,
            )
            return stream, ((sums, k["sums2"], k["grad"], k["branch2"]), biases)
        grad_hidden = features_sum(contract(k["g_qkv"], weights[b]["mixed"], mixed_cols, "hidden_back"))
        back = norm_backward(grad_hidden * (1.0 + mods[b][1]), k["normed"], k["inverse"])
        groups = groups_of[b]
        modulate_grad = jnp.stack(
            [
                group_sum(grad_hidden, groups),
                group_sum(grad_hidden * k["normed"], groups),
                group_sum(k["g_middle"] * k["branch"], groups),
                group_sum(k["g_hidden2"], groups),
                group_sum(k["g_hidden2"] * k["normed2"], groups),
                group_sum(k["grad"] * k["branch2"], groups),
            ],
            1,
        )
        return k["g_middle"] + back, (modulate_grad, biases)

    def modulate_sums(made):
        if not fused:
            return made
        sums, sums2, grad, branch = made
        last_sum = jnp.sum(grad * branch, 0, keepdims=True)
        return jnp.concatenate([sums, sums2[2:], sums2[:2], last_sum], 0)[None]

    def pack_small(small_space, small_time):
        mod_grad_space, biases_space = modulate_sums(small_space[0]), small_space[1]
        mod_grad_time, biases_time = modulate_sums(small_time[0]), small_time[1]
        onehot = (jnp.arange(lat_count) == lat_here).astype(f32)
        mod_grads = jnp.stack([onehot[:, None, None] * mod_grad_space, mod_grad_time], 1)
        row_sums = [pair[place] for place in (2, 4) for pair in (biases_space, biases_time)]
        streams = vector_plain(jnp.concatenate([mod_grads.reshape(-1, span)] + row_sums, 0))
        streams = jnp.moveaxis(streams.reshape(-1, parts, width), 1, 0)
        ordered = [pair[place] for place in (0, 1, 3) for pair in (biases_space, biases_time)]
        ordered = jnp.take(jnp.concatenate(ordered, 1), part_ids, axis=0)
        mods_count = lat_count * 12
        pieces = [
            streams[:, :mods_count].reshape(parts, -1),
            ordered[:, : 4 * width],
            streams[:, mods_count : mods_count + 2].reshape(parts, -1),
            ordered[:, 4 * width :],
            streams[:, mods_count + 2 :].reshape(parts, -1),
        ]
        packed = jnp.concatenate(pieces, 1)
        sizes = [mods_count * width] + [width] * 6 + [hidden_width] * 2 + [width] * 2
        packed = lax.all_to_all(packed, "m", split_axis=0, concat_axis=0, tiled=True)
        return packed, np.cumsum([0] + sizes)

    names = ("mixed", "fc1", "fc2")
    gathers = [Gather(shard_of(b, n), rows, parts, KINDS[b][n]) for b in range(2) for n in names]
    weights = [{}, {}]
    depth_of = len(gathers[0].plan)

    def move(*pairs, after=None):
        tail = None
        for item, until in pairs:
            while item.done < min(until, depth_of):
                if isinstance(item, Gather):
                    tail = item.step(tail)
                else:
                    item.step(after)

    def ready(number):
        weights[number // 3][names[number % 3]] = gathered(gathers[number])

    last = depth_of
    g = gathers
    first = depth_of - 3
    move((g[0], first - 1), (g[1], first - 1))
    fence(g, ())
    move((g[0], first), (g[1], first))
    first_in, top = fence(g, (own_batch(latents), own_batch(cotangent)))
    move((g[0], last - 2), (g[1], last - 2), (g[2], first - 1), (g[3], first - 1))
    first_in, mods, top = fence(g, (to_stream(first_in), mods, top.T))
    move((g[0], last - 1), (g[1], last - 1), (g[2], first), (g[3], first))
    k0 = fence(g, open_stage(0, first_in))
    move((g[2], last - 2), (g[3], last - 2), (g[4], first - 1), (g[5], first - 1), (g[0], last), (g[1], last))
    fence(g, ())
    ready(0)
    ready(1)
    move((g[2], last - 1), (g[3], last - 1), (g[4], first), (g[5], first))
    k0 = fence(g, middle_stage(0, attention_stage(0, k0)))
    move((g[2], last), (g[3], last), (g[4], last - 2), (g[5], last - 2))
    ready(2)
    first_out, k0 = down_stage(0, up_stage(0, k0))
    first_out = stream_plain(first_out.astype(bf16))
    k0, first_out, top = fence(g, (k0, first_out, top))
    ready(2)
    ready(3)
    move((g[4], last - 1), (g[5], last - 1))
    k1 = open_stage(1, stream_rel(send_positions(first_out)))
    k1 = attention_stage(1, k1)
    k0, k1, top = fence(g, (k0, k1, top))
    move((g[4], last), (g[5], last))
    grad_top = send_positions(top)
    k1 = middle_stage(1, k1)
    k0, k1, grad_top = fence(g, (k0, k1, grad_top))
    ready(4)
    ready(5)
    k1 = up_stage(1, k1)
    k1, s5 = fc2_grads(1, k1, stream_rel(grad_top))
    k0, k1 = fence([s5], (k0, k1))
    move((s5, 1))
    second_out, k1 = down_stage(1, k1)
    second_out, k1 = lax.optimization_barrier((stream_plain(second_out.astype(bf16)), k1))
    output = send_frames(second_out)
    k1, s4 = up_back(1, k1)
    k0, k1, output = fence([s4, s5], (k0, k1, output))
    move((s4, 1))
    k1 = hidden2_back(1, k1)
    k0, k1 = fence([s4, s5], (k0, k1))
    move((s5, 2), (s4, 2))
    k1 = attention_back(1, k1)
    k1, s3 = mixed_grads(1, k1)
    k0, k1, output = fence(s3 + [s4, s5], (k0, k1, output.T))
    move((s5, 3), (s4, 3))
    grad_mid, small_time = stream_back(1, k1)
    grad_mid = stream_plain(grad_mid.astype(bf16))
    k0, grad_mid, small_time, output = fence(s3 + [s4, s5], (k0, grad_mid, small_time, output))
    move(*[(s, 1) for s in s3])
    grad_low = send_frames(grad_mid)
    k0, grad_low, small_time, output = fence(s3 + [s4, s5], (k0, grad_low, small_time, output))
    k0, s2 = fc2_grads(0, k0, stream_rel(grad_low))
    move((s2, 1))
    k0, s1 = up_back(0, k0)
    move((s5, 4), (s4, 4), *[(s, 2) for s in s3], after=k0["pre"])
    k0, small_time, output = fence([s1, s2] + s3 + [s4, s5], (k0, small_time, output))
    move((s5, last), (s4, last), *[(s, 3) for s in s3])
    k0 = hidden2_back(0, k0)
    move((s1, 1))
    k0, small_time, output = fence([s1, s2] + s3 + [s4, s5], (k0, small_time, output))
    move((s2, 2), (s1, 2), *[(s, 4) for s in s3])
    k0 = attention_back(0, k0)
    k0, s0 = mixed_grads(0, k0)
    grad_first, small_space = stream_back(0, k0)
    grad_first, small, output = fence(s0 + [s1, s2] + s3, (grad_first, (small_space, small_time), output))
    move((s2, 3), (s1, 3), *[(s, last) for s in s3], *[(s, 1) for s in s0])
    small, _ = lax.optimization_barrier((small, s0[0].arrays[1]))
    packed, counts = pack_small(small[0], small[1])
    grad_first, packed, output = fence(s0 + [s1, s2] + s3, (grad_first, packed, output))
    move((s2, 4), (s1, 4), *[(s, 2) for s in s0])
    packed, _ = lax.optimization_barrier((packed, s0[0].arrays[-2]))
    output = to_argument(output)
    output, grad_first = fence(s0 + [s1, s2], (output, grad_first))
    move((s2, last), (s1, last), *[(s, 3) for s in s0])
    fence(s0 + [s1, s2], ())
    for item in s0 + [s1, s2] + s3 + [s4, s5]:
        move((item, last))
    weights_space = [jnp.concatenate([s.result() for s in s0], 1), s1.result(), s2.result()]
    weights_time = [jnp.concatenate([s.result() for s in s3], 1), s4.result(), s5.result()]
    grad_first = grad_first.astype(bf16)
    grad_first = dot_nt(exchange, grad_first).astype(bf16) if relative else grad_first.T
    grad_latents = to_argument(grad_first).astype(f32)

    mod_part = packed[:, : counts[1]]
    bias_part = jnp.sum(packed[:, counts[1] :], 0, keepdims=True)
    flat = jnp.concatenate([mod_part.reshape(1, -1), bias_part], 1)
    flat = all_sum(flat, "row")[0]
    mod_grad_low = flat[: batches * counts[1]].reshape(batches, lat_count, 2, 6, width).astype(bf16)
    bias_part = flat[batches * counts[1] :]
    bias_out = [bias_part[a - counts[1] : b - counts[1]] for a, b in zip(counts[1:-1], counts[2:])]
    grad_bias_qv = jnp.stack(
        [jnp.stack([bias_out[0], bias_out[2]]), jnp.stack([bias_out[1], bias_out[3]])]
    )
    grad_bias_out = jnp.stack(bias_out[4:6])
    grad_bias_fc1 = jnp.stack(bias_out[6:8])
    grad_bias_fc2 = jnp.stack(bias_out[8:10])
    grad_bias_ada = jnp.sum(mod_grad_low.astype(f32), (0, 1))
    grad_weight_ada = jnp.einsum("mlr,mlbjk->brjk", cond_low, mod_grad_low, preferred_element_type=f32)
    cond_partial = jnp.einsum("mlbjk,brjk->mlr", mod_grad_low, w_ada, preferred_element_type=f32)
    cond_total = over_u(all_sum(cond_partial, "m"))
    sigmoid_cond = jax.nn.sigmoid(cond_float)
    grad_condition = cond_total * sigmoid_cond * (1.0 + cond_float * (1.0 - sigmoid_cond))
    grad_weight_qkv, grad_weight_out, grad_weight_fc1, grad_weight_fc2 = [], [], [], []
    for mixed, first, second in (weights_space, weights_time):
        grad_weight_qkv.append(mixed[:, : 3 * width].reshape(depth, 3, width))
        grad_weight_out.append(mixed[:, 3 * width :])
        grad_weight_fc1.append(first)
        grad_weight_fc2.append(second)
    return (
        output,
        grad_latents,
        grad_condition,
        grad_weight_ada,
        grad_bias_ada,
        jnp.stack(grad_weight_qkv),
        grad_bias_qv,
        jnp.stack(grad_weight_out),
        grad_bias_out,
        jnp.stack(grad_weight_fc1),
        grad_bias_fc1,
        jnp.stack(grad_weight_fc2),
        grad_bias_fc2,
    )


def solution(mesh):
    rows, columns = mesh.devices.shape

    def placed(latents, *rest):
        parts = latents.shape[0]
        inner = Mesh(mesh.devices.reshape(rows, columns // parts, parts), ("row", "u", "m"))
        col = ("u", "m")
        in_specs = (
            P(None, col, "row"),
            P(None, None, "row"),
            P(None, "row", None, col),
            P(None, None, col),
            P(None, "row", None, col),
            P(None, None, col),
            P(None, "row", col),
            P(None, col),
            P(None, "row", col),
            P(None, col),
            P(None, "row", col),
            P(None, col),
            P(None, col, "row"),
        )
        out_specs = (P(None, col, "row"),) + in_specs[:1] + in_specs[1:-1]
        return jax.shard_map(
            shards, mesh=inner, in_specs=in_specs, out_specs=out_specs, check_vma=False
        )(latents, *rest)

    return placed
```

```python
import functools

import jax
import jax.numpy as jnp
import numpy as np
from jax import lax
from jax.experimental import pallas as pl
from jax.experimental.pallas import tpu as pltpu
from jax.sharding import Mesh
from jax.sharding import PartitionSpec as P

D = 1152
HD = 72
P_SIZE = 256
NF = 16
SCALE = HD ** (-0.5)
EPSILON = 1e-06


KINDS = ({"mixed": 0, "fc1": 1, "fc2": 0}, {"mixed": 1, "fc1": 0, "fc2": 1})

f32 = jnp.float32
bf16 = jnp.bfloat16


def bits_of(count):
    found = []
    bit = count // 2
    while bit:
        found.append(bit)
        bit //= 2
    return found


def swap(value, axis, bit):
    count = lax.axis_size(axis)
    return lax.ppermute(value, axis, [(i, i ^ bit) for i in range(count)])


def row_order(rows):
    order = [0]
    for bit in bits_of(rows):
        order = order + [j ^ bit for j in order]
    return order


def step_plan(rows, parts, kind):
    by_row = [("row", bit) for bit in bits_of(rows)]
    by_part = [("m", bit) for bit in bits_of(parts)]
    if kind == 0:
        return by_row + by_part
    return by_row[:-1] + by_part[:-1] + by_row[-1:] + by_part[-1:]


def moved(label, axis, bit):
    return (label[0] ^ bit, label[1]) if axis == "row" else (label[0], label[1] ^ bit)


def total(terms):
    result = terms[0].astype(f32)
    for term in terms[1:]:
        result = result + term.astype(f32)
    return result


def sum_rows(terms, names, first, count):
    width = terms[0][0].shape[2]
    rows = 576 if count % 576 == 0 else count // 2 if count % 32 == 0 else count
    assert first % rows == 0

    def body(*refs):
        value = refs[0][...].astype(f32)
        for ref in refs[1:-1]:
            value = value + ref[...].astype(f32)
        refs[-1][...] = value.astype(bf16)

    def spec(lead):
        return pl.BlockSpec((1, rows, width), lambda i, r: (lead + i, first // rows + r, 0))

    return pl.pallas_call(
        body,
        grid=(names, count // rows),
        in_specs=[spec(lead) for _, lead in terms],
        out_specs=pl.BlockSpec((1, rows, width), lambda i, r: (i, r, 0)),
        out_shape=jax.ShapeDtypeStruct((names, count, width), bf16),
        cost_estimate=pl.CostEstimate(
            flops=len(terms) * names * count * width,
            transcendentals=0,
            bytes_accessed=2 * (len(terms) + 1) * names * count * width,
        ),
        name="sum_rows",
    )(*[value for value, _ in terms])


class Gather:
    def __init__(self, shard, rows, parts, kind):
        self.rows, self.parts, self.depth = rows, parts, shard.shape[0]
        self.plan = step_plan(rows, parts, kind)
        self.labels = [[(0, 0)]]
        self.arrays = [shard]
        self.done = 0

    def step(self, after=None):
        axis, bit = self.plan[self.done]
        last_axis, last_bit = self.plan[-1]
        left = len(self.plan) - self.done

        def behind(value):
            return value if after is None else lax.optimization_barrier((value, after))[0]

        if left == 1:
            names, value = self.labels[1], self.arrays[1]
            result = swap(behind(value), axis, bit)
            self.labels.append([moved(name, axis, bit) for name in names])
            self.arrays.append(result)
        else:
            (names,), (value,) = self.labels, self.arrays
            result = after
            other = swap(value, axis, bit)
            other_names = [moved(name, axis, bit) for name in names]
            if left > 2:
                self.labels = [names + other_names]
                self.arrays = [jnp.concatenate([value, other], 0)]
            else:
                result = swap(behind(value), last_axis, last_bit)
                self.labels = [names, other_names, [moved(name, last_axis, last_bit) for name in names]]
                self.arrays = [value, other, result]
        self.done += 1
        return result

    def pieces(self):
        order, depth = row_order(self.rows), self.depth
        found = []
        for part in range(self.parts):
            entries = []
            for number, names in enumerate(self.labels):
                hits = [place for place, name in enumerate(names) if name[1] == part]
                if hits:
                    rank = order.index(names[hits[0]][0])
                    assert [names[h][0] for h in hits] == order[rank : rank + len(hits)]
                    assert hits == list(range(hits[0], hits[0] + len(hits)))
                    entries.append((number, hits[0] * depth, len(hits) * depth, rank * depth))
            found.append(entries)
        return found


class Scatter:
    def __init__(self, sent, kept, rows, parts, kind):
        self.plan = step_plan(rows, parts, kind)[::-1]
        self.order = row_order(rows)
        self.depth = kept.shape[1] // rows
        self.span = rows
        assert self.plan[0] == ("m", 1)
        self.arrays = [kept, sent]
        self.outgoing = 1
        self.gaining = [part for part in range(parts) if not part & 1]
        self.live = {part: [(0, place)] for place, part in enumerate(self.gaining)}
        self.done = 0

    def take(self, term, first, count):
        number, lead = term
        return self.arrays[number][lead, first : first + count]

    def sums(self, names, first, count):
        if self.depth % 16 == 0 and len(names) * count >= 4 * self.depth:
            leads = [[term[1] for term in terms] for terms in zip(*[self.live[n] for n in names])]
            numbers = [term[0] for term in self.live[names[0]]]
            assert all(list(l) == list(range(l[0], l[0] + len(l))) for l in leads)
            return sum_rows([(self.arrays[n], l[0]) for n, l in zip(numbers, leads)], len(names), first, count)
        return jnp.stack(
            [total([self.take(t, first, count) for t in self.live[n]]).astype(bf16) for n in names]
        )

    def step(self, after=None):
        axis, bit = self.plan[self.done]
        got = swap(self.arrays.pop(self.outgoing), axis, bit)
        if after is not None:
            got, _ = lax.optimization_barrier((got, after))
        self.arrays.append(got)
        for place, name in enumerate(self.gaining):
            self.live[name].append((len(self.arrays) - 1, place))
        self.done += 1
        self.prepare()

    def prepare(self):
        if self.done == len(self.plan):
            return
        axis, bit = self.plan[self.done]
        if axis == "m":
            names = [name for name in sorted(self.live) if name & bit]
            sent = self.sums(names, 0, self.span * self.depth)
            for name in names:
                self.live.pop(name)
            self.gaining = [name ^ bit for name in names]
        else:
            half = self.span // 2
            order = self.order
            assert all(order[half + p] == order[p] ^ bit for p in range(half))
            self.gaining = sorted(self.live)
            sent = self.sums(self.gaining, half * self.depth, half * self.depth)
            self.span = half
        self.outgoing = len(self.arrays)
        self.arrays.append(sent)

    def result(self):
        return total([self.take(t, 0, self.depth) for t in self.live[0]])


def fence(objects, values):
    arrays, values = lax.optimization_barrier(([o.arrays for o in objects], values))
    for o, fresh in zip(objects, arrays):
        o.arrays = list(fresh)
    return values


def all_sum(value, axis):
    for bit in bits_of(lax.axis_size(axis)):
        value = value + swap(value, axis, bit)
    return value


def over_u(value):
    return lax.psum(value, "u") if lax.axis_size("u") > 1 else value


def features_all(value):
    return lax.all_gather(value, "u", axis=1, tiled=True) if lax.axis_size("u") > 1 else value


def features_sum(value):
    if lax.axis_size("u") > 1:
        return lax.psum_scatter(value, "u", scatter_dimension=1, tiled=True)
    return value


def dot_nn(left, right):
    return lax.dot_general(left, right, (((1,), (0,)), ((), ())), preferred_element_type=f32)


def dot_nt(left, right):
    return lax.dot_general(left, right, (((1,), (1,)), ((), ())), preferred_element_type=f32)


def dot_tn(left, right):
    return lax.dot_general(left, right, (((0,), (0,)), ((), ())), preferred_element_type=f32)


LIMIT = 56 * 1024 * 1024


class Weight:
    def __init__(self, arrays, pieces):
        self.arrays = [value.reshape(-1, value.shape[-1]) for value in arrays]
        self.places = pieces
        self.parts = len(pieces)
        self.height = sum(rows for _, _, rows, _ in pieces[0])
        self.width = self.arrays[0].shape[1]

    def scratch(self):
        pieces = len(self.places[0])
        return [
            pltpu.VMEM((self.parts, self.height, self.width), bf16),
            pltpu.SemaphoreType.DMA((self.parts, pieces)),
        ]

    def copies(self, part, refs, held, sems):
        return [
            pltpu.make_async_copy(
                refs[number].at[pl.ds(start, rows)], held.at[part, pl.ds(to, rows)], sems.at[part, place]
            )
            for place, (number, start, rows, to) in enumerate(self.places[part])
        ]

    def arrive(self, step, refs, held, sems):
        @pl.when(step == 0)
        def _():
            for part in range(self.parts):
                for copy in self.copies(part, refs, held, sems):
                    copy.start()

        for part in range(self.parts):

            @pl.when(step == part)
            def _(part=part):
                for copy in self.copies(part, refs, held, sems):
                    copy.wait()


def cut_last(load, low, high):
    base = low // 128 * 128
    value = load(base, high)
    return value if base == low else value[:, low - base :]


def whole_spec(shape):
    return pl.BlockSpec(shape, lambda s: (0,) * len(shape))


def part_spec(shape):
    return pl.BlockSpec((1,) + shape, lambda s: (s,) + (0,) * len(shape))


def project(x, weight, columns, extras, epilogue, out_types, name):
    tokens, depth = x.shape
    low, high = columns
    n = high - low
    count = len(weight.arrays)

    def body(*refs):
        x_ref, refs = refs[0], refs[1:]
        w_refs, refs = refs[:count], refs[count:]
        extra_refs, refs = refs[: len(extras)], refs[len(extras) :]
        outs, (held, sems) = refs[: len(out_types)], refs[len(out_types) :]
        step = pl.program_id(0)
        weight.arrive(step, w_refs, held, sems)
        left = x_ref[...]
        right = cut_last(lambda a, b: held[step, :, a:b], low, high)
        made = epilogue(dot_nn(left, right), *[e[0] for e in extra_refs])
        for out, piece in zip(outs, made):
            out[0] = piece.astype(out.dtype)

    return pl.pallas_call(
        body,
        grid=(weight.parts,),
        in_specs=[whole_spec((tokens, depth))]
        + [pl.BlockSpec(memory_space=pl.ANY)] * count
        + [part_spec(e.shape[1:]) for e in extras],
        out_specs=[part_spec((tokens, n))] * len(out_types),
        out_shape=[jax.ShapeDtypeStruct((weight.parts, tokens, n), t) for t in out_types],
        scratch_shapes=weight.scratch(),
        compiler_params=pltpu.CompilerParams(vmem_limit_bytes=LIMIT),
        cost_estimate=pl.CostEstimate(
            flops=2 * tokens * depth * n * weight.parts,
            transcendentals=0,
            bytes_accessed=2 * weight.parts * n * (depth + 2 * tokens),
        ),
        name=name,
    )(x, *weight.arrays, *extras)


def contract(xs, weight, columns, name, large=(), small=(), outs=None, finish=None):
    parts, tokens, n = xs.shape
    low, high = columns
    count = len(weight.arrays)
    height = weight.height
    if finish is None:
        outs = [jax.ShapeDtypeStruct((tokens, height), f32)]

    def body(*refs):
        x_ref, refs = refs[0], refs[1:]
        w_refs, refs = refs[:count], refs[count:]
        large_refs, refs = refs[: len(large)], refs[len(large) :]
        small_refs, refs = refs[: len(small)], refs[len(small) :]
        out_refs, refs = refs[: len(outs)], refs[len(outs) :]
        held, sems = refs[:2]
        step = pl.program_id(0)
        acc = out_refs[0]
        if finish is not None:
            acc, local, large_sems = refs[2], refs[3:-1], refs[-1]
            copies = [
                pltpu.make_async_copy(ref, to, large_sems.at[place])
                for place, (ref, to) in enumerate(zip(large_refs, local))
            ]
        weight.arrive(step, w_refs, held, sems)
        if finish is not None:

            @pl.when(step == 0)
            def _():
                for copy in copies:
                    copy.start()

        right = cut_last(lambda a, b: held[step, :, a:b], low, high)
        value = dot_nt(x_ref[0], right)

        @pl.when(step == 0)
        def _():
            acc[...] = value

        @pl.when(step > 0)
        def _():
            acc[...] += value

        if finish is not None:

            @pl.when(step == parts - 1)
            def _():
                for copy in copies:
                    copy.wait()
                finish(acc, local, small_refs, out_refs)

    scratch = weight.scratch()
    if finish is not None:
        scratch.append(pltpu.VMEM((tokens, height), f32))
        scratch += [pltpu.VMEM(value.shape, value.dtype) for value in large]
        scratch.append(pltpu.SemaphoreType.DMA((max(len(large), 1),)))
    results = pl.pallas_call(
        body,
        grid=(parts,),
        in_specs=[part_spec((tokens, n))]
        + [pl.BlockSpec(memory_space=pl.ANY)] * (count + len(large))
        + [whole_spec(value.shape) for value in small],
        out_specs=[whole_spec(out.shape) for out in outs],
        out_shape=outs,
        scratch_shapes=scratch,
        compiler_params=pltpu.CompilerParams(vmem_limit_bytes=LIMIT),
        cost_estimate=pl.CostEstimate(
            flops=2 * tokens * height * n * parts,
            transcendentals=0,
            bytes_accessed=2 * parts * n * (height + tokens) + 4 * tokens * height * (1 + len(large)),
        ),
        name=name,
    )(xs, *weight.arrays, *large, *small)
    return results[0] if finish is None else results


ROWS = 32


def by_rows(tokens, work, sums=0, width=0):
    def turn(index, carried):
        made = work(pl.ds(pl.multiple_of(index * ROWS, ROWS), ROWS))
        return tuple(c + jnp.sum(m, 0, keepdims=True) for c, m in zip(carried, made or ()))

    return lax.fori_loop(0, tokens // ROWS, turn, (jnp.zeros((1, width), f32),) * sums)


def finish_middle(acc, large, small, outs):
    (stream,), (bias, gate, scale, shift) = large, small
    branch_out, middle_out, normed_out, inverse_out, hidden_out = outs

    def work(rows):
        branch = acc[rows, :] + bias[...]
        middle = stream[rows, :] + gate[...] * branch
        center = middle - jnp.sum(middle, 1, keepdims=True) / D
        inverse = lax.rsqrt(jnp.sum(center * center, 1, keepdims=True) / D + EPSILON)
        normed = center * inverse
        branch_out[rows, :] = branch
        middle_out[rows, :] = middle
        normed_out[rows, :] = normed
        inverse_out[rows, :] = inverse
        hidden_out[rows, :] = (normed * (1.0 + scale[...]) + shift[...]).astype(bf16)

    by_rows(acc.shape[0], work)


def finish_stream(acc, large, small, outs):
    (middle,), (bias, gate) = large, small
    branch_out, result_out = outs

    def work(rows):
        branch = acc[rows, :] + bias[...]
        branch_out[rows, :] = branch
        result_out[rows, :] = (middle[rows, :] + gate[...] * branch).astype(bf16)

    by_rows(acc.shape[0], work)


def norm_back(grad_hidden, scale, normed, inverse):
    grad_normed = grad_hidden * (1.0 + scale)
    first = jnp.sum(grad_normed, 1, keepdims=True) / D
    second = jnp.sum(grad_normed * normed, 1, keepdims=True) / D
    return inverse * (grad_normed - first - normed * second)


def finish_middle_back(acc, large, small, outs):
    (grad, normed, branch, inverse), (scale, gate) = large, small
    middle_out, low_out, sums_out = outs

    def work(rows):
        grad_hidden = acc[rows, :]
        middle = grad[rows, :] + norm_back(grad_hidden, scale[...], normed[rows, :], inverse[rows, :])
        middle_out[rows, :] = middle
        low_out[rows, :] = (gate[...] * middle).astype(bf16)
        return grad_hidden, grad_hidden * normed[rows, :], middle * branch[rows, :]

    made = by_rows(acc.shape[0], work, 3, acc.shape[1])
    sums_out[...] = jnp.concatenate(made, 0)


def finish_stream_back(acc, large, small, outs):
    (middle, normed, inverse), (scale,) = large, small
    stream_out, sums_out = outs

    def work(rows):
        grad_hidden = acc[rows, :]
        back = norm_back(grad_hidden, scale[...], normed[rows, :], inverse[rows, :])
        stream_out[rows, :] = (middle[rows, :] + back).astype(bf16)
        return grad_hidden, grad_hidden * normed[rows, :]

    made = by_rows(acc.shape[0], work, 2, acc.shape[1])
    sums_out[...] = jnp.concatenate(made, 0)


def weight_grads(pairs, cuts, name):
    tokens, depth = pairs[0][0].shape
    parts = pairs[0][1].shape[0]
    half = parts // 2
    widths = [g.shape[2] for _, g in pairs]
    full = sum(widths)
    count = len(pairs)

    def which(step):
        return jnp.where(step < half, 2 * step + 1, 2 * (step - half))

    def body(*refs):
        x_refs, refs = refs[:count], refs[count:]
        g_refs, refs = refs[:count], refs[count:]
        sent, refs = refs[: len(cuts)], refs[len(cuts) :]
        kept, refs = refs[: len(cuts)], refs[len(cuts) :]
        x_sums, refs = refs[:count], refs[count:]
        g_sums, turned = refs[:count], refs[count:]
        step = pl.program_id(0)

        @pl.when(step == 0)
        def _():
            for x_ref, x_sum, t_ref in zip(x_refs, x_sums, turned):
                value = x_ref[...].astype(f32)
                x_sum[...] = jnp.sum(value, 0, keepdims=True)
                t_ref[...] = value.T.astype(bf16)

        rights = [g_ref[0] for g_ref in g_refs]
        for right, g_sum in zip(rights, g_sums):
            g_sum[0] = jnp.sum(right.astype(f32), 0, keepdims=True)

        def fill(outs):
            made = [dot_nn(t_ref[...], r).astype(bf16) for t_ref, r in zip(turned, rights)]
            made = made[0] if count == 1 else jnp.concatenate(made, 1)
            for out, (low, high) in zip(outs, cuts):
                out[0] = made[:, low:high]

        @pl.when(step < half)
        def _():
            fill(sent)

        @pl.when(step >= half)
        def _():
            fill(kept)

    outs = pl.pallas_call(
        body,
        grid=(parts,),
        in_specs=[whole_spec((tokens, depth))] * count
        + [pl.BlockSpec((1, tokens, n), lambda s: (which(s), 0, 0)) for n in widths],
        out_specs=[
            pl.BlockSpec((1, depth, high - low), lambda s: (jnp.minimum(s, half - 1), 0, 0))
            for low, high in cuts
        ]
        + [
            pl.BlockSpec((1, depth, high - low), lambda s: (jnp.maximum(s - half, 0), 0, 0))
            for low, high in cuts
        ]
        + [whole_spec((1, depth))] * count
        + [pl.BlockSpec((1, 1, n), lambda s: (which(s), 0, 0)) for n in widths],
        out_shape=[jax.ShapeDtypeStruct((half, depth, high - low), bf16) for low, high in cuts] * 2
        + [jax.ShapeDtypeStruct((1, depth), f32)] * count
        + [jax.ShapeDtypeStruct((parts, 1, n), f32) for n in widths],
        scratch_shapes=[pltpu.VMEM((depth, tokens), bf16)] * count,
        compiler_params=pltpu.CompilerParams(vmem_limit_bytes=LIMIT),
        cost_estimate=pl.CostEstimate(
            flops=2 * tokens * depth * full * parts,
            transcendentals=0,
            bytes_accessed=2 * parts * full * (depth + tokens),
        ),
        name=name,
    )(*[x for x, _ in pairs], *[g for _, g in pairs])
    ranges = len(cuts)
    stacks = list(zip(outs[:ranges], outs[ranges : 2 * ranges]))
    outs = outs[2 * ranges :]
    return stacks, outs[:count], outs[count:]


def gelu_pair(value, bias):
    v = value + bias
    slope = 0.7978845608028654
    inner = jnp.tanh(slope * (v + 0.044715 * v * v * v))
    outer = 0.5 * (1.0 + inner)
    change = outer + 0.5 * v * (1.0 - inner * inner) * (slope * (1.0 + 3.0 * 0.044715 * v * v))
    return v * outer, change


POWER = SCALE * 1.4426950408889634


def allowed_pairs(temporal, span, tokens):
    if not temporal:
        return None
    first = lax.broadcasted_iota(jnp.int32, (tokens, tokens), 0)
    second = lax.broadcasted_iota(jnp.int32, (tokens, tokens), 1)
    return lax.rem(first, span) == lax.rem(second, span)


def head_columns(block, start, width):
    return [block[:, c * width + start : c * width + start + HD] for c in range(3)]


def forward_kernel(temporal, span, qkv, out, logs):
    width = qkv.shape[-1] // 3
    tokens = int(np.prod(qkv.shape[:-1]))
    allowed = allowed_pairs(temporal, span, tokens)
    block = qkv[...].reshape(tokens, 3 * width)
    done, kept = [], []
    for start in range(0, width, HD):
        query, key, value = head_columns(block, start, width)
        scores = dot_nt(key, query)
        if allowed is not None:
            scores = jnp.where(allowed, scores, -jnp.inf)
        largest = jnp.max(scores, 0, keepdims=True)
        powered = jnp.exp2((scores - largest) * POWER)
        summed = jnp.sum(powered, 0, keepdims=True)
        done.append(dot_tn(value, powered.astype(bf16)) / summed)
        kept.append(largest * POWER + jnp.log2(summed))
    out[...] = jnp.concatenate(done, 0).T.astype(bf16).reshape(out.shape)
    logs[...] = jnp.concatenate(kept, 0).reshape(logs.shape)


def backward_kernel(temporal, span, qkv, grad, attended, logs, out):
    width = qkv.shape[-1] // 3
    tokens = int(np.prod(qkv.shape[:-1]))
    allowed = allowed_pairs(temporal, span, tokens)
    block = qkv[...].reshape(tokens, 3 * width)
    outer = grad[...].reshape(tokens, width)
    turned = outer.astype(f32).T * attended[...].reshape(tokens, width).astype(f32).T
    log_rows = logs[...].reshape(width // HD, tokens)
    pieces = [[], [], []]
    for place, start in enumerate(range(0, width, HD)):
        query, key, value = head_columns(block, start, width)
        above = outer[:, start : start + HD]
        inner = jnp.sum(turned[start : start + HD], 0, keepdims=True)
        weights = jnp.exp2(dot_nt(key, query) * POWER - log_rows[place : place + 1])
        if allowed is not None:
            weights = jnp.where(allowed, weights, 0.0)
        grad_scores = (weights * (dot_nt(value, above) - inner)).astype(bf16)
        pieces[0].append(dot_tn(key, grad_scores) * SCALE)
        pieces[1].append((dot_nn(grad_scores, query) * SCALE).astype(bf16))
        pieces[2].append(dot_nn(weights.astype(bf16), above).astype(bf16))
    first = jnp.concatenate(pieces[0], 0).T.astype(bf16)
    out[...] = jnp.concatenate([first] + pieces[1] + pieces[2], 1).reshape(out.shape)


def attention_call(kernel, values, logs, layout, out_width, work, name):
    parts, tokens, triple = values[0].shape
    heads = triple // 3 // HD
    temporal = len(layout) == 3
    chunk = 16
    grid = (parts, layout[0])
    if temporal:
        assert layout[2] % chunk == 0
        grid = grid + (layout[2] // chunk,)
    groups = tokens // P_SIZE

    def spec(width):
        if temporal:
            return pl.BlockSpec((1, 1, layout[1], chunk, width), lambda p, g, c: (p, g, 0, c, 0))
        return pl.BlockSpec((1, 1, layout[1], width), lambda p, g: (p, g, 0, 0))

    if temporal:
        log_spec = pl.BlockSpec((1, 1, heads, P_SIZE), lambda p, g, c: (p, g * grid[2] + c, 0, 0))
    else:
        log_spec = pl.BlockSpec((1, 1, heads, P_SIZE), lambda p, g: (p, g, 0, 0))
    out_shape = [jax.ShapeDtypeStruct((parts,) + layout + (out_width,), bf16)]
    out_specs = [spec(out_width)]
    in_specs = [spec(v.shape[-1]) for v in values]
    given = [v.reshape((parts,) + layout + (v.shape[-1],)) for v in values]
    if logs is None:
        out_shape.append(jax.ShapeDtypeStruct((parts, groups, heads, P_SIZE), f32))
        out_specs.append(log_spec)
    else:
        in_specs.append(log_spec)
        given.append(logs)
    result = pl.pallas_call(
        functools.partial(kernel, temporal, chunk),
        grid=grid,
        in_specs=in_specs,
        out_specs=out_specs,
        out_shape=out_shape,
        cost_estimate=pl.CostEstimate(
            flops=tokens * parts * heads * P_SIZE * 128 * work,
            transcendentals=tokens * parts * heads * P_SIZE,
            bytes_accessed=tokens * parts * out_width * 8,
        ),
        name=name,
    )(*given)
    return [result[0].reshape(parts, tokens, out_width)] + list(result[1:])


def norm_forward(stream):
    center = stream - over_u(jnp.sum(stream, 1, keepdims=True)) / D
    inverse = lax.rsqrt(over_u(jnp.sum(center * center, 1, keepdims=True)) / D + EPSILON)
    return center * inverse, inverse


def norm_backward(grad_normed, normed, inverse):
    first, second = over_u(
        (
            jnp.sum(grad_normed, 1, keepdims=True),
            jnp.sum(grad_normed * normed, 1, keepdims=True),
        )
    )
    return inverse * (grad_normed - first / D - normed * (second / D))


def spread(vector, tokens):
    groups, width = vector.shape
    if groups == 1:
        return vector
    return jnp.broadcast_to(vector[:, None, :], (groups, tokens // groups, width)).reshape(tokens, width)


def group_sum(value, groups):
    return jnp.sum(value.reshape(groups, -1, value.shape[-1]), 1)


def shards(
    latents, cond, w_ada, b_ada, w_qkv, b_qv, w_out, b_out, w_fc1, b_fc1, w_fc2, b_fc2, cotangent
):
    batches, width, tokens = latents.shape
    lat_count = cond.shape[1]
    rows = lax.axis_size("row")
    parts = lax.axis_size("m")
    split = lax.axis_size("u")
    row = lax.axis_index("row")
    part_here = lax.axis_index("m")
    span = parts * width
    order = jnp.asarray(row_order(rows), jnp.int32)
    inverse_order = jnp.asarray(np.argsort(row_order(rows)), jnp.int32)
    part_ids = part_here ^ jnp.arange(parts)
    frames_dev = tokens // P_SIZE
    pos_block = tokens // (lat_count * NF)
    spatial = (frames_dev, P_SIZE)
    temporal = (lat_count, NF, pos_block)

    relative = split == 1
    depth = D // rows
    if relative:
        slot = jnp.arange(D)
        source = (row ^ order[slot // depth]) * depth + slot % depth
        exchange = (jnp.arange(D)[:, None] == source[None, :]).astype(bf16)

    def vector_rel(value):
        if not relative:
            return value
        shaped = value.reshape(value.shape[:-1] + (rows, depth))
        return jnp.take(shaped, row ^ order, axis=-2).reshape(value.shape)

    def vector_plain(value):
        if not relative:
            return value
        shaped = value.reshape(value.shape[:-1] + (rows, depth))
        return jnp.take(shaped, inverse_order[row ^ jnp.arange(rows)], axis=-2).reshape(value.shape)

    def stream_plain(value):
        return dot_nt(value, exchange).astype(bf16) if relative else value

    def stream_rel(value):
        return dot_nn(value, exchange) if relative else value.astype(f32)

    def send_positions(value):
        shaped = value.reshape(frames_dev, rows, pos_block, span).swapaxes(0, 1)
        return lax.all_to_all(shaped, "row", 0, 0).reshape(tokens, span)

    def send_frames(value):
        shaped = value.reshape(rows, frames_dev, pos_block, span)
        return lax.all_to_all(shaped, "row", 0, 0).swapaxes(0, 1).reshape(tokens, span)

    def gathered(gather):
        pieces = gather.pieces()
        arrays = [value.reshape(-1, value.shape[-1]) for value in gather.arrays]
        if relative:
            return Weight(arrays, pieces)
        places = inverse_order[row ^ jnp.arange(rows)]
        blocks = []
        for entries in pieces:
            entries = sorted(entries, key=lambda entry: entry[3])
            block = jnp.concatenate([arrays[n][a : a + count] for n, a, count, _ in entries], 0)
            blocks.append(jnp.take(block.reshape(rows, depth, -1), places, axis=0).reshape(block.shape))
        return Weight(blocks, [[(part, 0, D, 0)] for part in range(parts)])

    def scatter(stacks, kind):
        if not relative:
            stacks = [
                jnp.take(s.reshape(s.shape[0], rows, depth, -1), row ^ order, axis=1).reshape(s.shape)
                for s in stacks
            ]
        return Scatter(stacks[0], stacks[1], rows, parts, kind)

    def scatters(stacks, kind):
        if len(stacks) == 1:
            return [scatter(stacks[0], kind)]
        return [scatter(pair, place) for place, pair in enumerate(stacks)]

    def own_share(value):
        return value if relative else lax.dynamic_slice_in_dim(value, lax.axis_index("u") * span, span, 1)

    cond_float = cond.astype(f32)
    cond_low = jax.nn.silu(cond_float).astype(bf16)
    mod_partial = jnp.einsum("mlr,brjk->mlbjk", cond_low, w_ada, preferred_element_type=f32)
    mod_partial = mod_partial + jnp.where(row == 0, b_ada.astype(f32), 0.0)[None, None]
    small = jnp.concatenate(
        [b.astype(f32).reshape(-1) for b in (b_qv, b_out, b_fc1, b_fc2)]
    )
    packed = jnp.concatenate(
        [mod_partial.reshape(batches, -1), jnp.broadcast_to(small, (parts,) + small.shape)], 1
    )
    packed = lax.all_to_all(packed, "m", split_axis=0, concat_axis=0, tiled=True)
    mod_size = lat_count * 12 * width
    mod_here = all_sum(packed[:, :mod_size], "row").reshape(parts, lat_count, 2, 6, width)
    mod_here = vector_rel(jnp.moveaxis(mod_here, 0, -2).reshape(lat_count, 2, 6, span))
    small = packed[:, mod_size:]
    sizes = np.cumsum([0, 4 * width, 2 * width, 2 * b_fc1.shape[1], 2 * width])
    all_qv, all_out, all_fc1, all_fc2 = [small[:, a:b] for a, b in zip(sizes[:-1], sizes[1:])]
    all_qv = jnp.take(all_qv.reshape(parts, 2, 2, width), part_ids, axis=0)
    all_fc1 = jnp.take(all_fc1.reshape(parts, 2, -1), part_ids, axis=0)
    all_out = vector_rel(jnp.moveaxis(all_out.reshape(parts, 2, width), 0, 1).reshape(2, span))
    all_fc2 = vector_rel(jnp.moveaxis(all_fc2.reshape(parts, 2, width), 0, 1).reshape(2, span))

    zeros = jnp.zeros((parts, width), f32)
    bias_qkv = [
        jnp.concatenate([all_qv[:, b, 0], zeros, all_qv[:, b, 1]], 1)[:, None, :] for b in range(2)
    ]
    bias_fc1 = [all_fc1[:, b][:, None, :] for b in range(2)]
    hidden_width = w_fc1.shape[2]
    mixed_cols, out_cols, hidden_cols = (0, 3 * width), (3 * width, 4 * width), (0, hidden_width)
    middle_cut = 4 * width // 256 * 128 + 128
    mixed_cuts = [(0, middle_cut), (middle_cut, 4 * width)]
    hidden_cut = hidden_width // 256 * 128 + 128
    fc_cuts = ([hidden_cols], [(0, hidden_cut), (hidden_cut, hidden_width)])
    layouts = (spatial, temporal)
    groups_of = (1, lat_count)

    def shard_of(b, name):
        if name == "mixed":
            return jnp.concatenate([w_qkv[b].reshape(depth, 3 * width), w_out[b]], 1)
        return (w_fc1 if name == "fc1" else w_fc2)[b]

    def own_batch(value):
        return lax.all_to_all(value, "m", 0, 0).reshape(span, tokens)

    def to_stream(value):
        return dot_tn(value, exchange) if relative else value.T.astype(f32)

    def to_argument(value):
        return lax.all_to_all(value.reshape(parts, width, tokens), "m", 0, 0)

    lat_here = row * frames_dev // NF
    mod_space = lax.dynamic_slice_in_dim(mod_here[:, 0], lat_here, 1, 0)
    mods = [
        [spread(m[:, column], tokens) for column in range(6)] for m in (mod_space, mod_here[:, 1])
    ]

    def open_stage(b, stream):
        normed, inverse = norm_forward(stream)
        hidden = features_all((normed * (1.0 + mods[b][1]) + mods[b][0]).astype(bf16))
        return {"stream": stream, "normed": normed, "inverse": inverse, "hidden": hidden}

    def attention_stage(b, k):
        qkv = project(
            k["hidden"], weights[b]["mixed"], mixed_cols, [bias_qkv[b]], lambda v, c: (v + c,), [bf16], "qkv"
        )[0]
        attended, logs = attention_call(forward_kernel, [qkv], None, layouts[b], width, 4, "attend")
        return {**k, "qkv": qkv, "attended": attended, "logs": logs}

    fused = relative and lat_count == 1

    def shaped(*kinds):
        return [jax.ShapeDtypeStruct(shape, kind) for shape, kind in kinds]

    full = (tokens, span)

    def middle_stage(b, k):
        if fused:
            made = contract(
                k["attended"], weights[b]["mixed"], out_cols, "out",
                [k["stream"]], [all_out[b][None], mods[b][2], mods[b][4], mods[b][3]],
                shaped((full, f32), (full, f32), (full, f32), ((tokens, 1), f32), (full, bf16)),
                finish_middle,
            )
            return {**k, **dict(zip(("branch", "middle", "normed2", "inverse2", "hidden2"), made))}
        branch = features_sum(contract(k["attended"], weights[b]["mixed"], out_cols, "out")) + all_out[b]
        middle = k["stream"] + mods[b][2] * branch
        normed, inverse = norm_forward(middle)
        hidden = features_all((normed * (1.0 + mods[b][4]) + mods[b][3]).astype(bf16))
        return {**k, "branch": branch, "middle": middle, "normed2": normed, "inverse2": inverse, "hidden2": hidden}

    def up_stage(b, k):
        act, slope = project(
            k["hidden2"], weights[b]["fc1"], hidden_cols, [bias_fc1[b]], gelu_pair, [bf16, bf16], "up"
        )
        return {**k, "act": act, "slope": slope}

    def down_stage(b, k):
        if fused:
            branch, result = contract(
                k["act"], weights[b]["fc2"], hidden_cols, "down",
                [k["middle"]], [all_fc2[b][None], mods[b][5]],
                shaped((full, f32), (full, bf16)), finish_stream,
            )
            return result, {**k, "branch2": branch}
        branch = features_sum(contract(k["act"], weights[b]["fc2"], hidden_cols, "down")) + all_fc2[b]
        return k["middle"] + mods[b][5] * branch, {**k, "branch2": branch}

    def fc2_grads(b, k, grad):
        low = features_all((mods[b][5] * grad).astype(bf16))
        stacks, (total_low,), _ = weight_grads([(low, k["act"])], fc_cuts[b], "grad_fc2")
        return {**k, "grad": grad, "low2": low, "sum_b2": own_share(total_low)}, scatters(stacks, KINDS[b]["fc2"])

    def up_back(b, k):
        grad_pre = project(
            k["low2"], weights[b]["fc2"], hidden_cols, [k["slope"]],
            lambda v, s: (v * s.astype(f32),), [bf16], "up_back",
        )[0]
        stacks, _, (total_pre,) = weight_grads([(k["hidden2"], grad_pre)], fc_cuts[b], "grad_fc1")
        return {**k, "pre": grad_pre, "sum_b1": total_pre[:, 0]}, scatters(stacks, KINDS[b]["fc1"])

    def hidden2_back(b, k):
        if fused:
            middle, low, sums = contract(
                k["pre"], weights[b]["fc1"], hidden_cols, "hidden2_back",
                [k["grad"], k["normed2"], k["branch"], k["inverse2"]], [mods[b][4], mods[b][2]],
                shaped((full, f32), (full, bf16), ((3, span), f32)), finish_middle_back,
            )
            return {**k, "g_middle": middle, "low1": low, "sums2": sums}
        grad_hidden = features_sum(contract(k["pre"], weights[b]["fc1"], hidden_cols, "hidden2_back"))
        return {**k, "g_hidden2": grad_hidden}

    def attention_back(b, k):
        if fused:
            middle, low = k["g_middle"], k["low1"]
        else:
            grad_hidden = k["g_hidden2"]
            back = norm_backward(grad_hidden * (1.0 + mods[b][4]), k["normed2"], k["inverse2"])
            middle = k["grad"] + back
            low = features_all((mods[b][2] * middle).astype(bf16))
        grad_att = project(low, weights[b]["mixed"], out_cols, [], lambda v: (v,), [bf16], "out_back")[0]
        grad_qkv = attention_call(
            backward_kernel, [k["qkv"], grad_att, k["attended"]], k["logs"], layouts[b], 3 * width, 10, "attend_back"
        )[0]
        return {**k, "g_middle": middle, "low1": low, "g_qkv": grad_qkv}

    def mixed_grads(b, k):
        stacks, (_, total_low), (total_qkv, _) = weight_grads(
            [(k["hidden"], k["g_qkv"]), (k["low1"], k["attended"])], mixed_cuts, "grad_mixed"
        )
        return {**k, "sum_bo": own_share(total_low), "sum_qkv": total_qkv[:, 0]}, [
            scatter(pair, kind) for kind, pair in enumerate(stacks)
        ]

    def stream_back(b, k):
        biases = (
            k["sum_qkv"][:, :width], k["sum_qkv"][:, 2 * width :], k["sum_bo"], k["sum_b1"], k["sum_b2"],
        )
        if fused:
            stream, sums = contract(
                k["g_qkv"], weights[b]["mixed"], mixed_cols, "hidden_back",
                [k["g_middle"], k["normed"], k["inverse"]], [mods[b][1]],
                shaped((full, bf16), ((2, span), f32)), finish_stream_back,
            )
            return stream, ((sums, k["sums2"], k["grad"], k["branch2"]), biases)
        grad_hidden = features_sum(contract(k["g_qkv"], weights[b]["mixed"], mixed_cols, "hidden_back"))
        back = norm_backward(grad_hidden * (1.0 + mods[b][1]), k["normed"], k["inverse"])
        groups = groups_of[b]
        modulate_grad = jnp.stack(
            [
                group_sum(grad_hidden, groups),
                group_sum(grad_hidden * k["normed"], groups),
                group_sum(k["g_middle"] * k["branch"], groups),
                group_sum(k["g_hidden2"], groups),
                group_sum(k["g_hidden2"] * k["normed2"], groups),
                group_sum(k["grad"] * k["branch2"], groups),
            ],
            1,
        )
        return k["g_middle"] + back, (modulate_grad, biases)

    def modulate_sums(made):
        if not fused:
            return made
        sums, sums2, grad, branch = made
        last_sum = jnp.sum(grad * branch, 0, keepdims=True)
        return jnp.concatenate([sums, sums2[2:], sums2[:2], last_sum], 0)[None]

    def pack_small(small_space, small_time):
        mod_grad_space, biases_space = modulate_sums(small_space[0]), small_space[1]
        mod_grad_time, biases_time = modulate_sums(small_time[0]), small_time[1]
        onehot = (jnp.arange(lat_count) == lat_here).astype(f32)
        mod_grads = jnp.stack([onehot[:, None, None] * mod_grad_space, mod_grad_time], 1)
        row_sums = [pair[place] for place in (2, 4) for pair in (biases_space, biases_time)]
        streams = vector_plain(jnp.concatenate([mod_grads.reshape(-1, span)] + row_sums, 0))
        streams = jnp.moveaxis(streams.reshape(-1, parts, width), 1, 0)
        ordered = [pair[place] for place in (0, 1, 3) for pair in (biases_space, biases_time)]
        ordered = jnp.take(jnp.concatenate(ordered, 1), part_ids, axis=0)
        mods_count = lat_count * 12
        pieces = [
            streams[:, :mods_count].reshape(parts, -1),
            ordered[:, : 4 * width],
            streams[:, mods_count : mods_count + 2].reshape(parts, -1),
            ordered[:, 4 * width :],
            streams[:, mods_count + 2 :].reshape(parts, -1),
        ]
        packed = jnp.concatenate(pieces, 1)
        sizes = [mods_count * width] + [width] * 6 + [hidden_width] * 2 + [width] * 2
        sent = lax.all_to_all(packed, "m", split_axis=0, concat_axis=0, tiled=True)
        return packed, sent, np.cumsum([0] + sizes)

    names = ("mixed", "fc1", "fc2")
    gathers = [Gather(shard_of(b, n), rows, parts, KINDS[b][n]) for b in range(2) for n in names]
    weights = [{}, {}]
    depth_of = len(gathers[0].plan)

    def move(*pairs, after=None):
        tail = None
        for item, until in pairs:
            while item.done < min(until, depth_of):
                if isinstance(item, Gather):
                    tail = item.step(tail)
                else:
                    item.step(after)

    def ready(number):
        weights[number // 3][names[number % 3]] = gathered(gathers[number])

    last = depth_of
    g = gathers
    first = depth_of - 3
    move((g[0], first - 1), (g[1], first - 1))
    fence(g, ())
    move((g[0], first), (g[1], first))
    first_in, top = fence(g, (own_batch(latents), own_batch(cotangent)))
    move((g[0], last - 2), (g[1], last - 2), (g[2], first - 1), (g[3], first - 1))
    first_in, mods, top = fence(g, (to_stream(first_in), mods, top.T))
    move((g[0], last - 1), (g[1], last - 1), (g[2], first), (g[3], first))
    k0 = fence(g, open_stage(0, first_in))
    move((g[2], last - 2), (g[3], last - 2), (g[4], first - 1), (g[5], first - 1), (g[0], last), (g[1], last))
    fence(g, ())
    ready(0)
    ready(1)
    move((g[2], last - 1), (g[3], last - 1), (g[4], first), (g[5], first))
    k0 = fence(g, middle_stage(0, attention_stage(0, k0)))
    move((g[2], last), (g[3], last), (g[4], last - 2), (g[5], last - 2))
    ready(2)
    first_out, k0 = down_stage(0, up_stage(0, k0))
    first_out = stream_plain(first_out.astype(bf16))
    k0, first_out, top = fence(g, (k0, first_out, top))
    ready(2)
    ready(3)
    move((g[4], last - 1), (g[5], last - 1))
    k1 = open_stage(1, stream_rel(send_positions(first_out)))
    k1 = attention_stage(1, k1)
    k0, k1, top = fence(g, (k0, k1, top))
    move((g[4], last), (g[5], last))
    grad_top = send_positions(top)
    k1 = middle_stage(1, k1)
    k0, k1 = fence(g, (k0, k1))
    ready(4)
    ready(5)
    k1 = up_stage(1, k1)
    grad_top, _ = lax.optimization_barrier((grad_top, k1["act"]))
    k1, s5 = fc2_grads(1, k1, stream_rel(grad_top))

    def to(count, *lists, after=None):
        move(*[(s, count) for items in lists for s in items], after=after)

    k0, k1 = fence(s5, (k0, k1))
    to(1, s5)
    second_out, k1 = down_stage(1, k1)
    second_out = stream_plain(second_out.astype(bf16))
    k0, k1, second_out = fence(s5, (k0, k1, second_out))
    to(2, s5)
    output = send_frames(second_out)
    k1, s4 = up_back(1, k1)
    k0, k1, output = fence(s4 + s5, (k0, k1, output))
    to(1, s4)
    to(3, s5)
    k1 = hidden2_back(1, k1)
    k0, k1 = fence(s4 + s5, (k0, k1))
    to(2, s4)
    to(4, s5)
    k1 = attention_back(1, k1)
    k1, s3 = mixed_grads(1, k1)
    k0, k1, output = fence(s3 + s4 + s5, (k0, k1, output.T))
    to(3, s4)
    to(last, s5)
    grad_mid, small_time = stream_back(1, k1)
    grad_mid = stream_plain(grad_mid.astype(bf16))
    k0, grad_mid, small_time, output = fence(s3 + s4 + s5, (k0, grad_mid, small_time, output))
    to(1, s3)
    grad_low = send_frames(grad_mid)
    k0, grad_low, small_time, output = fence(s3 + s4 + s5, (k0, grad_low, small_time, output))
    k0, s2 = fc2_grads(0, k0, stream_rel(grad_low))
    to(1, s2)
    k0, s1 = up_back(0, k0)
    to(2, s3, after=k0["pre"])
    to(4, s4, after=k0["pre"])
    k0, small_time, output = fence(s1 + s2 + s3 + s4 + s5, (k0, small_time, output))
    to(last, s4)
    to(3, s3)
    k0 = hidden2_back(0, k0)
    to(1, s1)
    k0, small_time, output = fence(s1 + s2 + s3 + s4 + s5, (k0, small_time, output))
    to(2, s2, s1)
    to(4, s3)
    k0 = attention_back(0, k0)
    k0, s0 = mixed_grads(0, k0)
    grad_first, small_space = stream_back(0, k0)
    grad_first, small, output = fence(s0 + s1 + s2 + s3, (grad_first, (small_space, small_time), output))
    to(1, s0)
    small, _ = lax.optimization_barrier((small, s0[0].arrays[1]))
    made, packed, counts = pack_small(small[0], small[1])
    to(3, s2, s1, after=made)
    to(last, s3)
    grad_first, packed, output = fence(s0 + s1 + s2 + s3, (grad_first, packed, output))
    to(4, s2, s1)
    to(2, s0)
    packed, _ = lax.optimization_barrier((packed, s0[0].arrays[-2]))
    output = to_argument(output)
    output, grad_first = fence(s0 + s1 + s2, (output, grad_first))
    to(last, s2, s1)
    to(3, s0)
    fence(s0 + s1 + s2, ())
    to(last, s0, s1, s2, s3, s4, s5)
    joined = lambda items: jnp.concatenate([item.result() for item in items], 1)
    weights_space = [joined(items) for items in (s0, s1, s2)]
    weights_time = [joined(items) for items in (s3, s4, s5)]
    grad_first = grad_first.astype(bf16)
    grad_first = dot_nt(exchange, grad_first).astype(bf16) if relative else grad_first.T
    grad_latents = to_argument(grad_first).astype(f32)

    mod_part = packed[:, : counts[1]]
    bias_part = jnp.sum(packed[:, counts[1] :], 0, keepdims=True)
    flat = jnp.concatenate([mod_part.reshape(1, -1), bias_part], 1)
    flat = all_sum(flat, "row")[0]
    mod_grad_low = flat[: batches * counts[1]].reshape(batches, lat_count, 2, 6, width).astype(bf16)
    bias_part = flat[batches * counts[1] :]
    bias_out = [bias_part[a - counts[1] : b - counts[1]] for a, b in zip(counts[1:-1], counts[2:])]
    grad_bias_qv = jnp.stack(
        [jnp.stack([bias_out[0], bias_out[2]]), jnp.stack([bias_out[1], bias_out[3]])]
    )
    grad_bias_out = jnp.stack(bias_out[4:6])
    grad_bias_fc1 = jnp.stack(bias_out[6:8])
    grad_bias_fc2 = jnp.stack(bias_out[8:10])
    grad_bias_ada = jnp.sum(mod_grad_low.astype(f32), (0, 1))
    grad_weight_ada = jnp.einsum("mlr,mlbjk->brjk", cond_low, mod_grad_low, preferred_element_type=f32)
    cond_partial = jnp.einsum("mlbjk,brjk->mlr", mod_grad_low, w_ada, preferred_element_type=f32)
    cond_total = over_u(all_sum(cond_partial, "m"))
    sigmoid_cond = jax.nn.sigmoid(cond_float)
    grad_condition = cond_total * sigmoid_cond * (1.0 + cond_float * (1.0 - sigmoid_cond))
    grad_weight_qkv, grad_weight_out, grad_weight_fc1, grad_weight_fc2 = [], [], [], []
    for mixed, first, second in (weights_space, weights_time):
        grad_weight_qkv.append(mixed[:, : 3 * width].reshape(depth, 3, width))
        grad_weight_out.append(mixed[:, 3 * width :])
        grad_weight_fc1.append(first)
        grad_weight_fc2.append(second)
    return (
        output,
        grad_latents,
        grad_condition,
        grad_weight_ada,
        grad_bias_ada,
        jnp.stack(grad_weight_qkv),
        grad_bias_qv,
        jnp.stack(grad_weight_out),
        grad_bias_out,
        jnp.stack(grad_weight_fc1),
        grad_bias_fc1,
        jnp.stack(grad_weight_fc2),
        grad_bias_fc2,
    )


def solution(mesh):
    rows, columns = mesh.devices.shape

    def placed(latents, *rest):
        parts = latents.shape[0]
        inner = Mesh(mesh.devices.reshape(rows, columns // parts, parts), ("row", "u", "m"))
        col = ("u", "m")
        in_specs = (
            P(None, col, "row"),
            P(None, None, "row"),
            P(None, "row", None, col),
            P(None, None, col),
            P(None, "row", None, col),
            P(None, None, col),
            P(None, "row", col),
            P(None, col),
            P(None, "row", col),
            P(None, col),
            P(None, "row", col),
            P(None, col),
            P(None, col, "row"),
        )
        out_specs = (P(None, col, "row"),) + in_specs[:1] + in_specs[1:-1]
        return jax.shard_map(
            shards, mesh=inner, in_specs=in_specs, out_specs=out_specs, check_vma=False
        )(latents, *rest)

    return placed
```

```python
import functools

import jax
import jax.numpy as jnp
import numpy as np
from jax import lax
from jax.experimental import pallas as pl
from jax.experimental.pallas import tpu as pltpu
from jax.sharding import Mesh
from jax.sharding import PartitionSpec as P

D = 1152
HD = 72
P_SIZE = 256
NF = 16
SCALE = HD ** (-0.5)
EPSILON = 1e-06


KINDS = ({"mixed": 0, "fc1": 1, "fc2": 0}, {"mixed": 1, "fc1": 0, "fc2": 1})

f32 = jnp.float32
bf16 = jnp.bfloat16


def bits_of(count):
    found = []
    bit = count // 2
    while bit:
        found.append(bit)
        bit //= 2
    return found


def swap(value, axis, bit):
    count = lax.axis_size(axis)
    return lax.ppermute(value, axis, [(i, i ^ bit) for i in range(count)])


def row_order(rows):
    order = [0]
    for bit in bits_of(rows):
        order = order + [j ^ bit for j in order]
    return order


def step_plan(rows, parts, kind):
    by_row = [("row", bit) for bit in bits_of(rows)]
    by_part = [("m", bit) for bit in bits_of(parts)]
    if kind == 0:
        return by_row + by_part
    return by_row[:-1] + by_part[:-1] + by_row[-1:] + by_part[-1:]


def moved(label, axis, bit):
    return (label[0] ^ bit, label[1]) if axis == "row" else (label[0], label[1] ^ bit)


def total(terms):
    result = terms[0].astype(f32)
    for term in terms[1:]:
        result = result + term.astype(f32)
    return result


def sum_rows(terms, names, first, count):
    width = terms[0][0].shape[2]
    rows = 576 if count % 576 == 0 else count // 2 if count % 32 == 0 else count
    assert first % rows == 0

    def body(*refs):
        value = refs[0][...].astype(f32)
        for ref in refs[1:-1]:
            value = value + ref[...].astype(f32)
        refs[-1][...] = value.astype(bf16)

    def spec(lead):
        return pl.BlockSpec((1, rows, width), lambda i, r: (lead + i, first // rows + r, 0))

    return pl.pallas_call(
        body,
        grid=(names, count // rows),
        in_specs=[spec(lead) for _, lead in terms],
        out_specs=pl.BlockSpec((1, rows, width), lambda i, r: (i, r, 0)),
        out_shape=jax.ShapeDtypeStruct((names, count, width), bf16),
        cost_estimate=pl.CostEstimate(
            flops=len(terms) * names * count * width,
            transcendentals=0,
            bytes_accessed=2 * (len(terms) + 1) * names * count * width,
        ),
        name="sum_rows",
    )(*[value for value, _ in terms])


class Gather:
    def __init__(self, shard, rows, parts, kind):
        self.rows, self.parts, self.depth = rows, parts, shard.shape[0]
        self.plan = step_plan(rows, parts, kind)
        self.labels = [[(0, 0)]]
        self.arrays = [shard]
        self.done = 0

    def step(self, after=None):
        axis, bit = self.plan[self.done]
        last_axis, last_bit = self.plan[-1]
        left = len(self.plan) - self.done

        def behind(value):
            return value if after is None else lax.optimization_barrier((value, after))[0]

        if left == 1:
            names, value = self.labels[1], self.arrays[1]
            result = swap(behind(value), axis, bit)
            self.labels.append([moved(name, axis, bit) for name in names])
            self.arrays.append(result)
        else:
            (names,), (value,) = self.labels, self.arrays
            result = after
            other = swap(value, axis, bit)
            other_names = [moved(name, axis, bit) for name in names]
            if left > 2:
                self.labels = [names + other_names]
                self.arrays = [jnp.concatenate([value, other], 0)]
            else:
                result = swap(behind(value), last_axis, last_bit)
                self.labels = [names, other_names, [moved(name, last_axis, last_bit) for name in names]]
                self.arrays = [value, other, result]
        self.done += 1
        return result

    def pieces(self):
        order, depth = row_order(self.rows), self.depth
        found = []
        for part in range(self.parts):
            entries = []
            for number, names in enumerate(self.labels):
                hits = [place for place, name in enumerate(names) if name[1] == part]
                if hits:
                    rank = order.index(names[hits[0]][0])
                    assert [names[h][0] for h in hits] == order[rank : rank + len(hits)]
                    assert hits == list(range(hits[0], hits[0] + len(hits)))
                    entries.append((number, hits[0] * depth, len(hits) * depth, rank * depth))
            found.append(entries)
        return found


class Scatter:
    def __init__(self, sent, kept, rows, parts, kind):
        self.plan = step_plan(rows, parts, kind)[::-1]
        self.order = row_order(rows)
        self.depth = kept.shape[1] // rows
        self.span = rows
        assert self.plan[0] == ("m", 1)
        self.arrays = [kept, sent]
        self.outgoing = 1
        self.gaining = [part for part in range(parts) if not part & 1]
        self.live = {part: [(0, place)] for place, part in enumerate(self.gaining)}
        self.done = 0

    def take(self, term, first, count):
        number, lead = term
        return self.arrays[number][lead, first : first + count]

    def sums(self, names, first, count):
        if self.depth % 16 == 0 and len(names) * count >= 4 * self.depth:
            leads = [[term[1] for term in terms] for terms in zip(*[self.live[n] for n in names])]
            numbers = [term[0] for term in self.live[names[0]]]
            assert all(list(l) == list(range(l[0], l[0] + len(l))) for l in leads)
            return sum_rows([(self.arrays[n], l[0]) for n, l in zip(numbers, leads)], len(names), first, count)
        return jnp.stack(
            [total([self.take(t, first, count) for t in self.live[n]]).astype(bf16) for n in names]
        )

    def step(self, after=None):
        axis, bit = self.plan[self.done]
        got = swap(self.arrays.pop(self.outgoing), axis, bit)
        if after is not None:
            got, _ = lax.optimization_barrier((got, after))
        self.arrays.append(got)
        for place, name in enumerate(self.gaining):
            self.live[name].append((len(self.arrays) - 1, place))
        self.done += 1
        self.prepare()

    def prepare(self):
        if self.done == len(self.plan):
            return
        axis, bit = self.plan[self.done]
        if axis == "m":
            names = [name for name in sorted(self.live) if name & bit]
            sent = self.sums(names, 0, self.span * self.depth)
            for name in names:
                self.live.pop(name)
            self.gaining = [name ^ bit for name in names]
        else:
            half = self.span // 2
            order = self.order
            assert all(order[half + p] == order[p] ^ bit for p in range(half))
            self.gaining = sorted(self.live)
            sent = self.sums(self.gaining, half * self.depth, half * self.depth)
            self.span = half
        self.outgoing = len(self.arrays)
        self.arrays.append(sent)

    def result(self):
        return total([self.take(t, 0, self.depth) for t in self.live[0]])


def fence(objects, values):
    arrays, values = lax.optimization_barrier(([o.arrays for o in objects], values))
    for o, fresh in zip(objects, arrays):
        o.arrays = list(fresh)
    return values


def all_sum(value, axis):
    for bit in bits_of(lax.axis_size(axis)):
        value = value + swap(value, axis, bit)
    return value


def over_u(value):
    return lax.psum(value, "u") if lax.axis_size("u") > 1 else value


def features_all(value):
    return lax.all_gather(value, "u", axis=1, tiled=True) if lax.axis_size("u") > 1 else value


def features_sum(value):
    if lax.axis_size("u") > 1:
        return lax.psum_scatter(value, "u", scatter_dimension=1, tiled=True)
    return value


def dot_nn(left, right):
    return lax.dot_general(left, right, (((1,), (0,)), ((), ())), preferred_element_type=f32)


def dot_nt(left, right):
    return lax.dot_general(left, right, (((1,), (1,)), ((), ())), preferred_element_type=f32)


def dot_tn(left, right):
    return lax.dot_general(left, right, (((0,), (0,)), ((), ())), preferred_element_type=f32)


LIMIT = 56 * 1024 * 1024


class Weight:
    def __init__(self, arrays, pieces):
        self.arrays = [value.reshape(-1, value.shape[-1]) for value in arrays]
        self.places = pieces
        self.parts = len(pieces)
        self.height = sum(rows for _, _, rows, _ in pieces[0])
        self.width = self.arrays[0].shape[1]

    def scratch(self):
        pieces = len(self.places[0])
        return [
            pltpu.VMEM((self.parts, self.height, self.width), bf16),
            pltpu.SemaphoreType.DMA((self.parts, pieces)),
        ]

    def copies(self, part, refs, held, sems):
        return [
            pltpu.make_async_copy(
                refs[number].at[pl.ds(start, rows)], held.at[part, pl.ds(to, rows)], sems.at[part, place]
            )
            for place, (number, start, rows, to) in enumerate(self.places[part])
        ]

    def arrive(self, step, refs, held, sems):
        @pl.when(step == 0)
        def _():
            for part in range(self.parts):
                for copy in self.copies(part, refs, held, sems):
                    copy.start()

        for part in range(self.parts):

            @pl.when(step == part)
            def _(part=part):
                for copy in self.copies(part, refs, held, sems):
                    copy.wait()


def cut_last(load, low, high):
    base = low // 128 * 128
    value = load(base, high)
    return value if base == low else value[:, low - base :]


def whole_spec(shape):
    return pl.BlockSpec(shape, lambda s: (0,) * len(shape))


def part_spec(shape):
    return pl.BlockSpec((1,) + shape, lambda s: (s,) + (0,) * len(shape))


def project(x, weight, columns, extras, epilogue, out_types, name):
    tokens, depth = x.shape
    low, high = columns
    n = high - low
    count = len(weight.arrays)

    def body(*refs):
        x_ref, refs = refs[0], refs[1:]
        w_refs, refs = refs[:count], refs[count:]
        extra_refs, refs = refs[: len(extras)], refs[len(extras) :]
        outs, (held, sems) = refs[: len(out_types)], refs[len(out_types) :]
        step = pl.program_id(0)
        weight.arrive(step, w_refs, held, sems)
        left = x_ref[...]
        right = cut_last(lambda a, b: held[step, :, a:b], low, high)
        made = epilogue(dot_nn(left, right), *[e[0] for e in extra_refs])
        for out, piece in zip(outs, made):
            out[0] = piece.astype(out.dtype)

    return pl.pallas_call(
        body,
        grid=(weight.parts,),
        in_specs=[whole_spec((tokens, depth))]
        + [pl.BlockSpec(memory_space=pl.ANY)] * count
        + [part_spec(e.shape[1:]) for e in extras],
        out_specs=[part_spec((tokens, n))] * len(out_types),
        out_shape=[jax.ShapeDtypeStruct((weight.parts, tokens, n), t) for t in out_types],
        scratch_shapes=weight.scratch(),
        compiler_params=pltpu.CompilerParams(vmem_limit_bytes=LIMIT),
        cost_estimate=pl.CostEstimate(
            flops=2 * tokens * depth * n * weight.parts,
            transcendentals=0,
            bytes_accessed=2 * weight.parts * n * (depth + 2 * tokens),
        ),
        name=name,
    )(x, *weight.arrays, *extras)


def contract(xs, weight, columns, name, large=(), small=(), outs=None, finish=None):
    parts, tokens, n = xs.shape
    low, high = columns
    count = len(weight.arrays)
    height = weight.height
    if finish is None:
        outs = [jax.ShapeDtypeStruct((tokens, height), f32)]

    def body(*refs):
        x_ref, refs = refs[0], refs[1:]
        w_refs, refs = refs[:count], refs[count:]
        large_refs, refs = refs[: len(large)], refs[len(large) :]
        small_refs, refs = refs[: len(small)], refs[len(small) :]
        out_refs, refs = refs[: len(outs)], refs[len(outs) :]
        held, sems = refs[:2]
        step = pl.program_id(0)
        acc = out_refs[0]
        if finish is not None:
            acc, local, large_sems = refs[2], refs[3:-1], refs[-1]
            copies = [
                pltpu.make_async_copy(ref, to, large_sems.at[place])
                for place, (ref, to) in enumerate(zip(large_refs, local))
            ]
        weight.arrive(step, w_refs, held, sems)
        if finish is not None:

            @pl.when(step == 0)
            def _():
                for copy in copies:
                    copy.start()

        right = cut_last(lambda a, b: held[step, :, a:b], low, high)
        value = dot_nt(x_ref[0], right)

        @pl.when(step == 0)
        def _():
            acc[...] = value

        @pl.when(step > 0)
        def _():
            acc[...] += value

        if finish is not None:

            @pl.when(step == parts - 1)
            def _():
                for copy in copies:
                    copy.wait()
                finish(acc, local, small_refs, out_refs)

    scratch = weight.scratch()
    if finish is not None:
        scratch.append(pltpu.VMEM((tokens, height), f32))
        scratch += [pltpu.VMEM(value.shape, value.dtype) for value in large]
        scratch.append(pltpu.SemaphoreType.DMA((max(len(large), 1),)))
    results = pl.pallas_call(
        body,
        grid=(parts,),
        in_specs=[part_spec((tokens, n))]
        + [pl.BlockSpec(memory_space=pl.ANY)] * (count + len(large))
        + [whole_spec(value.shape) for value in small],
        out_specs=[whole_spec(out.shape) for out in outs],
        out_shape=outs,
        scratch_shapes=scratch,
        compiler_params=pltpu.CompilerParams(vmem_limit_bytes=LIMIT),
        cost_estimate=pl.CostEstimate(
            flops=2 * tokens * height * n * parts,
            transcendentals=0,
            bytes_accessed=2 * parts * n * (height + tokens) + 4 * tokens * height * (1 + len(large)),
        ),
        name=name,
    )(xs, *weight.arrays, *large, *small)
    return results[0] if finish is None else results


ROWS = 16


def by_rows(tokens, work, sums=0, width=0):
    def turn(index, carried):
        made = work(pl.ds(pl.multiple_of(index * ROWS, ROWS), ROWS))
        return tuple(c + jnp.sum(m, 0, keepdims=True) for c, m in zip(carried, made or ()))

    return lax.fori_loop(0, tokens // ROWS, turn, (jnp.zeros((1, width), f32),) * sums)


def finish_middle(acc, large, small, outs):
    (stream,), (bias, gate, scale, shift) = large, small
    branch_out, middle_out, normed_out, inverse_out, hidden_out = outs

    def work(rows):
        branch = acc[rows, :] + bias[...]
        middle = stream[rows, :] + gate[...] * branch
        center = middle - jnp.sum(middle, 1, keepdims=True) / D
        inverse = lax.rsqrt(jnp.sum(center * center, 1, keepdims=True) / D + EPSILON)
        normed = center * inverse
        branch_out[rows, :] = branch
        middle_out[rows, :] = middle
        normed_out[rows, :] = normed
        inverse_out[rows, :] = inverse
        hidden_out[rows, :] = (normed * (1.0 + scale[...]) + shift[...]).astype(bf16)

    by_rows(acc.shape[0], work)


def finish_stream(acc, large, small, outs):
    (middle,), (bias, gate) = large, small
    branch_out, result_out = outs

    def work(rows):
        branch = acc[rows, :] + bias[...]
        branch_out[rows, :] = branch
        result_out[rows, :] = (middle[rows, :] + gate[...] * branch).astype(bf16)

    by_rows(acc.shape[0], work)


def norm_back(grad_hidden, scale, normed, inverse):
    grad_normed = grad_hidden * (1.0 + scale)
    first = jnp.sum(grad_normed, 1, keepdims=True) / D
    second = jnp.sum(grad_normed * normed, 1, keepdims=True) / D
    return inverse * (grad_normed - first - normed * second)


def finish_middle_back(acc, large, small, outs):
    (grad, normed, branch, inverse), (scale, gate) = large, small
    middle_out, low_out, sums_out = outs

    def work(rows):
        grad_hidden = acc[rows, :]
        middle = grad[rows, :] + norm_back(grad_hidden, scale[...], normed[rows, :], inverse[rows, :])
        middle_out[rows, :] = middle
        low_out[rows, :] = (gate[...] * middle).astype(bf16)
        return grad_hidden, grad_hidden * normed[rows, :], middle * branch[rows, :]

    made = by_rows(acc.shape[0], work, 3, acc.shape[1])
    sums_out[...] = jnp.concatenate(made, 0)


def finish_stream_back(acc, large, small, outs):
    (middle, normed, inverse), (scale,) = large, small
    stream_out, sums_out = outs

    def work(rows):
        grad_hidden = acc[rows, :]
        back = norm_back(grad_hidden, scale[...], normed[rows, :], inverse[rows, :])
        stream_out[rows, :] = (middle[rows, :] + back).astype(bf16)
        return grad_hidden, grad_hidden * normed[rows, :]

    made = by_rows(acc.shape[0], work, 2, acc.shape[1])
    sums_out[...] = jnp.concatenate(made, 0)


def weight_grads(pairs, cuts, name):
    tokens, depth = pairs[0][0].shape
    parts = pairs[0][1].shape[0]
    half = parts // 2
    widths = [g.shape[2] for _, g in pairs]
    full = sum(widths)
    count = len(pairs)

    def which(step):
        return jnp.where(step < half, 2 * step + 1, 2 * (step - half))

    def body(*refs):
        x_refs, refs = refs[:count], refs[count:]
        g_refs, refs = refs[:count], refs[count:]
        sent, refs = refs[: len(cuts)], refs[len(cuts) :]
        kept, refs = refs[: len(cuts)], refs[len(cuts) :]
        x_sums, refs = refs[:count], refs[count:]
        g_sums, turned = refs[:count], refs[count:]
        step = pl.program_id(0)

        @pl.when(step == 0)
        def _():
            for x_ref, x_sum, t_ref in zip(x_refs, x_sums, turned):
                value = x_ref[...].astype(f32)
                x_sum[...] = jnp.sum(value, 0, keepdims=True)
                t_ref[...] = value.T.astype(bf16)

        rights = [g_ref[0] for g_ref in g_refs]
        for right, g_sum in zip(rights, g_sums):
            g_sum[0] = jnp.sum(right.astype(f32), 0, keepdims=True)

        def fill(outs):
            made = [dot_nn(t_ref[...], r).astype(bf16) for t_ref, r in zip(turned, rights)]
            made = made[0] if count == 1 else jnp.concatenate(made, 1)
            for out, (low, high) in zip(outs, cuts):
                out[0] = made[:, low:high]

        @pl.when(step < half)
        def _():
            fill(sent)

        @pl.when(step >= half)
        def _():
            fill(kept)

    outs = pl.pallas_call(
        body,
        grid=(parts,),
        in_specs=[whole_spec((tokens, depth))] * count
        + [pl.BlockSpec((1, tokens, n), lambda s: (which(s), 0, 0)) for n in widths],
        out_specs=[
            pl.BlockSpec((1, depth, high - low), lambda s: (jnp.minimum(s, half - 1), 0, 0))
            for low, high in cuts
        ]
        + [
            pl.BlockSpec((1, depth, high - low), lambda s: (jnp.maximum(s - half, 0), 0, 0))
            for low, high in cuts
        ]
        + [whole_spec((1, depth))] * count
        + [pl.BlockSpec((1, 1, n), lambda s: (which(s), 0, 0)) for n in widths],
        out_shape=[jax.ShapeDtypeStruct((half, depth, high - low), bf16) for low, high in cuts] * 2
        + [jax.ShapeDtypeStruct((1, depth), f32)] * count
        + [jax.ShapeDtypeStruct((parts, 1, n), f32) for n in widths],
        scratch_shapes=[pltpu.VMEM((depth, tokens), bf16)] * count,
        compiler_params=pltpu.CompilerParams(vmem_limit_bytes=LIMIT),
        cost_estimate=pl.CostEstimate(
            flops=2 * tokens * depth * full * parts,
            transcendentals=0,
            bytes_accessed=2 * parts * full * (depth + tokens),
        ),
        name=name,
    )(*[x for x, _ in pairs], *[g for _, g in pairs])
    ranges = len(cuts)
    stacks = list(zip(outs[:ranges], outs[ranges : 2 * ranges]))
    outs = outs[2 * ranges :]
    return stacks, outs[:count], outs[count:]


def gelu_pair(value, bias):
    v = value + bias
    slope = 0.7978845608028654
    inner = jnp.tanh(slope * (v + 0.044715 * v * v * v))
    outer = 0.5 * (1.0 + inner)
    change = outer + 0.5 * v * (1.0 - inner * inner) * (slope * (1.0 + 3.0 * 0.044715 * v * v))
    return v * outer, change


POWER = SCALE * 1.4426950408889634


def allowed_pairs(temporal, span, tokens):
    if not temporal:
        return None
    first = lax.broadcasted_iota(jnp.int32, (tokens, tokens), 0)
    second = lax.broadcasted_iota(jnp.int32, (tokens, tokens), 1)
    return lax.rem(first, span) == lax.rem(second, span)


def head_columns(block, start, width):
    return [block[:, c * width + start : c * width + start + HD] for c in range(3)]


def forward_kernel(temporal, span, qkv, out, logs):
    width = qkv.shape[-1] // 3
    tokens = int(np.prod(qkv.shape[:-1]))
    allowed = allowed_pairs(temporal, span, tokens)
    block = qkv[...].reshape(tokens, 3 * width)
    done, kept = [], []
    for start in range(0, width, HD):
        query, key, value = head_columns(block, start, width)
        scores = dot_nt(key, query)
        if allowed is not None:
            scores = jnp.where(allowed, scores, -jnp.inf)
        largest = jnp.max(scores, 0, keepdims=True)
        powered = jnp.exp2((scores - largest) * POWER)
        summed = jnp.sum(powered, 0, keepdims=True)
        done.append(dot_tn(value, powered.astype(bf16)) / summed)
        kept.append(largest * POWER + jnp.log2(summed))
    out[...] = jnp.concatenate(done, 0).T.astype(bf16).reshape(out.shape)
    logs[...] = jnp.concatenate(kept, 0).reshape(logs.shape)


def backward_kernel(temporal, span, qkv, grad, attended, logs, out):
    width = qkv.shape[-1] // 3
    tokens = int(np.prod(qkv.shape[:-1]))
    allowed = allowed_pairs(temporal, span, tokens)
    block = qkv[...].reshape(tokens, 3 * width)
    outer = grad[...].reshape(tokens, width)
    turned = outer.astype(f32).T * attended[...].reshape(tokens, width).astype(f32).T
    log_rows = logs[...].reshape(width // HD, tokens)
    pieces = [[], [], []]
    for place, start in enumerate(range(0, width, HD)):
        query, key, value = head_columns(block, start, width)
        above = outer[:, start : start + HD]
        inner = jnp.sum(turned[start : start + HD], 0, keepdims=True)
        weights = jnp.exp2(dot_nt(key, query) * POWER - log_rows[place : place + 1])
        if allowed is not None:
            weights = jnp.where(allowed, weights, 0.0)
        grad_scores = (weights * (dot_nt(value, above) - inner)).astype(bf16)
        pieces[0].append(dot_tn(key, grad_scores) * SCALE)
        pieces[1].append((dot_nn(grad_scores, query) * SCALE).astype(bf16))
        pieces[2].append(dot_nn(weights.astype(bf16), above).astype(bf16))
    first = jnp.concatenate(pieces[0], 0).T.astype(bf16)
    out[...] = jnp.concatenate([first] + pieces[1] + pieces[2], 1).reshape(out.shape)


def attention_call(kernel, values, logs, layout, out_width, work, name):
    parts, tokens, triple = values[0].shape
    heads = triple // 3 // HD
    temporal = len(layout) == 3
    chunk = 16
    grid = (parts, layout[0])
    if temporal:
        assert layout[2] % chunk == 0
        grid = grid + (layout[2] // chunk,)
    groups = tokens // P_SIZE

    def spec(width):
        if temporal:
            return pl.BlockSpec((1, 1, layout[1], chunk, width), lambda p, g, c: (p, g, 0, c, 0))
        return pl.BlockSpec((1, 1, layout[1], width), lambda p, g: (p, g, 0, 0))

    if temporal:
        log_spec = pl.BlockSpec((1, 1, heads, P_SIZE), lambda p, g, c: (p, g * grid[2] + c, 0, 0))
    else:
        log_spec = pl.BlockSpec((1, 1, heads, P_SIZE), lambda p, g: (p, g, 0, 0))
    out_shape = [jax.ShapeDtypeStruct((parts,) + layout + (out_width,), bf16)]
    out_specs = [spec(out_width)]
    in_specs = [spec(v.shape[-1]) for v in values]
    given = [v.reshape((parts,) + layout + (v.shape[-1],)) for v in values]
    if logs is None:
        out_shape.append(jax.ShapeDtypeStruct((parts, groups, heads, P_SIZE), f32))
        out_specs.append(log_spec)
    else:
        in_specs.append(log_spec)
        given.append(logs)
    result = pl.pallas_call(
        functools.partial(kernel, temporal, chunk),
        grid=grid,
        in_specs=in_specs,
        out_specs=out_specs,
        out_shape=out_shape,
        cost_estimate=pl.CostEstimate(
            flops=tokens * parts * heads * P_SIZE * 128 * work,
            transcendentals=tokens * parts * heads * P_SIZE,
            bytes_accessed=tokens * parts * out_width * 8,
        ),
        name=name,
    )(*given)
    return [result[0].reshape(parts, tokens, out_width)] + list(result[1:])


def norm_forward(stream):
    center = stream - over_u(jnp.sum(stream, 1, keepdims=True)) / D
    inverse = lax.rsqrt(over_u(jnp.sum(center * center, 1, keepdims=True)) / D + EPSILON)
    return center * inverse, inverse


def norm_backward(grad_normed, normed, inverse):
    first, second = over_u(
        (
            jnp.sum(grad_normed, 1, keepdims=True),
            jnp.sum(grad_normed * normed, 1, keepdims=True),
        )
    )
    return inverse * (grad_normed - first / D - normed * (second / D))


def spread(vector, tokens):
    groups, width = vector.shape
    if groups == 1:
        return vector
    return jnp.broadcast_to(vector[:, None, :], (groups, tokens // groups, width)).reshape(tokens, width)


def group_sum(value, groups):
    return jnp.sum(value.reshape(groups, -1, value.shape[-1]), 1)


def shards(
    latents, cond, w_ada, b_ada, w_qkv, b_qv, w_out, b_out, w_fc1, b_fc1, w_fc2, b_fc2, cotangent
):
    batches, width, tokens = latents.shape
    lat_count = cond.shape[1]
    rows = lax.axis_size("row")
    parts = lax.axis_size("m")
    split = lax.axis_size("u")
    row = lax.axis_index("row")
    part_here = lax.axis_index("m")
    span = parts * width
    order = jnp.asarray(row_order(rows), jnp.int32)
    inverse_order = jnp.asarray(np.argsort(row_order(rows)), jnp.int32)
    part_ids = part_here ^ jnp.arange(parts)
    frames_dev = tokens // P_SIZE
    pos_block = tokens // (lat_count * NF)
    spatial = (frames_dev, P_SIZE)
    temporal = (lat_count, NF, pos_block)

    relative = split == 1
    depth = D // rows
    if relative:
        slot = jnp.arange(D)
        source = (row ^ order[slot // depth]) * depth + slot % depth
        exchange = (jnp.arange(D)[:, None] == source[None, :]).astype(bf16)

    def vector_rel(value):
        if not relative:
            return value
        shaped = value.reshape(value.shape[:-1] + (rows, depth))
        return jnp.take(shaped, row ^ order, axis=-2).reshape(value.shape)

    def vector_plain(value):
        if not relative:
            return value
        shaped = value.reshape(value.shape[:-1] + (rows, depth))
        return jnp.take(shaped, inverse_order[row ^ jnp.arange(rows)], axis=-2).reshape(value.shape)

    def stream_plain(value):
        return dot_nt(value, exchange).astype(bf16) if relative else value

    def stream_rel(value):
        return dot_nn(value, exchange) if relative else value.astype(f32)

    def send_positions(value):
        shaped = value.reshape(frames_dev, rows, pos_block, span).swapaxes(0, 1)
        return lax.all_to_all(shaped, "row", 0, 0).reshape(tokens, span)

    def send_frames(value):
        shaped = value.reshape(rows, frames_dev, pos_block, span)
        return lax.all_to_all(shaped, "row", 0, 0).swapaxes(0, 1).reshape(tokens, span)

    def gathered(gather):
        pieces = gather.pieces()
        arrays = [value.reshape(-1, value.shape[-1]) for value in gather.arrays]
        if relative:
            return Weight(arrays, pieces)
        places = inverse_order[row ^ jnp.arange(rows)]
        blocks = []
        for entries in pieces:
            entries = sorted(entries, key=lambda entry: entry[3])
            block = jnp.concatenate([arrays[n][a : a + count] for n, a, count, _ in entries], 0)
            blocks.append(jnp.take(block.reshape(rows, depth, -1), places, axis=0).reshape(block.shape))
        return Weight(blocks, [[(part, 0, D, 0)] for part in range(parts)])

    def scatter(stacks, kind):
        if not relative:
            stacks = [
                jnp.take(s.reshape(s.shape[0], rows, depth, -1), row ^ order, axis=1).reshape(s.shape)
                for s in stacks
            ]
        return Scatter(stacks[0], stacks[1], rows, parts, kind)

    def scatters(stacks, kind):
        if len(stacks) == 1:
            return [scatter(stacks[0], kind)]
        return [scatter(pair, place) for place, pair in enumerate(stacks)]

    def own_share(value):
        return value if relative else lax.dynamic_slice_in_dim(value, lax.axis_index("u") * span, span, 1)

    cond_float = cond.astype(f32)
    cond_low = jax.nn.silu(cond_float).astype(bf16)
    mod_partial = jnp.einsum("mlr,brjk->mlbjk", cond_low, w_ada, preferred_element_type=f32)
    mod_partial = mod_partial + jnp.where(row == 0, b_ada.astype(f32), 0.0)[None, None]
    small = jnp.concatenate(
        [b.astype(f32).reshape(-1) for b in (b_qv, b_out, b_fc1, b_fc2)]
    )
    packed = jnp.concatenate(
        [mod_partial.reshape(batches, -1), jnp.broadcast_to(small, (parts,) + small.shape)], 1
    )
    packed = lax.all_to_all(packed, "m", split_axis=0, concat_axis=0, tiled=True)
    mod_size = lat_count * 12 * width
    mod_here = all_sum(packed[:, :mod_size], "row").reshape(parts, lat_count, 2, 6, width)
    mod_here = vector_rel(jnp.moveaxis(mod_here, 0, -2).reshape(lat_count, 2, 6, span))
    small = packed[:, mod_size:]
    sizes = np.cumsum([0, 4 * width, 2 * width, 2 * b_fc1.shape[1], 2 * width])
    all_qv, all_out, all_fc1, all_fc2 = [small[:, a:b] for a, b in zip(sizes[:-1], sizes[1:])]
    all_qv = jnp.take(all_qv.reshape(parts, 2, 2, width), part_ids, axis=0)
    all_fc1 = jnp.take(all_fc1.reshape(parts, 2, -1), part_ids, axis=0)
    all_out = vector_rel(jnp.moveaxis(all_out.reshape(parts, 2, width), 0, 1).reshape(2, span))
    all_fc2 = vector_rel(jnp.moveaxis(all_fc2.reshape(parts, 2, width), 0, 1).reshape(2, span))

    zeros = jnp.zeros((parts, width), f32)
    bias_qkv = [
        jnp.concatenate([all_qv[:, b, 0], zeros, all_qv[:, b, 1]], 1)[:, None, :] for b in range(2)
    ]
    bias_fc1 = [all_fc1[:, b][:, None, :] for b in range(2)]
    hidden_width = w_fc1.shape[2]
    mixed_cols, out_cols, hidden_cols = (0, 3 * width), (3 * width, 4 * width), (0, hidden_width)
    middle_cut = 4 * width // 256 * 128 + 128
    mixed_cuts = [(0, middle_cut), (middle_cut, 4 * width)]
    hidden_cut = hidden_width // 256 * 128 + 128
    fc_cuts = ([hidden_cols], [(0, hidden_cut), (hidden_cut, hidden_width)])
    layouts = (spatial, temporal)
    groups_of = (1, lat_count)

    def shard_of(b, name):
        if name == "mixed":
            return jnp.concatenate([w_qkv[b].reshape(depth, 3 * width), w_out[b]], 1)
        return (w_fc1 if name == "fc1" else w_fc2)[b]

    def own_batch(value):
        return lax.all_to_all(value, "m", 0, 0).reshape(span, tokens)

    def to_stream(value):
        return dot_tn(value, exchange) if relative else value.T.astype(f32)

    def to_argument(value):
        return lax.all_to_all(value.reshape(parts, width, tokens), "m", 0, 0)

    lat_here = row * frames_dev // NF
    mod_space = lax.dynamic_slice_in_dim(mod_here[:, 0], lat_here, 1, 0)
    mods = [
        [spread(m[:, column], tokens) for column in range(6)] for m in (mod_space, mod_here[:, 1])
    ]

    def open_stage(b, stream):
        normed, inverse = norm_forward(stream)
        hidden = features_all((normed * (1.0 + mods[b][1]) + mods[b][0]).astype(bf16))
        return {"stream": stream, "normed": normed, "inverse": inverse, "hidden": hidden}

    def attention_stage(b, k):
        qkv = project(
            k["hidden"], weights[b]["mixed"], mixed_cols, [bias_qkv[b]], lambda v, c: (v + c,), [bf16], "qkv"
        )[0]
        attended, logs = attention_call(forward_kernel, [qkv], None, layouts[b], width, 4, "attend")
        return {**k, "qkv": qkv, "attended": attended, "logs": logs}

    fused = relative and lat_count == 1

    def shaped(*kinds):
        return [jax.ShapeDtypeStruct(shape, kind) for shape, kind in kinds]

    full = (tokens, span)

    def middle_stage(b, k):
        if fused:
            made = contract(
                k["attended"], weights[b]["mixed"], out_cols, "out",
                [k["stream"]], [all_out[b][None], mods[b][2], mods[b][4], mods[b][3]],
                shaped((full, f32), (full, f32), (full, f32), ((tokens, 1), f32), (full, bf16)),
                finish_middle,
            )
            return {**k, **dict(zip(("branch", "middle", "normed2", "inverse2", "hidden2"), made))}
        branch = features_sum(contract(k["attended"], weights[b]["mixed"], out_cols, "out")) + all_out[b]
        middle = k["stream"] + mods[b][2] * branch
        normed, inverse = norm_forward(middle)
        hidden = features_all((normed * (1.0 + mods[b][4]) + mods[b][3]).astype(bf16))
        return {**k, "branch": branch, "middle": middle, "normed2": normed, "inverse2": inverse, "hidden2": hidden}

    def up_stage(b, k):
        act, slope = project(
            k["hidden2"], weights[b]["fc1"], hidden_cols, [bias_fc1[b]], gelu_pair, [bf16, bf16], "up"
        )
        return {**k, "act": act, "slope": slope}

    def down_stage(b, k):
        if fused:
            branch, result = contract(
                k["act"], weights[b]["fc2"], hidden_cols, "down",
                [k["middle"]], [all_fc2[b][None], mods[b][5]],
                shaped((full, f32), (full, bf16)), finish_stream,
            )
            return result, {**k, "branch2": branch}
        branch = features_sum(contract(k["act"], weights[b]["fc2"], hidden_cols, "down")) + all_fc2[b]
        return k["middle"] + mods[b][5] * branch, {**k, "branch2": branch}

    def fc2_grads(b, k, grad):
        low = features_all((mods[b][5] * grad).astype(bf16))
        stacks, (total_low,), _ = weight_grads([(low, k["act"])], fc_cuts[b], "grad_fc2")
        return {**k, "grad": grad, "low2": low, "sum_b2": own_share(total_low)}, scatters(stacks, KINDS[b]["fc2"])

    def up_back(b, k):
        grad_pre = project(
            k["low2"], weights[b]["fc2"], hidden_cols, [k["slope"]],
            lambda v, s: (v * s.astype(f32),), [bf16], "up_back",
        )[0]
        stacks, _, (total_pre,) = weight_grads([(k["hidden2"], grad_pre)], fc_cuts[b], "grad_fc1")
        return {**k, "pre": grad_pre, "sum_b1": total_pre[:, 0]}, scatters(stacks, KINDS[b]["fc1"])

    def hidden2_back(b, k):
        if fused:
            middle, low, sums = contract(
                k["pre"], weights[b]["fc1"], hidden_cols, "hidden2_back",
                [k["grad"], k["normed2"], k["branch"], k["inverse2"]], [mods[b][4], mods[b][2]],
                shaped((full, f32), (full, bf16), ((3, span), f32)), finish_middle_back,
            )
            return {**k, "g_middle": middle, "low1": low, "sums2": sums}
        grad_hidden = features_sum(contract(k["pre"], weights[b]["fc1"], hidden_cols, "hidden2_back"))
        return {**k, "g_hidden2": grad_hidden}

    def attention_back(b, k):
        if fused:
            middle, low = k["g_middle"], k["low1"]
        else:
            grad_hidden = k["g_hidden2"]
            back = norm_backward(grad_hidden * (1.0 + mods[b][4]), k["normed2"], k["inverse2"])
            middle = k["grad"] + back
            low = features_all((mods[b][2] * middle).astype(bf16))
        grad_att = project(low, weights[b]["mixed"], out_cols, [], lambda v: (v,), [bf16], "out_back")[0]
        grad_qkv = attention_call(
            backward_kernel, [k["qkv"], grad_att, k["attended"]], k["logs"], layouts[b], 3 * width, 10, "attend_back"
        )[0]
        return {**k, "g_middle": middle, "low1": low, "g_qkv": grad_qkv}

    def mixed_grads(b, k):
        stacks, (_, total_low), (total_qkv, _) = weight_grads(
            [(k["hidden"], k["g_qkv"]), (k["low1"], k["attended"])], mixed_cuts, "grad_mixed"
        )
        return {**k, "sum_bo": own_share(total_low), "sum_qkv": total_qkv[:, 0]}, [
            scatter(pair, kind) for kind, pair in enumerate(stacks)
        ]

    def stream_back(b, k):
        biases = (
            k["sum_qkv"][:, :width], k["sum_qkv"][:, 2 * width :], k["sum_bo"], k["sum_b1"], k["sum_b2"],
        )
        if fused:
            stream, sums = contract(
                k["g_qkv"], weights[b]["mixed"], mixed_cols, "hidden_back",
                [k["g_middle"], k["normed"], k["inverse"]], [mods[b][1]],
                shaped((full, bf16), ((2, span), f32)), finish_stream_back,
            )
            return stream, ((sums, k["sums2"], k["grad"], k["branch2"]), biases)
        grad_hidden = features_sum(contract(k["g_qkv"], weights[b]["mixed"], mixed_cols, "hidden_back"))
        back = norm_backward(grad_hidden * (1.0 + mods[b][1]), k["normed"], k["inverse"])
        groups = groups_of[b]
        modulate_grad = jnp.stack(
            [
                group_sum(grad_hidden, groups),
                group_sum(grad_hidden * k["normed"], groups),
                group_sum(k["g_middle"] * k["branch"], groups),
                group_sum(k["g_hidden2"], groups),
                group_sum(k["g_hidden2"] * k["normed2"], groups),
                group_sum(k["grad"] * k["branch2"], groups),
            ],
            1,
        )
        return k["g_middle"] + back, (modulate_grad, biases)

    def modulate_sums(made):
        if not fused:
            return made
        sums, sums2, grad, branch = made
        last_sum = jnp.sum(grad * branch, 0, keepdims=True)
        return jnp.concatenate([sums, sums2[2:], sums2[:2], last_sum], 0)[None]

    def pack_small(small_space, small_time):
        mod_grad_space, biases_space = modulate_sums(small_space[0]), small_space[1]
        mod_grad_time, biases_time = modulate_sums(small_time[0]), small_time[1]
        onehot = (jnp.arange(lat_count) == lat_here).astype(f32)
        mod_grads = jnp.stack([onehot[:, None, None] * mod_grad_space, mod_grad_time], 1)
        row_sums = [pair[place] for place in (2, 4) for pair in (biases_space, biases_time)]
        streams = vector_plain(jnp.concatenate([mod_grads.reshape(-1, span)] + row_sums, 0))
        streams = jnp.moveaxis(streams.reshape(-1, parts, width), 1, 0)
        ordered = [pair[place] for place in (0, 1, 3) for pair in (biases_space, biases_time)]
        ordered = jnp.take(jnp.concatenate(ordered, 1), part_ids, axis=0)
        mods_count = lat_count * 12
        pieces = [
            streams[:, :mods_count].reshape(parts, -1),
            ordered[:, : 4 * width],
            streams[:, mods_count : mods_count + 2].reshape(parts, -1),
            ordered[:, 4 * width :],
            streams[:, mods_count + 2 :].reshape(parts, -1),
        ]
        packed = jnp.concatenate(pieces, 1)
        sizes = [mods_count * width] + [width] * 6 + [hidden_width] * 2 + [width] * 2
        sent = lax.all_to_all(packed, "m", split_axis=0, concat_axis=0, tiled=True)
        return packed, sent, np.cumsum([0] + sizes)

    names = ("mixed", "fc1", "fc2")
    gathers = [Gather(shard_of(b, n), rows, parts, KINDS[b][n]) for b in range(2) for n in names]
    weights = [{}, {}]
    depth_of = len(gathers[0].plan)

    def move(*pairs, after=None):
        tail = None
        for item, until in pairs:
            while item.done < min(until, depth_of):
                if isinstance(item, Gather):
                    tail = item.step(tail)
                else:
                    item.step(after)

    def ready(number):
        weights[number // 3][names[number % 3]] = gathered(gathers[number])

    last = depth_of
    g = gathers
    first = depth_of - 3
    move((g[0], first - 1), (g[1], first - 1))
    fence(g, ())
    move((g[0], first), (g[1], first))
    first_in, top = fence(g, (own_batch(latents), own_batch(cotangent)))
    move((g[0], last - 2), (g[1], last - 2), (g[2], first - 1), (g[3], first - 1))
    first_in, mods, top = fence(g, (to_stream(first_in), mods, top.T))
    move((g[0], last - 1), (g[1], last - 1), (g[2], first), (g[3], first))
    k0 = fence(g, open_stage(0, first_in))
    move((g[2], last - 2), (g[3], last - 2), (g[4], first - 1), (g[5], first - 1), (g[0], last), (g[1], last))
    fence(g, ())
    ready(0)
    ready(1)
    move((g[2], last - 1), (g[3], last - 1), (g[4], first), (g[5], first))
    k0 = fence(g, middle_stage(0, attention_stage(0, k0)))
    move((g[2], last), (g[3], last), (g[4], last - 2), (g[5], last - 2))
    ready(2)
    first_out, k0 = down_stage(0, up_stage(0, k0))
    first_out = stream_plain(first_out.astype(bf16))
    k0, first_out, top = fence(g, (k0, first_out, top))
    ready(2)
    ready(3)
    move((g[4], last - 1), (g[5], last - 1))
    k1 = open_stage(1, stream_rel(send_positions(first_out)))
    k1 = attention_stage(1, k1)
    k0, k1, top = fence(g, (k0, k1, top))
    move((g[4], last), (g[5], last))
    grad_top = send_positions(top)
    k1 = middle_stage(1, k1)
    k0, k1 = fence(g, (k0, k1))
    ready(4)
    ready(5)
    k1 = up_stage(1, k1)
    grad_top, _ = lax.optimization_barrier((grad_top, k1["act"]))
    k1, s5 = fc2_grads(1, k1, stream_rel(grad_top))

    def to(count, *lists, after=None):
        move(*[(s, count) for items in lists for s in items], after=after)

    k0, k1 = fence(s5, (k0, k1))
    to(1, s5)
    second_out, k1 = down_stage(1, k1)
    second_out = stream_plain(second_out.astype(bf16))
    k0, k1, second_out = fence(s5, (k0, k1, second_out))
    to(2, s5)
    output = send_frames(second_out)
    k1, s4 = up_back(1, k1)
    k0, k1, output = fence(s4 + s5, (k0, k1, output))
    to(1, s4)
    to(3, s5)
    k1 = hidden2_back(1, k1)
    k0, k1 = fence(s4 + s5, (k0, k1))
    to(2, s4)
    to(4, s5)
    k1 = attention_back(1, k1)
    k1, s3 = mixed_grads(1, k1)
    k0, k1, output = fence(s3 + s4 + s5, (k0, k1, output.T))
    to(3, s4)
    to(last, s5)
    grad_mid, small_time = stream_back(1, k1)
    grad_mid = stream_plain(grad_mid.astype(bf16))
    k0, grad_mid, small_time, output = fence(s3 + s4 + s5, (k0, grad_mid, small_time, output))
    to(1, s3)
    grad_low = send_frames(grad_mid)
    k0, grad_low, small_time, output = fence(s3 + s4 + s5, (k0, grad_low, small_time, output))
    k0, s2 = fc2_grads(0, k0, stream_rel(grad_low))
    to(1, s2)
    k0, s1 = up_back(0, k0)
    to(2, s3, after=k0["pre"])
    to(4, s4, after=k0["pre"])
    k0, small_time, output = fence(s1 + s2 + s3 + s4 + s5, (k0, small_time, output))
    to(last, s4)
    to(3, s3)
    k0 = hidden2_back(0, k0)
    to(1, s1)
    k0, small_time, output = fence(s1 + s2 + s3 + s4 + s5, (k0, small_time, output))
    to(2, s2, s1)
    to(4, s3)
    k0 = attention_back(0, k0)
    k0, s0 = mixed_grads(0, k0)
    grad_first, small_space = stream_back(0, k0)
    grad_first, small, output = fence(s0 + s1 + s2 + s3, (grad_first, (small_space, small_time), output))
    to(1, s0)
    small, _ = lax.optimization_barrier((small, s0[0].arrays[1]))
    made, packed, counts = pack_small(small[0], small[1])
    to(3, s2, s1, after=made)
    to(last, s3)
    grad_first, packed, output = fence(s0 + s1 + s2 + s3, (grad_first, packed, output))
    to(4, s2, s1)
    to(2, s0)
    packed, _ = lax.optimization_barrier((packed, s0[0].arrays[-2]))
    output = to_argument(output)
    output, grad_first = fence(s0 + s1 + s2, (output, grad_first))
    to(last, s2, s1)
    to(3, s0)
    fence(s0 + s1 + s2, ())
    to(last, s0, s1, s2, s3, s4, s5)
    joined = lambda items: jnp.concatenate([item.result() for item in items], 1)
    weights_space = [joined(items) for items in (s0, s1, s2)]
    weights_time = [joined(items) for items in (s3, s4, s5)]
    grad_first = grad_first.astype(bf16)
    grad_first = dot_nt(exchange, grad_first).astype(bf16) if relative else grad_first.T
    grad_latents = to_argument(grad_first).astype(f32)

    mod_part = packed[:, : counts[1]]
    bias_part = jnp.sum(packed[:, counts[1] :], 0, keepdims=True)
    flat = jnp.concatenate([mod_part.reshape(1, -1), bias_part], 1)
    flat = all_sum(flat, "row")[0]
    mod_grad_low = flat[: batches * counts[1]].reshape(batches, lat_count, 2, 6, width).astype(bf16)
    bias_part = flat[batches * counts[1] :]
    bias_out = [bias_part[a - counts[1] : b - counts[1]] for a, b in zip(counts[1:-1], counts[2:])]
    grad_bias_qv = jnp.stack(
        [jnp.stack([bias_out[0], bias_out[2]]), jnp.stack([bias_out[1], bias_out[3]])]
    )
    grad_bias_out = jnp.stack(bias_out[4:6])
    grad_bias_fc1 = jnp.stack(bias_out[6:8])
    grad_bias_fc2 = jnp.stack(bias_out[8:10])
    grad_bias_ada = jnp.sum(mod_grad_low.astype(f32), (0, 1))
    grad_weight_ada = jnp.einsum("mlr,mlbjk->brjk", cond_low, mod_grad_low, preferred_element_type=f32)
    cond_partial = jnp.einsum("mlbjk,brjk->mlr", mod_grad_low, w_ada, preferred_element_type=f32)
    cond_total = over_u(all_sum(cond_partial, "m"))
    sigmoid_cond = jax.nn.sigmoid(cond_float)
    grad_condition = cond_total * sigmoid_cond * (1.0 + cond_float * (1.0 - sigmoid_cond))
    grad_weight_qkv, grad_weight_out, grad_weight_fc1, grad_weight_fc2 = [], [], [], []
    for mixed, first, second in (weights_space, weights_time):
        grad_weight_qkv.append(mixed[:, : 3 * width].reshape(depth, 3, width))
        grad_weight_out.append(mixed[:, 3 * width :])
        grad_weight_fc1.append(first)
        grad_weight_fc2.append(second)
    return (
        output,
        grad_latents,
        grad_condition,
        grad_weight_ada,
        grad_bias_ada,
        jnp.stack(grad_weight_qkv),
        grad_bias_qv,
        jnp.stack(grad_weight_out),
        grad_bias_out,
        jnp.stack(grad_weight_fc1),
        grad_bias_fc1,
        jnp.stack(grad_weight_fc2),
        grad_bias_fc2,
    )


def solution(mesh):
    rows, columns = mesh.devices.shape

    def placed(latents, *rest):
        parts = latents.shape[0]
        inner = Mesh(mesh.devices.reshape(rows, columns // parts, parts), ("row", "u", "m"))
        col = ("u", "m")
        in_specs = (
            P(None, col, "row"),
            P(None, None, "row"),
            P(None, "row", None, col),
            P(None, None, col),
            P(None, "row", None, col),
            P(None, None, col),
            P(None, "row", col),
            P(None, col),
            P(None, "row", col),
            P(None, col),
            P(None, "row", col),
            P(None, col),
            P(None, col, "row"),
        )
        out_specs = (P(None, col, "row"),) + in_specs[:1] + in_specs[1:-1]
        return jax.shard_map(
            shards, mesh=inner, in_specs=in_specs, out_specs=out_specs, check_vma=False
        )(latents, *rest)

    return placed
```
